32 devices in a mesh: ens: 8 (over y, x, core), lon: 4 (over z).
Axes of the slice: x: 2, y: 2, z: 4, core: 2. Of those that a mesh axis runs over, the one named last changes fastest.
Arguments:
- features: bfloat16 [8, 384, 46080], P('ens', None, 'lon'), may hold values from -6 to 6
- proj_weight: bfloat16 [648, 384], replicated, may hold values from -0.3125 to 0.3125
- basis_vals: float32 [32, 32, 9], replicated, may hold values from -0.375 to 0.375
- row_of: int32 [32, 32], replicated, may hold values from 0 to 31
- col_off: int32 [32, 32], replicated, may hold values from -4 to 4
- observed: float32 [72, 46080], P(None, 'lon'), may hold values from -6 to 6
- lat_weight: float32 [32], replicated, may hold values from 0.3 to 1
Outputs:
- feature_grad: bfloat16 [8, 384, 46080], P('ens', None, 'lon')
- weight_grad: float32 [648, 384], replicated
The draws below stay inside these ranges and needn't reach their ends.
Inputs may be any that keep to these rules, and one draw needn't show every extreme that they name: row_of names a row of the slab. col_off is a longitude offset in columns.
All inputs are finite; a program needn't handle non-finite values.
Results may differ from the reference program's by a relative error of at most 0.0089.
Values may be sent and summed in bfloat16 or wider, within the bound.
A program may use at most 256 MiB of HBM per device.

```python
import math
import jax
import jax.numpy as jnp
from jax import lax

C = 384
O = 72
NLON = 1440
K = 9
S = 32
R = 4
LAT = 32
MEMBERS = 8


def set_ends(entries, stream_key, low, largest):
    shape = entries.shape
    spot = [jax.random.randint(jax.random.fold_in(stream_key, axis), (), 0, shape[axis]) for axis in range(len(shape))]
    entries = entries.at[tuple(spot)].set(low)
    longest = shape.index(max(shape))
    spot[longest] = (spot[longest] + 1) % shape[longest]
    return entries.at[tuple(spot)].set(largest)


def block_scale(key, dims, pieces, least, high):
    level = 1.0
    for position, shards_of in pieces:
        draws = jax.random.uniform(jax.random.fold_in(jax.random.fold_in(key, 6), position), (shards_of,), jnp.float32, least / len(pieces), high / len(pieces))
        level = level * jnp.repeat(jnp.exp(draws), dims[position] // shards_of).reshape((-1,) + (1,) * (len(dims) - 1 - position))
    return level


def normal_values(own_key, shape, deviation, bound, shards=(), kind=jnp.bfloat16):
    array = deviation * jax.random.normal(own_key, shape, jnp.float32)
    if shards:
        array = array * block_scale(own_key, shape, shards, -0.22, 0.18)
    return jnp.clip(array, -bound, bound).astype(kind)


def setup_inputs(seed: int = 0) -> dict:
    streams_of = jax.random.split(jax.random.key(seed), 8)
    features = normal_values(streams_of[0], (MEMBERS, C, NLON * LAT), 1.0, 6.0, ((0, 8), (2, 4)))
    proj_weight = normal_values(streams_of[1], (K * O, C), C ** -0.5, 0.3125)
    basis_vals = normal_values(streams_of[2], (LAT, S, K), (S * K) ** -0.5, 0.375, (), jnp.float32)
    row_of = set_ends(jax.random.randint(streams_of[3], (LAT, S), 0, LAT), jax.random.fold_in(streams_of[3], 1), 0, LAT - 1).astype(jnp.int32)
    col_off = set_ends(jax.random.randint(streams_of[4], (LAT, S), 0 - R, R + 1), jax.random.fold_in(streams_of[4], 1), 0 - R, R).astype(jnp.int32)
    observed = normal_values(streams_of[5], (O, NLON * LAT), 1.0, 6.0, ((1, 4),), jnp.float32)
    lat_weight = jnp.clip(jnp.exp(jax.random.uniform(streams_of[6], (LAT,), jnp.float32, math.log(0.3), math.log(1.0))), 0.3, 1.0)
    return dict(features=features, proj_weight=proj_weight, basis_vals=basis_vals, row_of=row_of, col_off=col_off, observed=observed, lat_weight=lat_weight)


SMOOTH = 0.25

def kernel_table(basis_vals, row_of, col_off):
    offsets = jnp.arange(2 * R + 1, dtype=jnp.int32) - R
    row_ids = jnp.arange(LAT, dtype=jnp.int32)
    row_hit = (row_of[:, :, None] == row_ids[None, None, :]).astype(jnp.float32)
    col_hit = (col_off[:, :, None] == offsets[None, None, :]).astype(jnp.float32)
    kernel = jnp.einsum('isk,isr,isd->dkir', basis_vals.astype(jnp.float32), row_hit, col_hit, precision=lax.Precision.HIGHEST)
    return kernel.astype(jnp.bfloat16)

def smooth_slope(diff):
    return diff / jnp.sqrt(diff * diff + SMOOTH * SMOOTH)

def reference(features, proj_weight, basis_vals, row_of, col_off, observed, lat_weight):
    kernel = lax.optimization_barrier(kernel_table(basis_vals, row_of, col_off)).astype(jnp.float32)
    weight_wide = proj_weight.astype(jnp.float32)

    def forward(member):
        projected = jnp.dot(weight_wide, member.astype(jnp.float32), precision=lax.Precision.HIGHEST).astype(jnp.bfloat16)
        projected = lax.optimization_barrier(projected).astype(jnp.float32).reshape(K, O, NLON, LAT)
        decoded = jnp.zeros((O, NLON, LAT), jnp.float32)
        for offset in range(2 * R + 1):
            decoded = decoded + jnp.einsum('kir,kojr->oji', kernel[offset], jnp.roll(projected, R - offset, axis=2), precision=lax.Precision.HIGHEST)
        return decoded
    outputs = lax.map(forward, features)
    target = observed.reshape(O, NLON, LAT)

    def member_grad(own_row):
        spread = lax.optimization_barrier(jnp.sum(smooth_slope(own_row[None] - outputs), axis=0))
        return smooth_slope(own_row - target) - spread / (MEMBERS - 1)
    slopes = lax.map(member_grad, outputs)
    cotangent = lax.optimization_barrier((slopes * lat_weight).astype(jnp.bfloat16))

    def backward(paired):
        member, cot_member = paired
        cot_wide = cot_member.astype(jnp.float32)
        spread_grad = jnp.zeros((K, O, NLON, LAT), jnp.float32)
        for offset in range(2 * R + 1):
            spread_grad = spread_grad + jnp.einsum('kir,oji->kojr', kernel[offset], jnp.roll(cot_wide, offset - R, axis=1), precision=lax.Precision.HIGHEST)
        spread_grad = spread_grad.reshape(K * O, NLON * LAT).astype(jnp.bfloat16)
        spread_grad = lax.optimization_barrier(spread_grad).astype(jnp.float32)
        feature_grad = jnp.dot(weight_wide.T, spread_grad, precision=lax.Precision.HIGHEST).astype(jnp.bfloat16)
        weight_part = jnp.dot(spread_grad, member.astype(jnp.float32).T, precision=lax.Precision.HIGHEST)
        return (feature_grad, weight_part)
    feature_grads, weight_parts = lax.map(backward, (features, cotangent))
    weight_grad = lax.optimization_barrier(jnp.sum(weight_parts, axis=0)) / math.sqrt(MEMBERS * NLON * LAT)
    return (feature_grads, weight_grad)
```

```python
import functools
import math

import jax
import jax.numpy as jnp
from jax import lax
from jax.experimental import pallas as pl
from jax.experimental.pallas import tpu as pltpu
from jax.sharding import PartitionSpec as P

O = 72
OP = 80
K = 9
R = 4
LAT = 32
SMOOTH = 0.25
BLK = 256
HALF = 128
F32 = jnp.float32
BF16 = jnp.bfloat16
MESH = pl.DeviceIdType.MESH
VMEM_LIMIT = 60 * 1024 * 1024


def whole(shape):
    return pl.BlockSpec(shape, lambda s: (0,) * len(shape))


def kernel_rows(basis_vals, row_of, col_off):
    code = (col_off + R) * LAT + row_of
    ids = jnp.arange((2 * R + 1) * LAT, dtype=jnp.int32)
    hit = (code[:, :, None] == ids[None, None, :]).astype(F32)
    table = jnp.einsum("isk,isq->ikq", basis_vals, hit, precision=lax.Precision.HIGHEST)
    return table.astype(BF16)


def side_tables(table):
    taps = 2 * R + 1
    four = table.reshape(LAT, K, taps, LAT)
    ahead = four.transpose(1, 2, 3, 0).reshape(K, taps * LAT, LAT)
    back = four[:, :, ::-1].transpose(1, 2, 0, 3).reshape(K, taps * LAT, LAT)
    return ahead, back


def build_band(table, band):
    lane = lax.broadcasted_iota(jnp.int32, (LAT, BLK), 1)
    spread_lanes = (lane % LAT == lax.broadcasted_iota(jnp.int32, (LAT, BLK), 0)).astype(F32)
    spread_lanes = spread_lanes.astype(BF16)
    place = lane // LAT
    cols = BLK // LAT

    def one(k, carry):
        tiled = jnp.dot(table[k], spread_lanes, preferred_element_type=F32)
        for e in range(2 * cols):
            block = jnp.zeros((LAT, BLK), F32)
            for j in range(cols):
                d = e - j
                if 0 <= d <= 2 * R:
                    block = jnp.where(place == j, tiled[d * LAT : (d + 1) * LAT], block)
            band[k, e * LAT : (e + 1) * LAT, :] = block.astype(BF16)
        return carry

    lax.fori_loop(0, K, one, 0)


def padded_weight(weight):
    wide = weight[...].astype(F32)
    gap = jnp.zeros((OP - O, wide.shape[1]), F32)
    rows = []
    for k in range(K):
        rows += [wide[k * O : (k + 1) * O], gap]
    return jnp.concatenate(rows, axis=0)


def greet(peers):
    barrier = pltpu.get_barrier_semaphore()
    for peer in peers:
        pl.semaphore_signal(barrier, inc=1, device_id=peer, device_id_type=MESH)
    pl.semaphore_wait(barrier, len(peers))


def forward_kernel(
    n, nl, group, steps, share,
    feat, tail, head, weight, table, obs, lat, out, rims,
    wpad, band, proj, dec, flat, recv, send, cot, left, right, rim_left, rim_right,
    ssem1, rsem1, ssem2, rsem2, hsend, hrecv,
):
    s = pl.program_id(0)
    me = lax.axis_index("ens")
    real = group * 2 * O
    own = pl.multiple_of(me * share, 16)
    after = {"lon": lax.rem(lax.axis_index("lon") + 1, nl)}
    before = {"lon": lax.rem(lax.axis_index("lon") + nl - 1, nl)}

    def rim(src, dst, slot, peer):
        return pltpu.make_async_remote_copy(
            src_ref=src,
            dst_ref=dst,
            send_sem=hsend.at[slot],
            recv_sem=hrecv.at[slot],
            device_id=peer,
            device_id_type=MESH,
        )

    def first(q, off):
        peer = lax.rem(me + off, n)
        return pltpu.make_async_remote_copy(
            src_ref=dec.at[q, pl.ds(pl.multiple_of(peer * share, 16), share)],
            dst_ref=recv.at[q, off],
            send_sem=ssem1.at[q, off],
            recv_sem=rsem1.at[q, off],
            device_id={"ens": peer},
            device_id_type=MESH,
        )

    def second(q, off):
        return pltpu.make_async_remote_copy(
            src_ref=send.at[q, off],
            dst_ref=cot.at[q, pl.ds(own, share)],
            send_sem=ssem2.at[q, off],
            recv_sem=rsem2.at[q, off],
            device_id={"ens": lax.rem(me - off + n, n)},
            device_id_type=MESH,
        )

    def put(values, h, lo):
        for k in range(K):
            proj[k, h, :, lo : lo + HALF] = values[k * OP : (k + 1) * OP].astype(BF16)

    @pl.when(s == 0)
    def _():
        greet([{"ens": lax.rem(me + off, n)} for off in range(1, n)] + [after, before])
        rim(tail, left, 0, after).start()
        rim(head, right, 1, before).start()
        wpad[...] = padded_weight(weight).astype(BF16)
        build_band(table, band)
        if n * share > real:
            for q in range(steps):
                dec[q, real:, :] = jnp.zeros((n * share - real, HALF), BF16)
            flat[real:, :] = jnp.zeros((n * share - real, HALF), F32)

    @pl.when(s < steps)
    def _():
        def one(b, carry):
            lanes = pl.ds(pl.multiple_of(b * BLK, BLK), BLK)
            got = jnp.dot(wpad[...], feat[:, lanes], preferred_element_type=F32)
            h = s * group + b
            put(got[:, :HALF], h, HALF)
            put(got[:, HALF:], h + 1, 0)
            return carry

        lax.fori_loop(0, group, one, 0)

    @pl.when(s == 1)
    def _():
        rim(tail, left, 0, after).wait()
        put(jnp.dot(wpad[...], left[...], preferred_element_type=F32), 0, 0)

    @pl.when(s == steps)
    def _():
        rim(head, right, 1, before).wait()
        put(jnp.dot(wpad[...], right[...], preferred_element_type=F32), steps * group, HALF)

    @pl.when(jnp.logical_and(s > 0, s <= steps))
    def _():
        q = s - 1
        g0 = q * group
        acc = jnp.zeros((group * OP, BLK), F32)
        for k in range(K):
            for part in range(2):
                lhs = proj[k, pl.ds(g0 + part, group)].reshape(group * OP, BLK)
                acc = acc + jnp.dot(
                    lhs, band[k, part * BLK : (part + 1) * BLK, :], preferred_element_type=F32
                )
        for g in range(group):
            piece = acc[g * OP : g * OP + O]
            both = jnp.concatenate([piece[:, :HALF], piece[:, HALF:]], axis=0)
            dec[q, g * 2 * O : (g + 1) * 2 * O, :] = both.astype(BF16)
        for off in range(1, n):
            first(q, off).start()

    @pl.when(s > 1)
    def _():
        q = s - 2
        for t in range(2 * group):
            flat[t * O : (t + 1) * O, :] = obs[:, t * HALF : (t + 1) * HALF]
        for off in range(1, n):
            first(q, off).wait_recv()
        lat_row = jnp.broadcast_to(lat[0:1, :], (16, HALF))

        def smooth(diff):
            return diff * lax.rsqrt(diff * diff + SMOOTH * SMOOTH)

        def one(step, carry):
            at = pl.multiple_of(step * 16, 16)
            here = pl.ds(pl.multiple_of(own + at, 16), 16)
            values = [dec[q, here, :].astype(F32)]
            values += [recv[q, off, pl.ds(at, 16), :].astype(F32) for off in range(1, n)]
            sums = [None] * n
            for a in range(n):
                for b in range(a + 1, n):
                    pair = smooth(values[a] - values[b])
                    sums[a] = pair if sums[a] is None else sums[a] + pair
                    sums[b] = -pair if sums[b] is None else sums[b] - pair
            target = flat[here, :]
            for a in range(n):
                slope = smooth(values[a] - target) - sums[a] * (1.0 / (n - 1))
                result = (slope * lat_row).astype(BF16)
                if a == 0:
                    cot[q, here, :] = result
                else:
                    send[q, a, pl.ds(at, 16), :] = result
            return carry

        lax.fori_loop(0, share // 16, one, 0)
        for off in range(1, n):
            second(q, off).start()

    @pl.when(s == steps + 1)
    def _():
        for q in range(steps):
            for off in range(1, n):
                first(q, off).wait_send()
                second(q, off).wait()
        last = rim(cot.at[steps - 1, pl.ds(real - OP, OP)], rim_left, 2, after)
        opening = rim(cot.at[0, pl.ds(0, OP)], rim_right, 3, before)
        last.start()
        opening.start()
        for q in range(steps):
            out[q * n * share : (q + 1) * n * share, :] = cot[q]
        last.wait()
        opening.wait()
        rims[0] = rim_left[...]
        rims[1] = rim_right[...]


def forward(n, nl, feat, tail, head, weight, table, obs, lat, group, steps, share):
    chan = feat.shape[0]
    wide = group * BLK
    rows = n * share
    sem = pltpu.SemaphoreType.DMA((steps, n))
    return pl.pallas_call(
        functools.partial(forward_kernel, n, nl, group, steps, share),
        out_shape=(
            jax.ShapeDtypeStruct((steps * rows, HALF), BF16),
            jax.ShapeDtypeStruct((2, OP, HALF), BF16),
        ),
        grid=(steps + 2,),
        in_specs=[
            pl.BlockSpec((chan, wide), lambda s: (0, jnp.minimum(s, steps - 1))),
            whole(tail.shape),
            whole(head.shape),
            whole(weight.shape),
            whole(table.shape),
            pl.BlockSpec((O, wide), lambda s: (0, jnp.clip(s - 2, 0, steps - 1))),
            whole(lat.shape),
        ],
        out_specs=(whole((steps * rows, HALF)), whole((2, OP, HALF))),
        scratch_shapes=[
            pltpu.VMEM((K * OP, chan), BF16),
            pltpu.VMEM((K, 2 * BLK, BLK), BF16),
            pltpu.VMEM((K, steps * group + 1, OP, BLK), BF16),
            pltpu.VMEM((steps, rows, HALF), BF16),
            pltpu.VMEM((rows, HALF), F32),
            pltpu.VMEM((steps, n, share, HALF), BF16),
            pltpu.VMEM((steps, n, share, HALF), BF16),
            pltpu.VMEM((steps, rows, HALF), BF16),
            pltpu.VMEM((chan, HALF), BF16),
            pltpu.VMEM((chan, HALF), BF16),
            pltpu.VMEM((OP, HALF), BF16),
            pltpu.VMEM((OP, HALF), BF16),
            sem,
            sem,
            sem,
            sem,
            pltpu.SemaphoreType.DMA((4,)),
            pltpu.SemaphoreType.DMA((4,)),
        ],
        compiler_params=pltpu.CompilerParams(
            collective_id=0, has_side_effects=True, vmem_limit_bytes=VMEM_LIMIT
        ),
        name="forward_slopes",
    )(feat, tail, head, weight, table, obs, lat)


WG_ROWS = 2048
WG_PART = 656


def backward_kernel(
    group, steps, piece, share, cells, padded,
    cot, left, right, weight, table, feat, grad, wgrad,
    weight_t, band, ext, spread, acc,
):
    s = pl.program_id(0)
    blocks = steps * group

    @pl.when(s == 0)
    def _():
        ext[:, O:, :] = jnp.zeros((blocks + 1, OP - O, BLK), BF16)
        ext[0, :O, :HALF] = left[...].astype(F32)[OP - O :].astype(BF16)
        ext[blocks, :O, HALF:] = right[:O]

        weight_t[...] = padded_weight(weight).T.astype(BF16)
        build_band(table, band)

        def one(b, carry):
            start = lax.div(b, piece) * share + lax.rem(b, piece) * (2 * O)
            pair = cot[pl.ds(pl.multiple_of(start, 16), 2 * O), :].astype(F32)
            ext[b, :O, HALF:] = pair[:O].astype(BF16)
            ext[b + 1, :O, :HALF] = pair[O:].astype(BF16)
            return carry

        lax.fori_loop(0, blocks, one, 0)
        acc[...] = jnp.zeros_like(acc)

    g0 = s * group
    for k in range(K):
        got = jnp.zeros((group * OP, BLK), F32)
        for part in range(2):
            lhs = ext[pl.ds(g0 + part, group)].reshape(group * OP, BLK)
            got = got + jnp.dot(
                lhs, band[k, part * BLK : (part + 1) * BLK, :], preferred_element_type=F32
            )
        if padded:
            row = lax.broadcasted_iota(jnp.int32, got.shape, 0) // OP
            lane = lax.broadcasted_iota(jnp.int32, got.shape, 1)
            got = jnp.where((g0 + row) * BLK + lane < cells, got, 0.0)
        got = got.astype(BF16)
        for g in range(group):
            spread[k * OP : (k + 1) * OP, g * BLK : (g + 1) * BLK] = got[g * OP : (g + 1) * OP]

    acc[...] += lax.dot_general(
        spread[...], feat[...], (((1,), (1,)), ((), ())), preferred_element_type=F32
    )

    def one_grad(n, carry):
        lanes = pl.ds(pl.multiple_of(n * BLK, BLK), BLK)
        grad[:, lanes] = jnp.dot(
            weight_t[...], spread[:, lanes], preferred_element_type=F32
        ).astype(BF16)
        return carry

    lax.fori_loop(0, group, one_grad, 0)

    @pl.when(s == steps - 1)
    def _():
        parts = acc.shape[1] // HALF
        wgrad[parts * WG_PART - 16 :, :] = jnp.zeros((WG_ROWS - parts * WG_PART + 16, HALF), BF16)
        for t in range(parts):
            rows = [
                acc[k * OP : k * OP + O, t * HALF : (t + 1) * HALF] for k in range(K)
            ] + [jnp.zeros((8, HALF), F32)]
            wgrad[t * WG_PART : (t + 1) * WG_PART, :] = jnp.concatenate(rows, axis=0).astype(BF16)


def backward(cot, left, right, weight, table, feat, group, steps, piece, cells):
    chan = feat.shape[0]
    wide = group * BLK
    blocks = steps * group
    return pl.pallas_call(
        functools.partial(
            backward_kernel,
            group,
            steps,
            piece,
            cot.shape[0] * piece // blocks,
            cells,
            cells != blocks * BLK,
        ),
        out_shape=(
            jax.ShapeDtypeStruct(feat.shape, BF16),
            jax.ShapeDtypeStruct((WG_ROWS, HALF), BF16),
        ),
        grid=(steps,),
        in_specs=[
            whole(cot.shape),
            whole(left.shape),
            whole(right.shape),
            whole(weight.shape),
            whole(table.shape),
            pl.BlockSpec((chan, wide), lambda s: (0, s)),
        ],
        out_specs=(pl.BlockSpec((chan, wide), lambda s: (0, s)), whole((WG_ROWS, HALF))),
        scratch_shapes=[
            pltpu.VMEM((chan, K * OP), BF16),
            pltpu.VMEM((K, 2 * BLK, BLK), BF16),
            pltpu.VMEM((blocks + 1, OP, BLK), BF16),
            pltpu.VMEM((K * OP, wide), BF16),
            pltpu.VMEM((K * OP, chan), F32),
        ],
        compiler_params=pltpu.CompilerParams(vmem_limit_bytes=VMEM_LIMIT),
        name="backward_conv",
    )(cot, left, right, weight, table, feat)


def reduce_kernel(ne, nl, scale, part, out, recv1, mid, recv2, got, *sems):
    (ss1, rs1, ss2, rs2, ss3, rs3, ss4, rs4) = sems
    me = lax.axis_index("ens")
    at = lax.axis_index("lon")
    rows = WG_ROWS // ne
    small = rows // nl
    ens_peers = [{"ens": lax.rem(me + off, ne)} for off in range(1, ne)]
    lon_peers = [{"lon": lax.rem(at + off, nl)} for off in range(1, nl)]
    greet(ens_peers + lon_peers)

    def run(copies):
        for copy in copies:
            copy.start()
        for copy in copies:
            copy.wait()

    def send(src, dst, ssem, rsem, peer):
        return pltpu.make_async_remote_copy(
            src_ref=src, dst_ref=dst, send_sem=ssem, recv_sem=rsem, device_id=peer, device_id_type=MESH
        )

    own = pl.multiple_of(me * rows, 16)
    mine = pl.multiple_of(at * small, 8)
    run(
        [
            send(
                part.at[pl.ds(pl.multiple_of(lax.rem(me + off, ne) * rows, 16), rows)],
                recv1.at[off],
                ss1.at[off],
                rs1.at[off],
                {"ens": lax.rem(me + off, ne)},
            )
            for off in range(1, ne)
        ]
    )
    total = part[pl.ds(own, rows), :].astype(F32)
    for off in range(1, ne):
        total = total + recv1[off].astype(F32)
    mid[...] = total
    run(
        [
            send(
                mid.at[pl.ds(pl.multiple_of(lax.rem(at + off, nl) * small, 8), small)],
                recv2.at[off],
                ss2.at[off],
                rs2.at[off],
                {"lon": lax.rem(at + off, nl)},
            )
            for off in range(1, nl)
        ]
    )
    total = mid[pl.ds(mine, small), :]
    for off in range(1, nl):
        total = total + recv2[off]
    recv2[0] = total
    gat = got[1]
    gat[pl.ds(mine, small), :] = total
    run(
        [
            send(
                recv2.at[0],
                gat.at[pl.ds(mine, small)],
                ss3.at[off],
                rs3.at[off],
                {"lon": lax.rem(at + off, nl)},
            )
            for off in range(1, nl)
        ]
    )
    full = got[0]
    full[pl.ds(own, rows), :] = gat[...].astype(BF16)
    run(
        [
            send(
                full.at[pl.ds(own, rows)],
                full.at[pl.ds(own, rows)],
                ss4.at[off],
                rs4.at[off],
                {"ens": lax.rem(me + off, ne)},
            )
            for off in range(1, ne)
        ]
    )
    for t in range(out.shape[1] // HALF):
        piece = full[t * WG_PART : (t + 1) * WG_PART, :].astype(F32) * scale
        out[:, t * HALF : (t + 1) * HALF] = piece[: K * O]


def reduced(ne, nl, scale, part, chan):
    vmem = pl.BlockSpec(memory_space=pltpu.VMEM)
    rows = WG_ROWS // ne
    small = rows // nl

    def body(part, out, recv1, mid, recv2, full, gat, *sems):
        reduce_kernel(ne, nl, scale, part, out, recv1, mid, recv2, (full, gat), *sems)

    return pl.pallas_call(
        body,
        out_shape=jax.ShapeDtypeStruct((K * O, chan), F32),
        in_specs=[vmem],
        out_specs=vmem,
        scratch_shapes=[
            pltpu.VMEM((ne, rows, HALF), BF16),
            pltpu.VMEM((rows, HALF), F32),
            pltpu.VMEM((nl, small, HALF), F32),
            pltpu.VMEM((WG_ROWS, HALF), BF16),
            pltpu.VMEM((rows, HALF), F32),
        ]
        + [pltpu.SemaphoreType.DMA((n,)) for n in (ne, ne, nl, nl, nl, nl, ne, ne)],
        compiler_params=pltpu.CompilerParams(
            collective_id=1, has_side_effects=True, vmem_limit_bytes=VMEM_LIMIT
        ),
        name="weight_reduce",
    )(part)


def passed_along(value, axis, steps):
    count = lax.axis_size(axis)
    return lax.ppermute(value, axis, [(i, (i + steps) % count) for i in range(count)])


def split_shards(features, proj_weight, basis_vals, row_of, col_off, observed, lat_weight):
    ne = lax.axis_size("ens")
    nl = lax.axis_size("lon")
    assert features.shape[0] == 1
    feat = features[0]
    chan, cells = feat.shape
    aligned = cells % BLK == 0
    blocks = cells // BLK if aligned else pl.cdiv(cells + HALF, BLK)
    group_back = max(g for g in range(1, 10) if blocks % g == 0)
    steps_back = blocks // group_back
    group = max(g for g in range(1, 7) if blocks % g == 0)
    steps = blocks // group
    real = group * 2 * O
    share = pl.cdiv(pl.cdiv(real, ne), 16) * 16
    rows = ne * share
    extra = blocks * BLK - cells

    tail = feat[:, cells - HALF :]
    head = feat[:, :HALF]
    ahead, back = side_tables(kernel_rows(basis_vals, row_of, col_off))
    if not aligned:
        right = passed_along(head, "lon", -1)
        feat = jnp.pad(jnp.concatenate([feat, right], axis=1), ((0, 0), (0, extra - HALF)))
        observed = jnp.pad(observed, ((0, 0), (0, extra)))
    lat = jnp.broadcast_to(jnp.tile(lat_weight, HALF // LAT)[None, :], (8, HALF))
    cot, rims = forward(
        ne, nl, feat, tail, head, proj_weight, ahead, observed, lat, group, steps, share
    )

    if aligned:
        cot_left, cot_right = rims[0], rims[1]
    else:
        flat = cot.reshape(steps, rows, HALF)[:, :real].reshape(2 * blocks, O, HALF)
        flat = flat.transpose(1, 0, 2).reshape(O, blocks * BLK)[:, :cells]
        cot_left = passed_along(flat[:, cells - HALF :], "lon", 1)
        cot_right = passed_along(flat[:, :HALF], "lon", -1)
        flat = jnp.pad(
            jnp.concatenate([flat, cot_right], axis=1), ((0, 0), (0, extra - HALF))
        )
        flat = flat.reshape(O, 2 * blocks, HALF).transpose(1, 0, 2).reshape(steps, real, HALF)
        cot = jnp.pad(flat, ((0, 0), (0, rows - real), (0, 0))).reshape(steps * rows, HALF)
        cot_left = jnp.pad(cot_left, ((OP - O, 0), (0, 0)))
        cot_right = jnp.zeros((OP, HALF), BF16)
    grad, part = backward(
        cot, cot_left, cot_right, proj_weight, back, feat, group_back, steps_back, group, cells
    )
    scale = 1.0 / math.sqrt(ne * (cells // LAT) * nl * LAT)
    weight_grad = reduced(ne, nl, scale, part, chan)
    return (grad[:, :cells][None], weight_grad)


GROUP = 5
WIDE = GROUP * BLK
ROWS = GROUP * O
ROWS_P = ROWS + 8
PART = 256
PARTS = 3


def fused_kernel(
    n, nl, share, steps,
    feat, weight, table, table_back, obs, lat, grad, wout,
    wide, band, band_back, weight_t, lat_row, proj, edge, first_edge, edge_back,
    dec, recv, send, cot, seen, rim_left, rim_right, spread, gout,
    wpart, wrecv, wmid, wfull,
    fsem, osem, hsend, hrecv, ssem1, rsem1, ssem2, rsem2, gsem,
    ws1, wr1, ws2, wr2, ws3, wr3,
):
    me = lax.axis_index("ens")
    at = lax.axis_index("lon")
    cells = steps * WIDE
    chan = feat.shape[0]
    own = pl.multiple_of(me * share, 16)
    after = {"lon": lax.rem(at + 1, nl)}
    before = {"lon": lax.rem(at + nl - 1, nl)}
    prow = PART // n

    def remote(src, dst, ssem, rsem, peer):
        return pltpu.make_async_remote_copy(
            src_ref=src, dst_ref=dst, send_sem=ssem, recv_sem=rsem, device_id=peer, device_id_type=MESH
        )

    def piece(c):
        if isinstance(c, int) and c == steps:
            return pltpu.make_async_copy(
                feat.at[:, pl.ds(0, HALF)], wide.at[:, pl.ds(HALF, HALF)], fsem.at[steps]
            )
        if isinstance(c, int) and c == steps - 1:
            lo, size = c * WIDE, WIDE - HALF
        else:
            lo, size = c * WIDE, WIDE
        return pltpu.make_async_copy(
            feat.at[:, pl.ds(pl.multiple_of(lo + HALF, HALF), size)],
            wide.at[:, pl.ds(pl.multiple_of(lo + 2 * HALF, HALF), size)],
            fsem.at[c],
        )

    def seen_copy(q, u):
        c = lax.rem(q + steps - 1, steps)
        t = jnp.minimum(me * (share // 8) + u, ROWS // 8 - 1)
        row = pl.multiple_of(lax.rem(t, O // 8) * 8, 8)
        lane = pl.multiple_of(c * WIDE + lax.div(t, O // 8) * BLK, BLK)
        return pltpu.make_async_copy(
            obs.at[pl.ds(row, 8), pl.ds(lane, BLK)], seen.at[q, pl.ds(u * 8, 8)], osem.at[q, u]
        )

    def first(q, off):
        peer = lax.rem(me + off, n)
        return remote(
            dec.at[q, pl.ds(pl.multiple_of(peer * share, 16), share)],
            recv.at[q, off], ssem1.at[q, off], rsem1.at[q, off], {"ens": peer},
        )

    def second(q, off):
        return remote(
            send.at[q, off], cot.at[q, pl.ds(own, share)],
            ssem2.at[q, off], rsem2.at[q, off], {"ens": lax.rem(me - off + n, n)},
        )

    def halo(slot):
        if slot == 0:
            src, dst, peer = feat.at[:, pl.ds(cells - HALF, HALF)], wide.at[:, pl.ds(0, HALF)], after
        elif slot == 1:
            src, dst, peer = feat.at[:, pl.ds(0, HALF)], wide.at[:, pl.ds(cells + HALF, HALF)], before
        elif slot == 2:
            src = cot.at[0, pl.ds((GROUP - 1) * O, OP), pl.ds(HALF, HALF)]
            dst, peer = rim_left, after
        else:
            src, dst, peer = cot.at[1, pl.ds(0, OP), pl.ds(0, HALF)], rim_right, before
        return remote(src, dst, hsend.at[slot], hrecv.at[slot], peer)

    def out_copy(t):
        return pltpu.make_async_copy(
            gout.at[lax.rem(t, 2)], grad.at[:, pl.ds(pl.multiple_of(t * WIDE, WIDE), WIDE)], gsem.at[t]
        )

    def scatter(j, off):
        peer = lax.rem(me + off, n)
        return remote(
            wpart.at[j, pl.ds(pl.multiple_of(peer * prow, 16), prow)], wrecv.at[j, off],
            ws1.at[j, off], wr1.at[j, off], {"ens": peer},
        )

    def across(j, off):
        return remote(
            wmid.at[j, at], wmid.at[j, at], ws2.at[j, off], wr2.at[j, off], {"lon": lax.rem(at + off, nl)}
        )

    def gather(j, off):
        mine = pl.ds(pl.multiple_of(me * prow, 16), prow)
        return remote(
            wfull.at[j, mine], wfull.at[j, mine], ws3.at[j, off], wr3.at[j, off],
            {"ens": lax.rem(me + off, n)},
        )

    def project_edges():
        lanes = jnp.concatenate(
            [wide[:, :BLK], wide[:, (steps - 1) * WIDE : (steps - 1) * WIDE + BLK]], axis=1
        )
        got = jnp.dot(weight[...], lanes, preferred_element_type=F32)
        acc = jnp.zeros((2 * O, BLK), F32)
        for k in range(K):
            part = got[k * O : (k + 1) * O]
            lhs = jnp.concatenate([part[:, :BLK], part[:, BLK:]], axis=0).astype(BF16)
            acc = acc + jnp.dot(lhs, band[k, :BLK, :], preferred_element_type=F32)
        first_edge[...] = acc[:O]
        edge[...] = acc[O:]

    def forward_chunk(q):
        c = lax.rem(q + steps - 1, steps)
        got = jnp.dot(
            weight[...],
            wide[:, pl.ds(pl.multiple_of(c * WIDE + BLK, BLK), WIDE)],
            preferred_element_type=F32,
        )
        gap = jnp.zeros((ROWS_P - ROWS, BLK), F32)
        for k in range(K):
            rows = [got[k * O : (k + 1) * O, g * BLK : (g + 1) * BLK] for g in range(GROUP)]
            proj[k] = jnp.concatenate(rows + [gap], axis=0).astype(BF16)
        here = jnp.zeros((ROWS_P, BLK), F32)
        back = jnp.zeros((ROWS_P, BLK), F32)
        for k in range(K):
            here = here + jnp.dot(proj[k], band[k, :BLK, :], preferred_element_type=F32)
            back = back + jnp.dot(proj[k], band[k, BLK:, :], preferred_element_type=F32)
        total = jnp.concatenate([edge[...], here[: ROWS - O]], axis=0) + back[:ROWS]
        edge[...] = here[ROWS - O : ROWS]
        rest = jnp.zeros((n * share - ROWS, BLK), F32)
        dec[q] = jnp.concatenate([total, rest], axis=0).astype(BF16)
        for off in range(1, n):
            first(q, off).start()

    def smooth(diff):
        return diff * lax.rsqrt(diff * diff + SMOOTH * SMOOTH)

    def slopes(q):
        for u in range(share // 8):
            seen_copy(q, u).wait()
        for off in range(1, n):
            first(q, off).wait_recv()

        def one(step, carry):
            row = pl.multiple_of(lax.div(step, 2) * 16, 16)
            lanes = pl.ds(pl.multiple_of(lax.rem(step, 2) * HALF, HALF), HALF)
            here = pl.ds(pl.multiple_of(own + row, 16), 16)
            values = [dec[q, here, lanes].astype(F32)]
            values += [recv[q, off, pl.ds(row, 16), lanes].astype(F32) for off in range(1, n)]
            sums = [None] * n
            for a in range(n):
                for b in range(a + 1, n):
                    pair = smooth(values[a] - values[b])
                    sums[a] = pair if sums[a] is None else sums[a] + pair
                    sums[b] = -pair if sums[b] is None else sums[b] - pair
            target = seen[q, pl.ds(row, 16), lanes]
            area = jnp.broadcast_to(lat_row[0:1, lanes], (16, HALF))
            for a in range(n):
                slope = smooth(values[a] - target) - sums[a] * (1.0 / (n - 1))
                result = (slope * area).astype(BF16)
                if a == 0:
                    cot[q, here, lanes] = result
                else:
                    send[q, a, pl.ds(row, 16), lanes] = result
            return carry

        lax.fori_loop(0, share // 16 * 2, one, 0)
        for off in range(1, n):
            second(q, off).start()

    def backward_chunk(b):
        q = lax.rem(b + 1, steps)
        gap = jnp.zeros((OP - O, BLK), F32)
        lhs = cot[q, pl.ds(0, ROWS_P), :]
        for k in range(K):
            ahead = jnp.dot(lhs, band_back[k, :BLK, :], preferred_element_type=F32)
            here = jnp.dot(lhs, band_back[k, BLK:, :], preferred_element_type=F32)
            for g in range(GROUP):
                behind = edge_back[k] if g == 0 else ahead[(g - 1) * O : g * O]
                both = jnp.concatenate([here[g * O : (g + 1) * O] + behind, gap], axis=0)
                lanes = pl.ds(pl.multiple_of(b * WIDE + g * BLK, BLK), BLK)
                spread[k * OP : (k + 1) * OP, lanes] = both.astype(BF16)
            edge_back[k] = ahead[ROWS - O : ROWS]

    def one_grad(t, carry):
        @pl.when(t >= 2)
        def _():
            out_copy(t - 2).wait()

        lanes = pl.ds(pl.multiple_of(t * WIDE + HALF, HALF), WIDE)
        gout[lax.rem(t, 2)] = jnp.dot(
            weight_t[...], spread[: K * OP, lanes], preferred_element_type=F32
        ).astype(BF16)
        out_copy(t).start()
        return carry

    def after_scatter(j):
        for off in range(1, n):
            scatter(j, off).wait_recv()
        total = wpart[j, pl.ds(pl.multiple_of(me * prow, 16), prow), :].astype(F32)
        for off in range(1, n):
            total = total + wrecv[j, off].astype(F32)
        wmid[j, at] = total.astype(BF16)
        for off in range(1, nl):
            across(j, off).start()

    def after_across(j):
        for off in range(1, nl):
            across(j, off).wait_recv()
        total = wmid[j, 0].astype(F32)
        for z in range(1, nl):
            total = total + wmid[j, z].astype(F32)
        wfull[j, pl.ds(pl.multiple_of(me * prow, 16), prow), :] = total.astype(BF16)
        for off in range(1, n):
            gather(j, off).start()

    for c in [steps - 1, steps, steps - 2]:
        piece(c).start()
    for c in range(steps - 2):
        piece(c).start()

    def look(q, carry):
        for u in range(share // 8):
            seen_copy(q, u).start()
        return carry

    lax.fori_loop(0, steps, look, 0)
    peers = [{"ens": lax.rem(me + off, n)} for off in range(1, n)]
    peers += [{"lon": lax.rem(at + off, nl)} for off in range(1, nl)]
    barrier = pltpu.get_barrier_semaphore()
    for peer in peers:
        pl.semaphore_signal(barrier, inc=1, device_id=peer, device_id_type=MESH)
    build_band(table, band)
    lane = lax.broadcasted_iota(jnp.int32, (LAT, BLK), 1)
    ones = (lane % LAT == lax.broadcasted_iota(jnp.int32, (LAT, BLK), 0)).astype(F32)
    lat_row[...] = jnp.dot(
        jnp.broadcast_to(lat[...], (8, LAT)), ones, precision=lax.Precision.HIGHEST,
        preferred_element_type=F32,
    )
    pl.semaphore_wait(barrier, len(peers))
    halo(0).start()
    halo(1).start()
    for c in [steps - 1, steps, steps - 2]:
        piece(c).wait()
    halo(0).wait()
    halo(1).wait()
    project_edges()

    def step(s, carry):
        @pl.when(s == 1)
        def _():
            edge[...] = first_edge[...]

        @pl.when(jnp.logical_and(s >= 1, s < steps - 1))
        def _():
            piece(s - 1).wait()

        @pl.when(s < steps)
        def _():
            forward_chunk(s)

        @pl.when(s == 1)
        def _():
            build_band(table_back, band_back)

        @pl.when(s == 3)
        def _():
            weight_t[...] = padded_weight(weight).T.astype(BF16)
            spread[K * OP :, :] = jnp.zeros((PARTS * PART - K * OP, spread.shape[1]), BF16)

        @pl.when(jnp.logical_and(s >= 2, s < steps + 2))
        def _():
            slopes(s - 2)

        @pl.when(s >= steps + 1)
        def _():
            lo = jnp.minimum(2 * (s - steps - 1), 4)
            lax.fori_loop(lo, jnp.minimum(lo + 2, 4), one_grad, 0)

        @pl.when(jnp.logical_and(s >= 3, s < steps + 3))
        def _():
            for off in range(1, n):
                second(s - 3, off).wait_recv()

        @pl.when(s == 3)
        def _():
            halo(2).start()

        @pl.when(s == 4)
        def _():
            halo(3).start()
            halo(2).wait()
            for k in range(K):
                got = jnp.dot(rim_left[...], band_back[k, HALF:BLK, :], preferred_element_type=F32)
                edge_back[k] = got[:O]

        @pl.when(s >= 4)
        def _():
            backward_chunk(s - 4)

        return carry

    lax.fori_loop(0, steps + 4, step, 0)
    halo(3).wait()
    for k in range(K):
        got = jnp.dot(rim_right[...], band_back[k, BLK : BLK + HALF, :], preferred_element_type=F32)
        both = jnp.concatenate([got[:O] + edge_back[k], jnp.zeros((OP - O, BLK), F32)], axis=0)
        spread[k * OP : (k + 1) * OP, cells : cells + BLK] = both.astype(BF16)

    def one_part(j, carry):
        got = lax.dot_general(
            wide[:, HALF : HALF + cells],
            spread[pl.ds(pl.multiple_of(j * PART, PART), PART), HALF : HALF + cells],
            (((1,), (1,)), ((), ())),
            preferred_element_type=F32,
        )
        wpart[j] = got.T.astype(BF16)
        for off in range(1, n):
            scatter(j, off).start()

        @pl.when(j >= 1)
        def _():
            after_scatter(j - 1)

        @pl.when(j >= 2)
        def _():
            after_across(j - 2)

        return carry

    lax.fori_loop(0, PARTS, one_part, 0)

    def late(t, carry):
        one_grad(t, 0)

        @pl.when(t == 5)
        def _():
            after_scatter(2)
            after_across(1)

        @pl.when(t == 7)
        def _():
            after_across(2)

        return carry

    lax.fori_loop(4, steps, late, 0)
    for j in range(PARTS):
        for off in range(1, n):
            gather(j, off).wait_recv()
        wout[j * PART : (j + 1) * PART, :] = wfull[j]

    def drain(q, carry):
        for off in range(1, n):
            first(q, off).wait_send()
            second(q, off).wait_send()
        return carry

    lax.fori_loop(0, steps, drain, 0)
    for j in range(PARTS):
        for off in range(1, n):
            scatter(j, off).wait_send()
            gather(j, off).wait_send()
        for off in range(1, nl):
            across(j, off).wait_send()
    out_copy(steps - 2).wait()
    out_copy(steps - 1).wait()


def fused(n, nl, feat, weight, table, table_back, obs, lat, share):
    chan, cells = feat.shape
    steps = cells // WIDE
    vmem = pl.BlockSpec(memory_space=pltpu.VMEM)
    anywhere = pl.BlockSpec(memory_space=pl.ANY)
    dma = pltpu.SemaphoreType.DMA
    prow = PART // n
    return pl.pallas_call(
        functools.partial(fused_kernel, n, nl, share, steps),
        out_shape=(
            jax.ShapeDtypeStruct((chan, cells), BF16),
            jax.ShapeDtypeStruct((PARTS * PART, chan), BF16),
        ),
        in_specs=[anywhere, vmem, vmem, vmem, anywhere, vmem],
        out_specs=(anywhere, vmem),
        scratch_shapes=[
            pltpu.VMEM((chan, cells + BLK), BF16),
            pltpu.VMEM((K, 2 * BLK, BLK), BF16),
            pltpu.VMEM((K, 2 * BLK, BLK), BF16),
            pltpu.VMEM((chan, K * OP), BF16),
            pltpu.VMEM((8, BLK), F32),
            pltpu.VMEM((K, ROWS_P, BLK), BF16),
            pltpu.VMEM((O, BLK), F32),
            pltpu.VMEM((O, BLK), F32),
            pltpu.VMEM((K, O, BLK), F32),
            pltpu.VMEM((steps, n * share, BLK), BF16),
            pltpu.VMEM((steps, n, share, BLK), BF16),
            pltpu.VMEM((steps, n, share, BLK), BF16),
            pltpu.VMEM((steps, n * share, BLK), BF16),
            pltpu.VMEM((steps, share, BLK), F32),
            pltpu.VMEM((OP, HALF), BF16),
            pltpu.VMEM((OP, HALF), BF16),
            pltpu.VMEM((PARTS * PART, cells + BLK), BF16),
            pltpu.VMEM((2, chan, WIDE), BF16),
            pltpu.VMEM((PARTS, PART, chan), BF16),
            pltpu.VMEM((PARTS, n, prow, chan), BF16),
            pltpu.VMEM((PARTS, nl, prow, chan), BF16),
            pltpu.VMEM((PARTS, PART, chan), BF16),
            dma((steps + 1,)),
            dma((steps, share // 8)),
            dma((4,)),
            dma((4,)),
            dma((steps, n)),
            dma((steps, n)),
            dma((steps, n)),
            dma((steps, n)),
            dma((steps,)),
            dma((PARTS, n)),
            dma((PARTS, n)),
            dma((PARTS, nl)),
            dma((PARTS, nl)),
            dma((PARTS, n)),
            dma((PARTS, n)),
        ],
        compiler_params=pltpu.CompilerParams(
            collective_id=2, has_side_effects=True, vmem_limit_bytes=VMEM_LIMIT
        ),
        name="fused_decoder",
    )(feat, weight, table, table_back, obs, lat)


def fused_shards(features, proj_weight, basis_vals, row_of, col_off, observed, lat_weight):
    ne = lax.axis_size("ens")
    nl = lax.axis_size("lon")
    feat = features[0]
    chan, cells = feat.shape
    share = pl.cdiv(pl.cdiv(ROWS, ne), 16) * 16
    ahead, back = side_tables(kernel_rows(basis_vals, row_of, col_off))
    grad, part = fused(
        ne, nl, feat, proj_weight, ahead, back, observed, lat_weight.reshape(1, LAT), share
    )
    scale = 1.0 / math.sqrt(ne * (cells // LAT) * nl * LAT)
    part = part[: K * OP].reshape(K, OP, chan)[:, :O].reshape(K * O, chan)
    return (grad[None], part.astype(F32) * scale)


def shards(*args):
    cells = args[0].shape[2]
    sizes = (lax.axis_size("ens"), lax.axis_size("lon"))
    if cells % WIDE == 0 and cells // WIDE >= 8 and PART % (16 * sizes[0]) == 0 and sizes[1] > 1:
        return fused_shards(*args)
    return split_shards(*args)


def solution(mesh):
    in_specs = (P("ens", None, "lon"), P(), P(), P(), P(), P(None, "lon"), P())
    out_specs = (P("ens", None, "lon"), P())
    return jax.shard_map(shards, mesh=mesh, in_specs=in_specs, out_specs=out_specs, check_vma=False)
```

```python
import functools
import math

import jax
import jax.numpy as jnp
from jax import lax
from jax.experimental import pallas as pl
from jax.experimental.pallas import tpu as pltpu
from jax.sharding import PartitionSpec as P

O = 72
OP = 80
K = 9
R = 4
LAT = 32
SMOOTH = 0.25
BLK = 256
HALF = 128
F32 = jnp.float32
BF16 = jnp.bfloat16
MESH = pl.DeviceIdType.MESH
VMEM_LIMIT = 60 * 1024 * 1024


def whole(shape):
    return pl.BlockSpec(shape, lambda s: (0,) * len(shape))


def kernel_rows(basis_vals, row_of, col_off):
    code = (col_off + R) * LAT + row_of
    ids = jnp.arange((2 * R + 1) * LAT, dtype=jnp.int32)
    hit = (code[:, :, None] == ids[None, None, :]).astype(F32)
    table = jnp.einsum("isk,isq->ikq", basis_vals, hit, precision=lax.Precision.HIGHEST)
    return table.astype(BF16)


def side_tables(table):
    taps = 2 * R + 1
    four = table.reshape(LAT, K, taps, LAT)
    ahead = four.transpose(1, 2, 3, 0).reshape(K, taps * LAT, LAT)
    back = four[:, :, ::-1].transpose(1, 2, 0, 3).reshape(K, taps * LAT, LAT)
    return ahead, back


def build_band(table, band):
    lane = lax.broadcasted_iota(jnp.int32, (LAT, BLK), 1)
    spread_lanes = (lane % LAT == lax.broadcasted_iota(jnp.int32, (LAT, BLK), 0)).astype(F32)
    spread_lanes = spread_lanes.astype(BF16)
    place = lane // LAT
    cols = BLK // LAT

    def one(k, carry):
        tiled = jnp.dot(table[k], spread_lanes, preferred_element_type=F32)
        for e in range(2 * cols):
            block = jnp.zeros((LAT, BLK), F32)
            for j in range(cols):
                d = e - j
                if 0 <= d <= 2 * R:
                    block = jnp.where(place == j, tiled[d * LAT : (d + 1) * LAT], block)
            band[k, e * LAT : (e + 1) * LAT, :] = block.astype(BF16)
        return carry

    lax.fori_loop(0, K, one, 0)


def padded_weight(weight):
    wide = weight[...].astype(F32)
    gap = jnp.zeros((OP - O, wide.shape[1]), F32)
    rows = []
    for k in range(K):
        rows += [wide[k * O : (k + 1) * O], gap]
    return jnp.concatenate(rows, axis=0)


def greet(peers):
    barrier = pltpu.get_barrier_semaphore()
    for peer in peers:
        pl.semaphore_signal(barrier, inc=1, device_id=peer, device_id_type=MESH)
    pl.semaphore_wait(barrier, len(peers))


def forward_kernel(
    n, nl, group, steps, share,
    feat, tail, head, weight, table, obs, lat, out, rims,
    wpad, band, proj, dec, flat, recv, send, cot, left, right, rim_left, rim_right,
    ssem1, rsem1, ssem2, rsem2, hsend, hrecv,
):
    s = pl.program_id(0)
    me = lax.axis_index("ens")
    real = group * 2 * O
    own = pl.multiple_of(me * share, 16)
    after = {"lon": lax.rem(lax.axis_index("lon") + 1, nl)}
    before = {"lon": lax.rem(lax.axis_index("lon") + nl - 1, nl)}

    def rim(src, dst, slot, peer):
        return pltpu.make_async_remote_copy(
            src_ref=src,
            dst_ref=dst,
            send_sem=hsend.at[slot],
            recv_sem=hrecv.at[slot],
            device_id=peer,
            device_id_type=MESH,
        )

    def first(q, off):
        peer = lax.rem(me + off, n)
        return pltpu.make_async_remote_copy(
            src_ref=dec.at[q, pl.ds(pl.multiple_of(peer * share, 16), share)],
            dst_ref=recv.at[q, off],
            send_sem=ssem1.at[q, off],
            recv_sem=rsem1.at[q, off],
            device_id={"ens": peer},
            device_id_type=MESH,
        )

    def second(q, off):
        return pltpu.make_async_remote_copy(
            src_ref=send.at[q, off],
            dst_ref=cot.at[q, pl.ds(own, share)],
            send_sem=ssem2.at[q, off],
            recv_sem=rsem2.at[q, off],
            device_id={"ens": lax.rem(me - off + n, n)},
            device_id_type=MESH,
        )

    def put(values, h, lo):
        for k in range(K):
            proj[k, h, :, lo : lo + HALF] = values[k * OP : (k + 1) * OP].astype(BF16)

    @pl.when(s == 0)
    def _():
        greet([{"ens": lax.rem(me + off, n)} for off in range(1, n)] + [after, before])
        rim(tail, left, 0, after).start()
        rim(head, right, 1, before).start()
        wpad[...] = padded_weight(weight).astype(BF16)
        build_band(table, band)
        if n * share > real:
            for q in range(steps):
                dec[q, real:, :] = jnp.zeros((n * share - real, HALF), BF16)
            flat[real:, :] = jnp.zeros((n * share - real, HALF), F32)

    @pl.when(s < steps)
    def _():
        def one(b, carry):
            lanes = pl.ds(pl.multiple_of(b * BLK, BLK), BLK)
            got = jnp.dot(wpad[...], feat[:, lanes], preferred_element_type=F32)
            h = s * group + b
            put(got[:, :HALF], h, HALF)
            put(got[:, HALF:], h + 1, 0)
            return carry

        lax.fori_loop(0, group, one, 0)

    @pl.when(s == 1)
    def _():
        rim(tail, left, 0, after).wait()
        put(jnp.dot(wpad[...], left[...], preferred_element_type=F32), 0, 0)

    @pl.when(s == steps)
    def _():
        rim(head, right, 1, before).wait()
        put(jnp.dot(wpad[...], right[...], preferred_element_type=F32), steps * group, HALF)

    @pl.when(jnp.logical_and(s > 0, s <= steps))
    def _():
        q = s - 1
        g0 = q * group
        acc = jnp.zeros((group * OP, BLK), F32)
        for k in range(K):
            for part in range(2):
                lhs = proj[k, pl.ds(g0 + part, group)].reshape(group * OP, BLK)
                acc = acc + jnp.dot(
                    lhs, band[k, part * BLK : (part + 1) * BLK, :], preferred_element_type=F32
                )
        for g in range(group):
            piece = acc[g * OP : g * OP + O]
            both = jnp.concatenate([piece[:, :HALF], piece[:, HALF:]], axis=0)
            dec[q, g * 2 * O : (g + 1) * 2 * O, :] = both.astype(BF16)
        for off in range(1, n):
            first(q, off).start()

    @pl.when(s > 1)
    def _():
        q = s - 2
        for t in range(2 * group):
            flat[t * O : (t + 1) * O, :] = obs[:, t * HALF : (t + 1) * HALF]
        for off in range(1, n):
            first(q, off).wait_recv()
        lat_row = jnp.broadcast_to(lat[0:1, :], (16, HALF))

        def smooth(diff):
            return diff * lax.rsqrt(diff * diff + SMOOTH * SMOOTH)

        def one(step, carry):
            at = pl.multiple_of(step * 16, 16)
            here = pl.ds(pl.multiple_of(own + at, 16), 16)
            values = [dec[q, here, :].astype(F32)]
            values += [recv[q, off, pl.ds(at, 16), :].astype(F32) for off in range(1, n)]
            sums = [None] * n
            for a in range(n):
                for b in range(a + 1, n):
                    pair = smooth(values[a] - values[b])
                    sums[a] = pair if sums[a] is None else sums[a] + pair
                    sums[b] = -pair if sums[b] is None else sums[b] - pair
            target = flat[here, :]
            for a in range(n):
                slope = smooth(values[a] - target) - sums[a] * (1.0 / (n - 1))
                result = (slope * lat_row).astype(BF16)
                if a == 0:
                    cot[q, here, :] = result
                else:
                    send[q, a, pl.ds(at, 16), :] = result
            return carry

        lax.fori_loop(0, share // 16, one, 0)
        for off in range(1, n):
            second(q, off).start()

    @pl.when(s == steps + 1)
    def _():
        for q in range(steps):
            for off in range(1, n):
                first(q, off).wait_send()
                second(q, off).wait()
        last = rim(cot.at[steps - 1, pl.ds(real - OP, OP)], rim_left, 2, after)
        opening = rim(cot.at[0, pl.ds(0, OP)], rim_right, 3, before)
        last.start()
        opening.start()
        for q in range(steps):
            out[q * n * share : (q + 1) * n * share, :] = cot[q]
        last.wait()
        opening.wait()
        rims[0] = rim_left[...]
        rims[1] = rim_right[...]


def forward(n, nl, feat, tail, head, weight, table, obs, lat, group, steps, share):
    chan = feat.shape[0]
    wide = group * BLK
    rows = n * share
    sem = pltpu.SemaphoreType.DMA((steps, n))
    return pl.pallas_call(
        functools.partial(forward_kernel, n, nl, group, steps, share),
        out_shape=(
            jax.ShapeDtypeStruct((steps * rows, HALF), BF16),
            jax.ShapeDtypeStruct((2, OP, HALF), BF16),
        ),
        grid=(steps + 2,),
        in_specs=[
            pl.BlockSpec((chan, wide), lambda s: (0, jnp.minimum(s, steps - 1))),
            whole(tail.shape),
            whole(head.shape),
            whole(weight.shape),
            whole(table.shape),
            pl.BlockSpec((O, wide), lambda s: (0, jnp.clip(s - 2, 0, steps - 1))),
            whole(lat.shape),
        ],
        out_specs=(whole((steps * rows, HALF)), whole((2, OP, HALF))),
        scratch_shapes=[
            pltpu.VMEM((K * OP, chan), BF16),
            pltpu.VMEM((K, 2 * BLK, BLK), BF16),
            pltpu.VMEM((K, steps * group + 1, OP, BLK), BF16),
            pltpu.VMEM((steps, rows, HALF), BF16),
            pltpu.VMEM((rows, HALF), F32),
            pltpu.VMEM((steps, n, share, HALF), BF16),
            pltpu.VMEM((steps, n, share, HALF), BF16),
            pltpu.VMEM((steps, rows, HALF), BF16),
            pltpu.VMEM((chan, HALF), BF16),
            pltpu.VMEM((chan, HALF), BF16),
            pltpu.VMEM((OP, HALF), BF16),
            pltpu.VMEM((OP, HALF), BF16),
            sem,
            sem,
            sem,
            sem,
            pltpu.SemaphoreType.DMA((4,)),
            pltpu.SemaphoreType.DMA((4,)),
        ],
        compiler_params=pltpu.CompilerParams(
            collective_id=0, has_side_effects=True, vmem_limit_bytes=VMEM_LIMIT
        ),
        name="forward_slopes",
    )(feat, tail, head, weight, table, obs, lat)


WG_ROWS = 2048
WG_PART = 656


def backward_kernel(
    group, steps, piece, share, cells, padded,
    cot, left, right, weight, table, feat, grad, wgrad,
    weight_t, band, ext, spread, acc,
):
    s = pl.program_id(0)
    blocks = steps * group

    @pl.when(s == 0)
    def _():
        ext[:, O:, :] = jnp.zeros((blocks + 1, OP - O, BLK), BF16)
        ext[0, :O, :HALF] = left[...].astype(F32)[OP - O :].astype(BF16)
        ext[blocks, :O, HALF:] = right[:O]

        weight_t[...] = padded_weight(weight).T.astype(BF16)
        build_band(table, band)

        def one(b, carry):
            start = lax.div(b, piece) * share + lax.rem(b, piece) * (2 * O)
            pair = cot[pl.ds(pl.multiple_of(start, 16), 2 * O), :].astype(F32)
            ext[b, :O, HALF:] = pair[:O].astype(BF16)
            ext[b + 1, :O, :HALF] = pair[O:].astype(BF16)
            return carry

        lax.fori_loop(0, blocks, one, 0)
        acc[...] = jnp.zeros_like(acc)

    g0 = s * group
    for k in range(K):
        got = jnp.zeros((group * OP, BLK), F32)
        for part in range(2):
            lhs = ext[pl.ds(g0 + part, group)].reshape(group * OP, BLK)
            got = got + jnp.dot(
                lhs, band[k, part * BLK : (part + 1) * BLK, :], preferred_element_type=F32
            )
        if padded:
            row = lax.broadcasted_iota(jnp.int32, got.shape, 0) // OP
            lane = lax.broadcasted_iota(jnp.int32, got.shape, 1)
            got = jnp.where((g0 + row) * BLK + lane < cells, got, 0.0)
        got = got.astype(BF16)
        for g in range(group):
            spread[k * OP : (k + 1) * OP, g * BLK : (g + 1) * BLK] = got[g * OP : (g + 1) * OP]

    acc[...] += lax.dot_general(
        spread[...], feat[...], (((1,), (1,)), ((), ())), preferred_element_type=F32
    )

    def one_grad(n, carry):
        lanes = pl.ds(pl.multiple_of(n * BLK, BLK), BLK)
        grad[:, lanes] = jnp.dot(
            weight_t[...], spread[:, lanes], preferred_element_type=F32
        ).astype(BF16)
        return carry

    lax.fori_loop(0, group, one_grad, 0)

    @pl.when(s == steps - 1)
    def _():
        parts = acc.shape[1] // HALF
        wgrad[parts * WG_PART - 16 :, :] = jnp.zeros((WG_ROWS - parts * WG_PART + 16, HALF), BF16)
        for t in range(parts):
            rows = [
                acc[k * OP : k * OP + O, t * HALF : (t + 1) * HALF] for k in range(K)
            ] + [jnp.zeros((8, HALF), F32)]
            wgrad[t * WG_PART : (t + 1) * WG_PART, :] = jnp.concatenate(rows, axis=0).astype(BF16)


def backward(cot, left, right, weight, table, feat, group, steps, piece, cells):
    chan = feat.shape[0]
    wide = group * BLK
    blocks = steps * group
    return pl.pallas_call(
        functools.partial(
            backward_kernel,
            group,
            steps,
            piece,
            cot.shape[0] * piece // blocks,
            cells,
            cells != blocks * BLK,
        ),
        out_shape=(
            jax.ShapeDtypeStruct(feat.shape, BF16),
            jax.ShapeDtypeStruct((WG_ROWS, HALF), BF16),
        ),
        grid=(steps,),
        in_specs=[
            whole(cot.shape),
            whole(left.shape),
            whole(right.shape),
            whole(weight.shape),
            whole(table.shape),
            pl.BlockSpec((chan, wide), lambda s: (0, s)),
        ],
        out_specs=(pl.BlockSpec((chan, wide), lambda s: (0, s)), whole((WG_ROWS, HALF))),
        scratch_shapes=[
            pltpu.VMEM((chan, K * OP), BF16),
            pltpu.VMEM((K, 2 * BLK, BLK), BF16),
            pltpu.VMEM((blocks + 1, OP, BLK), BF16),
            pltpu.VMEM((K * OP, wide), BF16),
            pltpu.VMEM((K * OP, chan), F32),
        ],
        compiler_params=pltpu.CompilerParams(vmem_limit_bytes=VMEM_LIMIT),
        name="backward_conv",
    )(cot, left, right, weight, table, feat)


def reduce_kernel(ne, nl, scale, part, out, recv1, mid, recv2, got, *sems):
    (ss1, rs1, ss2, rs2, ss3, rs3, ss4, rs4) = sems
    me = lax.axis_index("ens")
    at = lax.axis_index("lon")
    rows = WG_ROWS // ne
    small = rows // nl
    ens_peers = [{"ens": lax.rem(me + off, ne)} for off in range(1, ne)]
    lon_peers = [{"lon": lax.rem(at + off, nl)} for off in range(1, nl)]
    greet(ens_peers + lon_peers)

    def run(copies):
        for copy in copies:
            copy.start()
        for copy in copies:
            copy.wait()

    def send(src, dst, ssem, rsem, peer):
        return pltpu.make_async_remote_copy(
            src_ref=src, dst_ref=dst, send_sem=ssem, recv_sem=rsem, device_id=peer, device_id_type=MESH
        )

    own = pl.multiple_of(me * rows, 16)
    mine = pl.multiple_of(at * small, 8)
    run(
        [
            send(
                part.at[pl.ds(pl.multiple_of(lax.rem(me + off, ne) * rows, 16), rows)],
                recv1.at[off],
                ss1.at[off],
                rs1.at[off],
                {"ens": lax.rem(me + off, ne)},
            )
            for off in range(1, ne)
        ]
    )
    total = part[pl.ds(own, rows), :].astype(F32)
    for off in range(1, ne):
        total = total + recv1[off].astype(F32)
    mid[...] = total
    run(
        [
            send(
                mid.at[pl.ds(pl.multiple_of(lax.rem(at + off, nl) * small, 8), small)],
                recv2.at[off],
                ss2.at[off],
                rs2.at[off],
                {"lon": lax.rem(at + off, nl)},
            )
            for off in range(1, nl)
        ]
    )
    total = mid[pl.ds(mine, small), :]
    for off in range(1, nl):
        total = total + recv2[off]
    recv2[0] = total
    gat = got[1]
    gat[pl.ds(mine, small), :] = total
    run(
        [
            send(
                recv2.at[0],
                gat.at[pl.ds(mine, small)],
                ss3.at[off],
                rs3.at[off],
                {"lon": lax.rem(at + off, nl)},
            )
            for off in range(1, nl)
        ]
    )
    full = got[0]
    full[pl.ds(own, rows), :] = gat[...].astype(BF16)
    run(
        [
            send(
                full.at[pl.ds(own, rows)],
                full.at[pl.ds(own, rows)],
                ss4.at[off],
                rs4.at[off],
                {"ens": lax.rem(me + off, ne)},
            )
            for off in range(1, ne)
        ]
    )
    for t in range(out.shape[1] // HALF):
        piece = full[t * WG_PART : (t + 1) * WG_PART, :].astype(F32) * scale
        out[:, t * HALF : (t + 1) * HALF] = piece[: K * O]


def reduced(ne, nl, scale, part, chan):
    vmem = pl.BlockSpec(memory_space=pltpu.VMEM)
    rows = WG_ROWS // ne
    small = rows // nl

    def body(part, out, recv1, mid, recv2, full, gat, *sems):
        reduce_kernel(ne, nl, scale, part, out, recv1, mid, recv2, (full, gat), *sems)

    return pl.pallas_call(
        body,
        out_shape=jax.ShapeDtypeStruct((K * O, chan), F32),
        in_specs=[vmem],
        out_specs=vmem,
        scratch_shapes=[
            pltpu.VMEM((ne, rows, HALF), BF16),
            pltpu.VMEM((rows, HALF), F32),
            pltpu.VMEM((nl, small, HALF), F32),
            pltpu.VMEM((WG_ROWS, HALF), BF16),
            pltpu.VMEM((rows, HALF), F32),
        ]
        + [pltpu.SemaphoreType.DMA((n,)) for n in (ne, ne, nl, nl, nl, nl, ne, ne)],
        compiler_params=pltpu.CompilerParams(
            collective_id=1, has_side_effects=True, vmem_limit_bytes=VMEM_LIMIT
        ),
        name="weight_reduce",
    )(part)


def passed_along(value, axis, steps):
    count = lax.axis_size(axis)
    return lax.ppermute(value, axis, [(i, (i + steps) % count) for i in range(count)])


def split_shards(features, proj_weight, basis_vals, row_of, col_off, observed, lat_weight):
    ne = lax.axis_size("ens")
    nl = lax.axis_size("lon")
    assert features.shape[0] == 1
    feat = features[0]
    chan, cells = feat.shape
    aligned = cells % BLK == 0
    blocks = cells // BLK if aligned else pl.cdiv(cells + HALF, BLK)
    group_back = max(g for g in range(1, 10) if blocks % g == 0)
    steps_back = blocks // group_back
    group = max(g for g in range(1, 7) if blocks % g == 0)
    steps = blocks // group
    real = group * 2 * O
    share = pl.cdiv(pl.cdiv(real, ne), 16) * 16
    rows = ne * share
    extra = blocks * BLK - cells

    tail = feat[:, cells - HALF :]
    head = feat[:, :HALF]
    ahead, back = side_tables(kernel_rows(basis_vals, row_of, col_off))
    if not aligned:
        right = passed_along(head, "lon", -1)
        feat = jnp.pad(jnp.concatenate([feat, right], axis=1), ((0, 0), (0, extra - HALF)))
        observed = jnp.pad(observed, ((0, 0), (0, extra)))
    lat = jnp.broadcast_to(jnp.tile(lat_weight, HALF // LAT)[None, :], (8, HALF))
    cot, rims = forward(
        ne, nl, feat, tail, head, proj_weight, ahead, observed, lat, group, steps, share
    )

    if aligned:
        cot_left, cot_right = rims[0], rims[1]
    else:
        flat = cot.reshape(steps, rows, HALF)[:, :real].reshape(2 * blocks, O, HALF)
        flat = flat.transpose(1, 0, 2).reshape(O, blocks * BLK)[:, :cells]
        cot_left = passed_along(flat[:, cells - HALF :], "lon", 1)
        cot_right = passed_along(flat[:, :HALF], "lon", -1)
        flat = jnp.pad(
            jnp.concatenate([flat, cot_right], axis=1), ((0, 0), (0, extra - HALF))
        )
        flat = flat.reshape(O, 2 * blocks, HALF).transpose(1, 0, 2).reshape(steps, real, HALF)
        cot = jnp.pad(flat, ((0, 0), (0, rows - real), (0, 0))).reshape(steps * rows, HALF)
        cot_left = jnp.pad(cot_left, ((OP - O, 0), (0, 0)))
        cot_right = jnp.zeros((OP, HALF), BF16)
    grad, part = backward(
        cot, cot_left, cot_right, proj_weight, back, feat, group_back, steps_back, group, cells
    )
    scale = 1.0 / math.sqrt(ne * (cells // LAT) * nl * LAT)
    weight_grad = reduced(ne, nl, scale, part, chan)
    return (grad[:, :cells][None], weight_grad)


GROUP = 5
WIDE = GROUP * BLK
ROWS = GROUP * O
ROWS_P = ROWS + 8
MAIN = 64
LEFT = O - MAIN
SPLIT = GROUP * MAIN
TOPS = K * MAIN
USED = K * O + 8
PART = 256
PARTS = 3


def ordered_weight(weight):
    rows = weight[...].astype(F32)
    parts = [rows[k * O : k * O + MAIN] for k in range(K)]
    parts += [rows[k * O + MAIN : (k + 1) * O] for k in range(K)]
    return jnp.concatenate(parts, axis=0)


def fused_kernel(
    n, nl, share, steps,
    feat, weight, table, table_back, obs, lat, grad, wout,
    wide, wrows, band, band_back, weight_t, lat_row, proj, sums, edge, first_edge, extra, edge_back,
    give, take, dec, recv, send, cot, seen, rim_left, rim_top, rim_low, spread, gout,
    wpart, wrecv, wmid, wfull,
    fsem, osem, hsend, hrecv, ssem1, rsem1, ssem2, rsem2, gsem,
    ws1, wr1, ws2, wr2, ws3, wr3,
):
    me = lax.axis_index("ens")
    at = lax.axis_index("lon")
    cells = steps * WIDE
    chan = feat.shape[0]
    own = pl.multiple_of(me * share, 16)
    after = {"lon": lax.rem(at + 1, nl)}
    before = {"lon": lax.rem(at + nl - 1, nl)}
    prow = PART // n

    def remote(src, dst, ssem, rsem, peer):
        return pltpu.make_async_remote_copy(
            src_ref=src, dst_ref=dst, send_sem=ssem, recv_sem=rsem, device_id=peer, device_id_type=MESH
        )

    def piece(c):
        if isinstance(c, int) and c == steps:
            return pltpu.make_async_copy(
                feat.at[:, pl.ds(0, HALF)], wide.at[:, pl.ds(HALF, HALF)], fsem.at[steps]
            )
        if isinstance(c, int) and c == steps - 1:
            lo, size = c * WIDE, WIDE - HALF
        else:
            lo, size = c * WIDE, WIDE
        return pltpu.make_async_copy(
            feat.at[:, pl.ds(pl.multiple_of(lo + HALF, HALF), size)],
            wide.at[:, pl.ds(pl.multiple_of(lo + 2 * HALF, HALF), size)],
            fsem.at[c],
        )

    def seen_copy(q, u):
        c = lax.rem(q + steps - 1, steps)
        t = jnp.minimum(me * (share // 8) + u, ROWS // 8 - 1)
        low = t // (SPLIT // 8)
        row = pl.multiple_of((1 - low) * (t % (MAIN // 8)) * 8 + low * MAIN, 8)
        block = (1 - low) * (t // (MAIN // 8)) + low * (ROWS // 8 - 1 - t)
        lane = pl.multiple_of(c * WIDE + block * BLK, BLK)
        return pltpu.make_async_copy(
            obs.at[pl.ds(row, 8), pl.ds(lane, BLK)], seen.at[q, pl.ds(u * 8, 8)], osem.at[q, u]
        )

    def first(q, off):
        peer = lax.rem(me + off, n)
        return remote(
            dec.at[q, pl.ds(pl.multiple_of(peer * share, 16), share)],
            recv.at[q, off], ssem1.at[q, off], rsem1.at[q, off], {"ens": peer},
        )

    def second(q, off):
        return remote(
            send.at[q, off], cot.at[q, pl.ds(own, share)],
            ssem2.at[q, off], rsem2.at[q, off], {"ens": lax.rem(me - off + n, n)},
        )

    def halo(slot):
        if slot == 0:
            src, dst, peer = give.at[0], take.at[0], after
        elif slot == 1:
            src, dst, peer = give.at[1], take.at[1], before
        elif slot == 2:
            src = cot.at[0, pl.ds(SPLIT - MAIN, MAIN + 16), pl.ds(HALF, HALF)]
            dst, peer = rim_left, after
        elif slot == 3:
            src, dst, peer = cot.at[1, pl.ds(0, MAIN), pl.ds(0, HALF)], rim_top, before
        else:
            src = cot.at[1, pl.ds(ROWS - LEFT, 16), pl.ds(0, HALF)]
            dst, peer = rim_low, before
        return remote(src, dst, hsend.at[slot], hrecv.at[slot], peer)

    def out_copy(t):
        return pltpu.make_async_copy(
            gout.at[lax.rem(t, 2)], grad.at[:, pl.ds(pl.multiple_of(t * WIDE, WIDE), WIDE)], gsem.at[t]
        )

    def scatter(j, off):
        peer = lax.rem(me + off, n)
        return remote(
            wpart.at[j, pl.ds(pl.multiple_of(peer * prow, 16), prow)], wrecv.at[j, off],
            ws1.at[j, off], wr1.at[j, off], {"ens": peer},
        )

    def across(j, off):
        return remote(
            wmid.at[j, at], wmid.at[j, at], ws2.at[j, off], wr2.at[j, off], {"lon": lax.rem(at + off, nl)}
        )

    def gather(j, off):
        mine = pl.ds(pl.multiple_of(me * prow, 16), prow)
        return remote(
            wfull.at[j, mine], wfull.at[j, mine], ws3.at[j, off], wr3.at[j, off],
            {"ens": lax.rem(me + off, n)},
        )

    def project_edges():
        start = (steps - 1) * WIDE
        lanes = jnp.concatenate(
            [wide[:, HALF:BLK], wide[:, cells : cells + HALF], wide[:, start : start + BLK]], axis=1
        )
        got = jnp.dot(wrows[...], lanes, preferred_element_type=F32)
        acc = jnp.zeros((3 * O, BLK), F32)
        out = jnp.zeros((O, BLK), F32)
        none = jnp.zeros((O, HALF), F32)
        for k in range(K):
            part = jnp.concatenate(
                [got[k * MAIN : (k + 1) * MAIN], got[TOPS + k * LEFT : TOPS + (k + 1) * LEFT]], axis=0
            )
            head = jnp.concatenate([none, part[:, :HALF]], axis=1)
            tail = jnp.concatenate([part[:, HALF:BLK], none], axis=1)
            lhs = jnp.concatenate([head, tail, part[:, BLK:]], axis=0).astype(BF16)
            acc = acc + jnp.dot(lhs, band[k, :BLK, :], preferred_element_type=F32)
            out = out + jnp.dot(head.astype(BF16), band[k, BLK:, :], preferred_element_type=F32)
        first_edge[...] = acc[:O]
        edge[...] = acc[2 * O :]
        give[0] = acc[O : 2 * O, :HALF]
        give[1] = out[:, HALF:]
        halo(0).start()
        halo(1).start()

    def forward_chunk(q):
        c = lax.rem(q + steps - 1, steps)
        got = jnp.dot(
            wrows[...],
            wide[:, pl.ds(pl.multiple_of(c * WIDE + BLK, BLK), WIDE)],
            preferred_element_type=F32,
        )
        gap = jnp.zeros((ROWS_P - ROWS, BLK), F32)
        tops = got[:TOPS].astype(BF16)
        for k in range(K):
            for g in range(GROUP):
                proj[k, g * MAIN : (g + 1) * MAIN, :] = tops[
                    k * MAIN : (k + 1) * MAIN, g * BLK : (g + 1) * BLK
                ]
            lows = [
                got[TOPS + k * LEFT : TOPS + (k + 1) * LEFT, g * BLK : (g + 1) * BLK]
                for g in reversed(range(GROUP))
            ]
            proj[k, SPLIT:, :] = jnp.concatenate(lows + [gap], axis=0).astype(BF16)
        for half in range(2):
            acc = jnp.zeros((ROWS_P, BLK), F32)
            for k in range(K):
                acc = acc + jnp.dot(
                    proj[k], band[k, half * BLK : (half + 1) * BLK, :], preferred_element_type=F32
                )
            sums[half] = acc

        @pl.when(q == 0)
        def _():
            halo(1).wait()
            extra[:, HALF:] = take[1]

        @pl.when(q == 1)
        def _():
            halo(0).wait()
            extra[...] = jnp.zeros_like(extra)
            edge[...] = first_edge[...]
            edge[:, :HALF] += take[0]

        last = SPLIT - MAIN
        dec[q, :last, :] = (
            jnp.concatenate([edge[:MAIN], sums[0, : last - MAIN]], axis=0) + sums[1, :last]
        ).astype(BF16)
        dec[q, last:SPLIT, :] = (
            sums[0, last - MAIN : last] + sums[1, last:SPLIT] + extra[:MAIN]
        ).astype(BF16)
        lows = jnp.concatenate([sums[0, SPLIT + LEFT : ROWS], edge[MAIN:]], axis=0) + sums[1, SPLIT:ROWS]
        lows = [lows[:LEFT] + extra[MAIN:], lows[LEFT:]]
        rest = jnp.zeros((n * share - ROWS, BLK), F32)
        dec[q, SPLIT:, :] = jnp.concatenate(lows + [rest], axis=0).astype(BF16)
        edge[...] = sums[0, last : SPLIT + LEFT]
        for off in range(1, n):
            first(q, off).start()

    def smooth(diff):
        return diff * lax.rsqrt(diff * diff + SMOOTH * SMOOTH)

    def slopes(q):
        for u in range(share // 8):
            seen_copy(q, u).wait()
        for off in range(1, n):
            first(q, off).wait_recv()

        def one(step, carry):
            row = pl.multiple_of(lax.div(step, 2) * 16, 16)
            lanes = pl.ds(pl.multiple_of(lax.rem(step, 2) * HALF, HALF), HALF)
            here = pl.ds(pl.multiple_of(own + row, 16), 16)
            values = [dec[q, here, lanes].astype(F32)]
            values += [recv[q, off, pl.ds(row, 16), lanes].astype(F32) for off in range(1, n)]
            sums = [None] * n
            for a in range(n):
                for b in range(a + 1, n):
                    pair = smooth(values[a] - values[b])
                    sums[a] = pair if sums[a] is None else sums[a] + pair
                    sums[b] = -pair if sums[b] is None else sums[b] - pair
            target = seen[q, pl.ds(row, 16), lanes]
            area = jnp.broadcast_to(lat_row[0:1, lanes], (16, HALF))
            for a in range(n):
                slope = smooth(values[a] - target) - sums[a] * (1.0 / (n - 1))
                result = (slope * area).astype(BF16)
                if a == 0:
                    cot[q, here, lanes] = result
                else:
                    send[q, a, pl.ds(row, 16), lanes] = result
            return carry

        lax.fori_loop(0, share // 16 * 2, one, 0)
        for off in range(1, n):
            second(q, off).start()

    def store_lows(lows, lanes):
        both = jnp.concatenate(lows + [jnp.zeros((USED - K * O, BLK), F32)], axis=0)
        spread[TOPS:USED, lanes] = both.astype(BF16)

    def backward_chunk(b):
        q = lax.rem(b + 1, steps)
        lhs = cot[q, pl.ds(0, ROWS_P), :]
        lows = [[] for _ in range(GROUP)]
        for k in range(K):
            ahead = jnp.dot(lhs, band_back[k, :BLK, :], preferred_element_type=F32)
            here = jnp.dot(lhs, band_back[k, BLK:, :], preferred_element_type=F32)
            for g in range(GROUP):
                low = SPLIT + (GROUP - 1 - g) * LEFT
                top = edge_back[k, :MAIN] if g == 0 else ahead[(g - 1) * MAIN : g * MAIN]
                end = edge_back[k, MAIN:] if g == 0 else ahead[low + LEFT : low + 2 * LEFT]
                lanes = pl.ds(pl.multiple_of(b * WIDE + g * BLK, BLK), BLK)
                spread[k * MAIN : (k + 1) * MAIN, lanes] = (
                    here[g * MAIN : (g + 1) * MAIN] + top
                ).astype(BF16)
                lows[g].append(here[low : low + LEFT] + end)
            edge_back[k] = ahead[SPLIT - MAIN : SPLIT + LEFT]
        for g in range(GROUP):
            store_lows(lows[g], pl.ds(pl.multiple_of(b * WIDE + g * BLK, BLK), BLK))

    def one_grad(t, carry):
        @pl.when(t >= 2)
        def _():
            out_copy(t - 2).wait()

        lanes = pl.ds(pl.multiple_of(t * WIDE + HALF, HALF), WIDE)
        gout[lax.rem(t, 2)] = jnp.dot(
            weight_t[:, :USED], spread[:USED, lanes], preferred_element_type=F32
        ).astype(BF16)
        out_copy(t).start()
        return carry

    def after_scatter(j):
        for off in range(1, n):
            scatter(j, off).wait_recv()
        total = wpart[j, pl.ds(pl.multiple_of(me * prow, 16), prow), :].astype(F32)
        for off in range(1, n):
            total = total + wrecv[j, off].astype(F32)
        wmid[j, at] = total.astype(BF16)
        for off in range(1, nl):
            across(j, off).start()

    def after_across(j):
        for off in range(1, nl):
            across(j, off).wait_recv()
        total = wmid[j, 0].astype(F32)
        for z in range(1, nl):
            total = total + wmid[j, z].astype(F32)
        wfull[j, pl.ds(pl.multiple_of(me * prow, 16), prow), :] = total.astype(BF16)
        for off in range(1, n):
            gather(j, off).start()

    for c in [steps - 1, steps, steps - 2]:
        piece(c).start()
    for c in range(steps - 2):
        piece(c).start()

    def look(q, carry):
        for u in range(share // 8):
            seen_copy(q, u).start()
        return carry

    lax.fori_loop(0, steps, look, 0)
    peers = [{"ens": lax.rem(me + off, n)} for off in range(1, n)]
    peers += [{"lon": lax.rem(at + off, nl)} for off in range(1, nl)]
    barrier = pltpu.get_barrier_semaphore()
    for peer in peers:
        pl.semaphore_signal(barrier, inc=1, device_id=peer, device_id_type=MESH)
    build_band(table, band)
    lane = lax.broadcasted_iota(jnp.int32, (LAT, BLK), 1)
    ones = (lane % LAT == lax.broadcasted_iota(jnp.int32, (LAT, BLK), 0)).astype(F32)
    lat_row[...] = jnp.dot(
        jnp.broadcast_to(lat[...], (8, LAT)), ones, precision=lax.Precision.HIGHEST,
        preferred_element_type=F32,
    )
    wrows[...] = ordered_weight(weight).astype(BF16)
    wide[:, :HALF] = jnp.zeros((chan, HALF), BF16)
    wide[:, cells + HALF :] = jnp.zeros((chan, HALF), BF16)
    extra[...] = jnp.zeros_like(extra)
    for c in [steps - 1, steps, steps - 2]:
        piece(c).wait()
    pl.semaphore_wait(barrier, len(peers))
    project_edges()

    def step(s, carry):
        @pl.when(jnp.logical_and(s >= 1, s < steps - 1))
        def _():
            piece(s - 1).wait()

        @pl.when(s < steps)
        def _():
            forward_chunk(s)

        @pl.when(s == 1)
        def _():
            build_band(table_back, band_back)

        @pl.when(s == 3)
        def _():
            gap = jnp.zeros((PARTS * PART - K * O, chan), F32)
            rows = jnp.concatenate([ordered_weight(weight), gap], axis=0)
            weight_t[...] = rows.T.astype(BF16)
            spread[USED:, :] = jnp.zeros((PARTS * PART - USED, spread.shape[1]), BF16)

        @pl.when(jnp.logical_and(s >= 2, s < steps + 2))
        def _():
            slopes(s - 2)

        @pl.when(s >= steps + 1)
        def _():
            lo = jnp.minimum(2 * (s - steps - 1), 4)
            lax.fori_loop(lo, jnp.minimum(lo + 2, 4), one_grad, 0)

        @pl.when(jnp.logical_and(s >= 3, s < steps + 3))
        def _():
            for off in range(1, n):
                second(s - 3, off).wait_recv()

        @pl.when(s == 3)
        def _():
            halo(2).start()

        @pl.when(s == 4)
        def _():
            halo(3).start()
            halo(4).start()
            halo(2).wait()
            for k in range(K):
                got = jnp.dot(rim_left[...], band_back[k, HALF:BLK, :], preferred_element_type=F32)
                edge_back[k] = got[:O]

        @pl.when(s >= 4)
        def _():
            backward_chunk(s - 4)

        return carry

    lax.fori_loop(0, steps + 4, step, 0)
    halo(3).wait()
    halo(4).wait()
    rim = jnp.concatenate([rim_top[...].astype(F32), rim_low[...].astype(F32)], axis=0).astype(BF16)
    lows = []
    for k in range(K):
        got = jnp.dot(rim, band_back[k, BLK : BLK + HALF, :], preferred_element_type=F32)
        both = got[:O] + edge_back[k]
        spread[k * MAIN : (k + 1) * MAIN, cells : cells + BLK] = both[:MAIN].astype(BF16)
        lows.append(both[MAIN:])
    store_lows(lows, slice(cells, cells + BLK))

    def one_part(j, carry):
        got = lax.dot_general(
            wide[:, HALF : HALF + cells],
            spread[pl.ds(pl.multiple_of(j * PART, PART), PART), HALF : HALF + cells],
            (((1,), (1,)), ((), ())),
            preferred_element_type=F32,
        )
        wpart[j] = got.T.astype(BF16)
        for off in range(1, n):
            scatter(j, off).start()

        @pl.when(j >= 1)
        def _():
            after_scatter(j - 1)

        @pl.when(j >= 2)
        def _():
            after_across(j - 2)

        return carry

    lax.fori_loop(0, PARTS, one_part, 0)

    def late(t, carry):
        one_grad(t, 0)

        @pl.when(t == 5)
        def _():
            after_scatter(2)
            after_across(1)

        @pl.when(t == 7)
        def _():
            after_across(2)

        return carry

    lax.fori_loop(4, steps, late, 0)
    for j in range(PARTS):
        for off in range(1, n):
            gather(j, off).wait_recv()
        wout[j * PART : (j + 1) * PART, :] = wfull[j]

    def drain(q, carry):
        for off in range(1, n):
            first(q, off).wait_send()
            second(q, off).wait_send()
        return carry

    lax.fori_loop(0, steps, drain, 0)
    for j in range(PARTS):
        for off in range(1, n):
            scatter(j, off).wait_send()
            gather(j, off).wait_send()
        for off in range(1, nl):
            across(j, off).wait_send()
    out_copy(steps - 2).wait()
    out_copy(steps - 1).wait()


def fused(n, nl, feat, weight, table, table_back, obs, lat, share):
    chan, cells = feat.shape
    steps = cells // WIDE
    vmem = pl.BlockSpec(memory_space=pltpu.VMEM)
    anywhere = pl.BlockSpec(memory_space=pl.ANY)
    dma = pltpu.SemaphoreType.DMA
    prow = PART // n
    return pl.pallas_call(
        functools.partial(fused_kernel, n, nl, share, steps),
        out_shape=(
            jax.ShapeDtypeStruct((chan, cells), BF16),
            jax.ShapeDtypeStruct((PARTS * PART, chan), BF16),
        ),
        in_specs=[anywhere, vmem, vmem, vmem, anywhere, vmem],
        out_specs=(anywhere, vmem),
        scratch_shapes=[
            pltpu.VMEM((chan, cells + BLK), BF16),
            pltpu.VMEM((K * O, chan), BF16),
            pltpu.VMEM((K, 2 * BLK, BLK), BF16),
            pltpu.VMEM((K, 2 * BLK, BLK), BF16),
            pltpu.VMEM((chan, PARTS * PART), BF16),
            pltpu.VMEM((8, BLK), F32),
            pltpu.VMEM((K, ROWS_P, BLK), BF16),
            pltpu.VMEM((2, ROWS_P, BLK), F32),
            pltpu.VMEM((O, BLK), F32),
            pltpu.VMEM((O, BLK), F32),
            pltpu.VMEM((O, BLK), F32),
            pltpu.VMEM((K, O, BLK), F32),
            pltpu.VMEM((2, O, HALF), F32),
            pltpu.VMEM((2, O, HALF), F32),
            pltpu.VMEM((steps, n * share, BLK), BF16),
            pltpu.VMEM((steps, n, share, BLK), BF16),
            pltpu.VMEM((steps, n, share, BLK), BF16),
            pltpu.VMEM((steps, n * share, BLK), BF16),
            pltpu.VMEM((steps, share, BLK), F32),
            pltpu.VMEM((MAIN + 16, HALF), BF16),
            pltpu.VMEM((MAIN, HALF), BF16),
            pltpu.VMEM((16, HALF), BF16),
            pltpu.VMEM((PARTS * PART, cells + BLK), BF16),
            pltpu.VMEM((2, chan, WIDE), BF16),
            pltpu.VMEM((PARTS, PART, chan), BF16),
            pltpu.VMEM((PARTS, n, prow, chan), BF16),
            pltpu.VMEM((PARTS, nl, prow, chan), BF16),
            pltpu.VMEM((PARTS, PART, chan), BF16),
            dma((steps + 1,)),
            dma((steps, share // 8)),
            dma((5,)),
            dma((5,)),
            dma((steps, n)),
            dma((steps, n)),
            dma((steps, n)),
            dma((steps, n)),
            dma((steps,)),
            dma((PARTS, n)),
            dma((PARTS, n)),
            dma((PARTS, nl)),
            dma((PARTS, nl)),
            dma((PARTS, n)),
            dma((PARTS, n)),
        ],
        compiler_params=pltpu.CompilerParams(
            collective_id=2, has_side_effects=True, vmem_limit_bytes=VMEM_LIMIT
        ),
        name="fused_decoder",
    )(feat, weight, table, table_back, obs, lat)


def fused_shards(features, proj_weight, basis_vals, row_of, col_off, observed, lat_weight):
    ne = lax.axis_size("ens")
    nl = lax.axis_size("lon")
    feat = features[0]
    chan, cells = feat.shape
    share = pl.cdiv(pl.cdiv(ROWS, ne), 16) * 16
    ahead, back = side_tables(kernel_rows(basis_vals, row_of, col_off))
    grad, part = fused(
        ne, nl, feat, proj_weight, ahead, back, observed, lat_weight.reshape(1, LAT), share
    )
    scale = 1.0 / math.sqrt(ne * (cells // LAT) * nl * LAT)
    tops = part[:TOPS].reshape(K, MAIN, chan)
    lows = part[TOPS : K * O].reshape(K, LEFT, chan)
    part = jnp.concatenate([tops, lows], axis=1).reshape(K * O, chan)
    return (grad[None], part.astype(F32) * scale)


def shards(*args):
    cells = args[0].shape[2]
    sizes = (lax.axis_size("ens"), lax.axis_size("lon"))
    if cells % WIDE == 0 and cells // WIDE >= 8 and PART % (16 * sizes[0]) == 0 and sizes[1] > 1:
        return fused_shards(*args)
    return split_shards(*args)


def solution(mesh):
    in_specs = (P("ens", None, "lon"), P(), P(), P(), P(), P(None, "lon"), P())
    out_specs = (P("ens", None, "lon"), P())
    return jax.shard_map(shards, mesh=mesh, in_specs=in_specs, out_specs=out_specs, check_vma=False)
```

```python
import functools
import math

import jax
import jax.numpy as jnp
from jax import lax
from jax.experimental import pallas as pl
from jax.experimental.pallas import tpu as pltpu
from jax.sharding import PartitionSpec as P

O = 72
OP = 80
K = 9
R = 4
LAT = 32
SMOOTH = 0.25
BLK = 256
HALF = 128
F32 = jnp.float32
BF16 = jnp.bfloat16
MESH = pl.DeviceIdType.MESH
VMEM_LIMIT = 60 * 1024 * 1024


def whole(shape):
    return pl.BlockSpec(shape, lambda s: (0,) * len(shape))


def kernel_rows(basis_vals, row_of, col_off):
    code = (col_off + R) * LAT + row_of
    ids = jnp.arange((2 * R + 1) * LAT, dtype=jnp.int32)
    hit = (code[:, :, None] == ids[None, None, :]).astype(F32)
    table = jnp.einsum("isk,isq->ikq", basis_vals, hit, precision=lax.Precision.HIGHEST)
    return table.astype(BF16)


def side_tables(table):
    taps = 2 * R + 1
    four = table.reshape(LAT, K, taps, LAT)
    ahead = four.transpose(1, 2, 3, 0).reshape(K, taps * LAT, LAT)
    back = four[:, :, ::-1].transpose(1, 2, 0, 3).reshape(K, taps * LAT, LAT)
    return ahead, back


def build_band(table, band):
    lane = lax.broadcasted_iota(jnp.int32, (LAT, BLK), 1)
    spread_lanes = (lane % LAT == lax.broadcasted_iota(jnp.int32, (LAT, BLK), 0)).astype(F32)
    spread_lanes = spread_lanes.astype(BF16)
    place = lane // LAT
    cols = BLK // LAT

    def one(k, carry):
        tiled = jnp.dot(table[k], spread_lanes, preferred_element_type=F32)
        for e in range(2 * cols):
            block = jnp.zeros((LAT, BLK), F32)
            for j in range(cols):
                d = e - j
                if 0 <= d <= 2 * R:
                    block = jnp.where(place == j, tiled[d * LAT : (d + 1) * LAT], block)
            band[k, e * LAT : (e + 1) * LAT, :] = block.astype(BF16)
        return carry

    lax.fori_loop(0, K, one, 0)


def padded_weight(weight):
    wide = weight[...].astype(F32)
    gap = jnp.zeros((OP - O, wide.shape[1]), F32)
    rows = []
    for k in range(K):
        rows += [wide[k * O : (k + 1) * O], gap]
    return jnp.concatenate(rows, axis=0)


def greet(peers):
    barrier = pltpu.get_barrier_semaphore()
    for peer in peers:
        pl.semaphore_signal(barrier, inc=1, device_id=peer, device_id_type=MESH)
    pl.semaphore_wait(barrier, len(peers))


def forward_kernel(
    n, nl, group, steps, share,
    feat, tail, head, weight, table, obs, lat, out, rims,
    wpad, band, proj, dec, flat, recv, send, cot, left, right, rim_left, rim_right,
    ssem1, rsem1, ssem2, rsem2, hsend, hrecv,
):
    s = pl.program_id(0)
    me = lax.axis_index("ens")
    real = group * 2 * O
    own = pl.multiple_of(me * share, 16)
    after = {"lon": lax.rem(lax.axis_index("lon") + 1, nl)}
    before = {"lon": lax.rem(lax.axis_index("lon") + nl - 1, nl)}

    def rim(src, dst, slot, peer):
        return pltpu.make_async_remote_copy(
            src_ref=src,
            dst_ref=dst,
            send_sem=hsend.at[slot],
            recv_sem=hrecv.at[slot],
            device_id=peer,
            device_id_type=MESH,
        )

    def first(q, off):
        peer = lax.rem(me + off, n)
        return pltpu.make_async_remote_copy(
            src_ref=dec.at[q, pl.ds(pl.multiple_of(peer * share, 16), share)],
            dst_ref=recv.at[q, off],
            send_sem=ssem1.at[q, off],
            recv_sem=rsem1.at[q, off],
            device_id={"ens": peer},
            device_id_type=MESH,
        )

    def second(q, off):
        return pltpu.make_async_remote_copy(
            src_ref=send.at[q, off],
            dst_ref=cot.at[q, pl.ds(own, share)],
            send_sem=ssem2.at[q, off],
            recv_sem=rsem2.at[q, off],
            device_id={"ens": lax.rem(me - off + n, n)},
            device_id_type=MESH,
        )

    def put(values, h, lo):
        for k in range(K):
            proj[k, h, :, lo : lo + HALF] = values[k * OP : (k + 1) * OP].astype(BF16)

    @pl.when(s == 0)
    def _():
        greet([{"ens": lax.rem(me + off, n)} for off in range(1, n)] + [after, before])
        rim(tail, left, 0, after).start()
        rim(head, right, 1, before).start()
        wpad[...] = padded_weight(weight).astype(BF16)
        build_band(table, band)
        if n * share > real:
            for q in range(steps):
                dec[q, real:, :] = jnp.zeros((n * share - real, HALF), BF16)
            flat[real:, :] = jnp.zeros((n * share - real, HALF), F32)

    @pl.when(s < steps)
    def _():
        def one(b, carry):
            lanes = pl.ds(pl.multiple_of(b * BLK, BLK), BLK)
            got = jnp.dot(wpad[...], feat[:, lanes], preferred_element_type=F32)
            h = s * group + b
            put(got[:, :HALF], h, HALF)
            put(got[:, HALF:], h + 1, 0)
            return carry

        lax.fori_loop(0, group, one, 0)

    @pl.when(s == 1)
    def _():
        rim(tail, left, 0, after).wait()
        put(jnp.dot(wpad[...], left[...], preferred_element_type=F32), 0, 0)

    @pl.when(s == steps)
    def _():
        rim(head, right, 1, before).wait()
        put(jnp.dot(wpad[...], right[...], preferred_element_type=F32), steps * group, HALF)

    @pl.when(jnp.logical_and(s > 0, s <= steps))
    def _():
        q = s - 1
        g0 = q * group
        acc = jnp.zeros((group * OP, BLK), F32)
        for k in range(K):
            for part in range(2):
                lhs = proj[k, pl.ds(g0 + part, group)].reshape(group * OP, BLK)
                acc = acc + jnp.dot(
                    lhs, band[k, part * BLK : (part + 1) * BLK, :], preferred_element_type=F32
                )
        for g in range(group):
            piece = acc[g * OP : g * OP + O]
            both = jnp.concatenate([piece[:, :HALF], piece[:, HALF:]], axis=0)
            dec[q, g * 2 * O : (g + 1) * 2 * O, :] = both.astype(BF16)
        for off in range(1, n):
            first(q, off).start()

    @pl.when(s > 1)
    def _():
        q = s - 2
        for t in range(2 * group):
            flat[t * O : (t + 1) * O, :] = obs[:, t * HALF : (t + 1) * HALF]
        for off in range(1, n):
            first(q, off).wait_recv()
        lat_row = jnp.broadcast_to(lat[0:1, :], (16, HALF))

        def smooth(diff):
            return diff * lax.rsqrt(diff * diff + SMOOTH * SMOOTH)

        def one(step, carry):
            at = pl.multiple_of(step * 16, 16)
            here = pl.ds(pl.multiple_of(own + at, 16), 16)
            values = [dec[q, here, :].astype(F32)]
            values += [recv[q, off, pl.ds(at, 16), :].astype(F32) for off in range(1, n)]
            sums = [None] * n
            for a in range(n):
                for b in range(a + 1, n):
                    pair = smooth(values[a] - values[b])
                    sums[a] = pair if sums[a] is None else sums[a] + pair
                    sums[b] = -pair if sums[b] is None else sums[b] - pair
            target = flat[here, :]
            for a in range(n):
                slope = smooth(values[a] - target) - sums[a] * (1.0 / (n - 1))
                result = (slope * lat_row).astype(BF16)
                if a == 0:
                    cot[q, here, :] = result
                else:
                    send[q, a, pl.ds(at, 16), :] = result
            return carry

        lax.fori_loop(0, share // 16, one, 0)
        for off in range(1, n):
            second(q, off).start()

    @pl.when(s == steps + 1)
    def _():
        for q in range(steps):
            for off in range(1, n):
                first(q, off).wait_send()
                second(q, off).wait()
        last = rim(cot.at[steps - 1, pl.ds(real - OP, OP)], rim_left, 2, after)
        opening = rim(cot.at[0, pl.ds(0, OP)], rim_right, 3, before)
        last.start()
        opening.start()
        for q in range(steps):
            out[q * n * share : (q + 1) * n * share, :] = cot[q]
        last.wait()
        opening.wait()
        rims[0] = rim_left[...]
        rims[1] = rim_right[...]


def forward(n, nl, feat, tail, head, weight, table, obs, lat, group, steps, share):
    chan = feat.shape[0]
    wide = group * BLK
    rows = n * share
    sem = pltpu.SemaphoreType.DMA((steps, n))
    return pl.pallas_call(
        functools.partial(forward_kernel, n, nl, group, steps, share),
        out_shape=(
            jax.ShapeDtypeStruct((steps * rows, HALF), BF16),
            jax.ShapeDtypeStruct((2, OP, HALF), BF16),
        ),
        grid=(steps + 2,),
        in_specs=[
            pl.BlockSpec((chan, wide), lambda s: (0, jnp.minimum(s, steps - 1))),
            whole(tail.shape),
            whole(head.shape),
            whole(weight.shape),
            whole(table.shape),
            pl.BlockSpec((O, wide), lambda s: (0, jnp.clip(s - 2, 0, steps - 1))),
            whole(lat.shape),
        ],
        out_specs=(whole((steps * rows, HALF)), whole((2, OP, HALF))),
        scratch_shapes=[
            pltpu.VMEM((K * OP, chan), BF16),
            pltpu.VMEM((K, 2 * BLK, BLK), BF16),
            pltpu.VMEM((K, steps * group + 1, OP, BLK), BF16),
            pltpu.VMEM((steps, rows, HALF), BF16),
            pltpu.VMEM((rows, HALF), F32),
            pltpu.VMEM((steps, n, share, HALF), BF16),
            pltpu.VMEM((steps, n, share, HALF), BF16),
            pltpu.VMEM((steps, rows, HALF), BF16),
            pltpu.VMEM((chan, HALF), BF16),
            pltpu.VMEM((chan, HALF), BF16),
            pltpu.VMEM((OP, HALF), BF16),
            pltpu.VMEM((OP, HALF), BF16),
            sem,
            sem,
            sem,
            sem,
            pltpu.SemaphoreType.DMA((4,)),
            pltpu.SemaphoreType.DMA((4,)),
        ],
        compiler_params=pltpu.CompilerParams(
            collective_id=0, has_side_effects=True, vmem_limit_bytes=VMEM_LIMIT
        ),
        name="forward_slopes",
    )(feat, tail, head, weight, table, obs, lat)


WG_ROWS = 2048
WG_PART = 656


def backward_kernel(
    group, steps, piece, share, cells, padded,
    cot, left, right, weight, table, feat, grad, wgrad,
    weight_t, band, ext, spread, acc,
):
    s = pl.program_id(0)
    blocks = steps * group

    @pl.when(s == 0)
    def _():
        ext[:, O:, :] = jnp.zeros((blocks + 1, OP - O, BLK), BF16)
        ext[0, :O, :HALF] = left[...].astype(F32)[OP - O :].astype(BF16)
        ext[blocks, :O, HALF:] = right[:O]

        weight_t[...] = padded_weight(weight).T.astype(BF16)
        build_band(table, band)

        def one(b, carry):
            start = lax.div(b, piece) * share + lax.rem(b, piece) * (2 * O)
            pair = cot[pl.ds(pl.multiple_of(start, 16), 2 * O), :].astype(F32)
            ext[b, :O, HALF:] = pair[:O].astype(BF16)
            ext[b + 1, :O, :HALF] = pair[O:].astype(BF16)
            return carry

        lax.fori_loop(0, blocks, one, 0)
        acc[...] = jnp.zeros_like(acc)

    g0 = s * group
    for k in range(K):
        got = jnp.zeros((group * OP, BLK), F32)
        for part in range(2):
            lhs = ext[pl.ds(g0 + part, group)].reshape(group * OP, BLK)
            got = got + jnp.dot(
                lhs, band[k, part * BLK : (part + 1) * BLK, :], preferred_element_type=F32
            )
        if padded:
            row = lax.broadcasted_iota(jnp.int32, got.shape, 0) // OP
            lane = lax.broadcasted_iota(jnp.int32, got.shape, 1)
            got = jnp.where((g0 + row) * BLK + lane < cells, got, 0.0)
        got = got.astype(BF16)
        for g in range(group):
            spread[k * OP : (k + 1) * OP, g * BLK : (g + 1) * BLK] = got[g * OP : (g + 1) * OP]

    acc[...] += lax.dot_general(
        spread[...], feat[...], (((1,), (1,)), ((), ())), preferred_element_type=F32
    )

    def one_grad(n, carry):
        lanes = pl.ds(pl.multiple_of(n * BLK, BLK), BLK)
        grad[:, lanes] = jnp.dot(
            weight_t[...], spread[:, lanes], preferred_element_type=F32
        ).astype(BF16)
        return carry

    lax.fori_loop(0, group, one_grad, 0)

    @pl.when(s == steps - 1)
    def _():
        parts = acc.shape[1] // HALF
        wgrad[parts * WG_PART - 16 :, :] = jnp.zeros((WG_ROWS - parts * WG_PART + 16, HALF), BF16)
        for t in range(parts):
            rows = [
                acc[k * OP : k * OP + O, t * HALF : (t + 1) * HALF] for k in range(K)
            ] + [jnp.zeros((8, HALF), F32)]
            wgrad[t * WG_PART : (t + 1) * WG_PART, :] = jnp.concatenate(rows, axis=0).astype(BF16)


def backward(cot, left, right, weight, table, feat, group, steps, piece, cells):
    chan = feat.shape[0]
    wide = group * BLK
    blocks = steps * group
    return pl.pallas_call(
        functools.partial(
            backward_kernel,
            group,
            steps,
            piece,
            cot.shape[0] * piece // blocks,
            cells,
            cells != blocks * BLK,
        ),
        out_shape=(
            jax.ShapeDtypeStruct(feat.shape, BF16),
            jax.ShapeDtypeStruct((WG_ROWS, HALF), BF16),
        ),
        grid=(steps,),
        in_specs=[
            whole(cot.shape),
            whole(left.shape),
            whole(right.shape),
            whole(weight.shape),
            whole(table.shape),
            pl.BlockSpec((chan, wide), lambda s: (0, s)),
        ],
        out_specs=(pl.BlockSpec((chan, wide), lambda s: (0, s)), whole((WG_ROWS, HALF))),
        scratch_shapes=[
            pltpu.VMEM((chan, K * OP), BF16),
            pltpu.VMEM((K, 2 * BLK, BLK), BF16),
            pltpu.VMEM((blocks + 1, OP, BLK), BF16),
            pltpu.VMEM((K * OP, wide), BF16),
            pltpu.VMEM((K * OP, chan), F32),
        ],
        compiler_params=pltpu.CompilerParams(vmem_limit_bytes=VMEM_LIMIT),
        name="backward_conv",
    )(cot, left, right, weight, table, feat)


def reduce_kernel(ne, nl, scale, part, out, recv1, mid, recv2, got, *sems):
    (ss1, rs1, ss2, rs2, ss3, rs3, ss4, rs4) = sems
    me = lax.axis_index("ens")
    at = lax.axis_index("lon")
    rows = WG_ROWS // ne
    small = rows // nl
    ens_peers = [{"ens": lax.rem(me + off, ne)} for off in range(1, ne)]
    lon_peers = [{"lon": lax.rem(at + off, nl)} for off in range(1, nl)]
    greet(ens_peers + lon_peers)

    def run(copies):
        for copy in copies:
            copy.start()
        for copy in copies:
            copy.wait()

    def send(src, dst, ssem, rsem, peer):
        return pltpu.make_async_remote_copy(
            src_ref=src, dst_ref=dst, send_sem=ssem, recv_sem=rsem, device_id=peer, device_id_type=MESH
        )

    own = pl.multiple_of(me * rows, 16)
    mine = pl.multiple_of(at * small, 8)
    run(
        [
            send(
                part.at[pl.ds(pl.multiple_of(lax.rem(me + off, ne) * rows, 16), rows)],
                recv1.at[off],
                ss1.at[off],
                rs1.at[off],
                {"ens": lax.rem(me + off, ne)},
            )
            for off in range(1, ne)
        ]
    )
    total = part[pl.ds(own, rows), :].astype(F32)
    for off in range(1, ne):
        total = total + recv1[off].astype(F32)
    mid[...] = total
    run(
        [
            send(
                mid.at[pl.ds(pl.multiple_of(lax.rem(at + off, nl) * small, 8), small)],
                recv2.at[off],
                ss2.at[off],
                rs2.at[off],
                {"lon": lax.rem(at + off, nl)},
            )
            for off in range(1, nl)
        ]
    )
    total = mid[pl.ds(mine, small), :]
    for off in range(1, nl):
        total = total + recv2[off]
    recv2[0] = total
    gat = got[1]
    gat[pl.ds(mine, small), :] = total
    run(
        [
            send(
                recv2.at[0],
                gat.at[pl.ds(mine, small)],
                ss3.at[off],
                rs3.at[off],
                {"lon": lax.rem(at + off, nl)},
            )
            for off in range(1, nl)
        ]
    )
    full = got[0]
    full[pl.ds(own, rows), :] = gat[...].astype(BF16)
    run(
        [
            send(
                full.at[pl.ds(own, rows)],
                full.at[pl.ds(own, rows)],
                ss4.at[off],
                rs4.at[off],
                {"ens": lax.rem(me + off, ne)},
            )
            for off in range(1, ne)
        ]
    )
    for t in range(out.shape[1] // HALF):
        piece = full[t * WG_PART : (t + 1) * WG_PART, :].astype(F32) * scale
        out[:, t * HALF : (t + 1) * HALF] = piece[: K * O]


def reduced(ne, nl, scale, part, chan):
    vmem = pl.BlockSpec(memory_space=pltpu.VMEM)
    rows = WG_ROWS // ne
    small = rows // nl

    def body(part, out, recv1, mid, recv2, full, gat, *sems):
        reduce_kernel(ne, nl, scale, part, out, recv1, mid, recv2, (full, gat), *sems)

    return pl.pallas_call(
        body,
        out_shape=jax.ShapeDtypeStruct((K * O, chan), F32),
        in_specs=[vmem],
        out_specs=vmem,
        scratch_shapes=[
            pltpu.VMEM((ne, rows, HALF), BF16),
            pltpu.VMEM((rows, HALF), F32),
            pltpu.VMEM((nl, small, HALF), F32),
            pltpu.VMEM((WG_ROWS, HALF), BF16),
            pltpu.VMEM((rows, HALF), F32),
        ]
        + [pltpu.SemaphoreType.DMA((n,)) for n in (ne, ne, nl, nl, nl, nl, ne, ne)],
        compiler_params=pltpu.CompilerParams(
            collective_id=1, has_side_effects=True, vmem_limit_bytes=VMEM_LIMIT
        ),
        name="weight_reduce",
    )(part)


def passed_along(value, axis, steps):
    count = lax.axis_size(axis)
    return lax.ppermute(value, axis, [(i, (i + steps) % count) for i in range(count)])


def split_shards(features, proj_weight, basis_vals, row_of, col_off, observed, lat_weight):
    ne = lax.axis_size("ens")
    nl = lax.axis_size("lon")
    assert features.shape[0] == 1
    feat = features[0]
    chan, cells = feat.shape
    aligned = cells % BLK == 0
    blocks = cells // BLK if aligned else pl.cdiv(cells + HALF, BLK)
    group_back = max(g for g in range(1, 10) if blocks % g == 0)
    steps_back = blocks // group_back
    group = max(g for g in range(1, 7) if blocks % g == 0)
    steps = blocks // group
    real = group * 2 * O
    share = pl.cdiv(pl.cdiv(real, ne), 16) * 16
    rows = ne * share
    extra = blocks * BLK - cells

    tail = feat[:, cells - HALF :]
    head = feat[:, :HALF]
    ahead, back = side_tables(kernel_rows(basis_vals, row_of, col_off))
    if not aligned:
        right = passed_along(head, "lon", -1)
        feat = jnp.pad(jnp.concatenate([feat, right], axis=1), ((0, 0), (0, extra - HALF)))
        observed = jnp.pad(observed, ((0, 0), (0, extra)))
    lat = jnp.broadcast_to(jnp.tile(lat_weight, HALF // LAT)[None, :], (8, HALF))
    cot, rims = forward(
        ne, nl, feat, tail, head, proj_weight, ahead, observed, lat, group, steps, share
    )

    if aligned:
        cot_left, cot_right = rims[0], rims[1]
    else:
        flat = cot.reshape(steps, rows, HALF)[:, :real].reshape(2 * blocks, O, HALF)
        flat = flat.transpose(1, 0, 2).reshape(O, blocks * BLK)[:, :cells]
        cot_left = passed_along(flat[:, cells - HALF :], "lon", 1)
        cot_right = passed_along(flat[:, :HALF], "lon", -1)
        flat = jnp.pad(
            jnp.concatenate([flat, cot_right], axis=1), ((0, 0), (0, extra - HALF))
        )
        flat = flat.reshape(O, 2 * blocks, HALF).transpose(1, 0, 2).reshape(steps, real, HALF)
        cot = jnp.pad(flat, ((0, 0), (0, rows - real), (0, 0))).reshape(steps * rows, HALF)
        cot_left = jnp.pad(cot_left, ((OP - O, 0), (0, 0)))
        cot_right = jnp.zeros((OP, HALF), BF16)
    grad, part = backward(
        cot, cot_left, cot_right, proj_weight, back, feat, group_back, steps_back, group, cells
    )
    scale = 1.0 / math.sqrt(ne * (cells // LAT) * nl * LAT)
    weight_grad = reduced(ne, nl, scale, part, chan)
    return (grad[:, :cells][None], weight_grad)


GROUP = 5
WIDE = GROUP * BLK
ROWS = GROUP * O
ROWS_P = ROWS + 8
MAIN = 64
LEFT = O - MAIN
SPLIT = GROUP * MAIN
TOPS = K * MAIN
USED = K * O + 8
EARLY = 4
PART = 256
PARTS = 3


def ordered_weight(weight):
    rows = weight[...].astype(F32)
    parts = [rows[k * O : k * O + MAIN] for k in range(K)]
    parts += [rows[k * O + MAIN : (k + 1) * O] for k in range(K)]
    return jnp.concatenate(parts, axis=0)


def fused_kernel(
    n, nl, share, steps,
    feat, weight, table, table_back, obs, lat, grad, wout,
    wide, wrows, band, band_back, weight_t, lat_row, proj, sums, edge, first_edge, extra, edge_back,
    give, take, dec, recv, send, cot, seen, rim_left, rim_top, rim_low, spread, gout,
    wpart, wrecv, wmid, wfull,
    fsem, osem, hsend, hrecv, ssem1, rsem1, ssem2, rsem2, gsem,
    ws1, wr1, ws2, wr2, ws3, wr3,
):
    me = lax.axis_index("ens")
    at = lax.axis_index("lon")
    cells = steps * WIDE
    chan = feat.shape[0]
    own = pl.multiple_of(me * share, 16)
    after = {"lon": lax.rem(at + 1, nl)}
    before = {"lon": lax.rem(at + nl - 1, nl)}
    prow = PART // n

    def remote(src, dst, ssem, rsem, peer):
        return pltpu.make_async_remote_copy(
            src_ref=src, dst_ref=dst, send_sem=ssem, recv_sem=rsem, device_id=peer, device_id_type=MESH
        )

    def piece(c):
        if isinstance(c, int) and c == steps:
            return pltpu.make_async_copy(
                feat.at[:, pl.ds(0, HALF)], wide.at[:, pl.ds(HALF, HALF)], fsem.at[steps]
            )
        if isinstance(c, int) and c == steps - 1:
            lo, size = c * WIDE, WIDE - HALF
        else:
            lo, size = c * WIDE, WIDE
        return pltpu.make_async_copy(
            feat.at[:, pl.ds(pl.multiple_of(lo + HALF, HALF), size)],
            wide.at[:, pl.ds(pl.multiple_of(lo + 2 * HALF, HALF), size)],
            fsem.at[c],
        )

    def seen_copy(q, u):
        c = lax.rem(q + steps - 1, steps)
        t = jnp.minimum(me * (share // 8) + u, ROWS // 8 - 1)
        low = t // (SPLIT // 8)
        row = pl.multiple_of((1 - low) * (t % (MAIN // 8)) * 8 + low * MAIN, 8)
        block = (1 - low) * (t // (MAIN // 8)) + low * (ROWS // 8 - 1 - t)
        lane = pl.multiple_of(c * WIDE + block * BLK, BLK)
        return pltpu.make_async_copy(
            obs.at[pl.ds(row, 8), pl.ds(lane, BLK)], seen.at[q, pl.ds(u * 8, 8)], osem.at[q, u]
        )

    def first(q, off):
        peer = lax.rem(me + off, n)
        return remote(
            dec.at[q, pl.ds(pl.multiple_of(peer * share, 16), share)],
            recv.at[q, off], ssem1.at[q, off], rsem1.at[q, off], {"ens": peer},
        )

    def second(q, off):
        return remote(
            send.at[q, off], cot.at[q, pl.ds(own, share)],
            ssem2.at[q, off], rsem2.at[q, off], {"ens": lax.rem(me - off + n, n)},
        )

    def halo(slot):
        if slot == 0:
            src, dst, peer = give.at[0], take.at[0], after
        elif slot == 1:
            src, dst, peer = give.at[1], take.at[1], before
        elif slot == 2:
            src = cot.at[0, pl.ds(SPLIT - MAIN, MAIN + 16), pl.ds(HALF, HALF)]
            dst, peer = rim_left, after
        elif slot == 3:
            src, dst, peer = cot.at[1, pl.ds(0, MAIN), pl.ds(0, HALF)], rim_top, before
        else:
            src = cot.at[1, pl.ds(ROWS - LEFT, 16), pl.ds(0, HALF)]
            dst, peer = rim_low, before
        return remote(src, dst, hsend.at[slot], hrecv.at[slot], peer)

    def out_copy(t):
        return pltpu.make_async_copy(
            gout.at[lax.rem(t, 2)], grad.at[:, pl.ds(pl.multiple_of(t * WIDE, WIDE), WIDE)], gsem.at[t]
        )

    def scatter(j, off):
        peer = lax.rem(me + off, n)
        return remote(
            wpart.at[j, pl.ds(pl.multiple_of(peer * prow, 16), prow)], wrecv.at[j, off],
            ws1.at[j, off], wr1.at[j, off], {"ens": peer},
        )

    def across(j, off):
        return remote(
            wmid.at[j, at], wmid.at[j, at], ws2.at[j, off], wr2.at[j, off], {"lon": lax.rem(at + off, nl)}
        )

    def gather(j, off):
        mine = pl.ds(pl.multiple_of(me * prow, 16), prow)
        return remote(
            wfull.at[j, mine], wfull.at[j, mine], ws3.at[j, off], wr3.at[j, off],
            {"ens": lax.rem(me + off, n)},
        )

    def project_edges():
        start = (steps - 1) * WIDE
        lanes = jnp.concatenate(
            [wide[:, HALF:BLK], wide[:, cells : cells + HALF], wide[:, start : start + BLK]], axis=1
        )
        got = jnp.dot(wrows[...], lanes, preferred_element_type=F32)
        acc = jnp.zeros((3 * O, BLK), F32)
        out = jnp.zeros((O, BLK), F32)
        none = jnp.zeros((O, HALF), F32)
        for k in range(K):
            part = jnp.concatenate(
                [got[k * MAIN : (k + 1) * MAIN], got[TOPS + k * LEFT : TOPS + (k + 1) * LEFT]], axis=0
            )
            head = jnp.concatenate([none, part[:, :HALF]], axis=1)
            tail = jnp.concatenate([part[:, HALF:BLK], none], axis=1)
            lhs = jnp.concatenate([head, tail, part[:, BLK:]], axis=0).astype(BF16)
            acc = acc + jnp.dot(lhs, band[k, :BLK, :], preferred_element_type=F32)
            out = out + jnp.dot(head.astype(BF16), band[k, BLK:, :], preferred_element_type=F32)
        first_edge[...] = acc[:O]
        edge[...] = acc[2 * O :]
        give[0] = acc[O : 2 * O, :HALF]
        give[1] = out[:, HALF:]
        halo(0).start()
        halo(1).start()

    def forward_chunk(q):
        c = lax.rem(q + steps - 1, steps)
        got = jnp.dot(
            wrows[...],
            wide[:, pl.ds(pl.multiple_of(c * WIDE + BLK, BLK), WIDE)],
            preferred_element_type=F32,
        )
        gap = jnp.zeros((ROWS_P - ROWS, BLK), F32)
        tops = got[:TOPS].astype(BF16)
        for k in range(K):
            for g in range(GROUP):
                proj[k, g * MAIN : (g + 1) * MAIN, :] = tops[
                    k * MAIN : (k + 1) * MAIN, g * BLK : (g + 1) * BLK
                ]
            lows = [
                got[TOPS + k * LEFT : TOPS + (k + 1) * LEFT, g * BLK : (g + 1) * BLK]
                for g in reversed(range(GROUP))
            ]
            proj[k, SPLIT:, :] = jnp.concatenate(lows + [gap], axis=0).astype(BF16)
        def one_half(half, carry):
            acc = jnp.zeros((ROWS_P, BLK), F32)
            rows = pl.ds(pl.multiple_of(half * BLK, BLK), BLK)
            for k in range(K):
                acc = acc + jnp.dot(proj[k], band[k, rows, :], preferred_element_type=F32)
            sums[half] = acc
            return carry

        lax.fori_loop(0, 2, one_half, 0)

        @pl.when(q == 0)
        def _():
            halo(1).wait()
            extra[:, HALF:] = take[1]

        @pl.when(q == 1)
        def _():
            halo(0).wait()
            extra[...] = jnp.zeros_like(extra)
            edge[...] = first_edge[...]
            edge[:, :HALF] += take[0]

        last = SPLIT - MAIN
        dec[q, :last, :] = (
            jnp.concatenate([edge[:MAIN], sums[0, : last - MAIN]], axis=0) + sums[1, :last]
        ).astype(BF16)
        dec[q, last:SPLIT, :] = (
            sums[0, last - MAIN : last] + sums[1, last:SPLIT] + extra[:MAIN]
        ).astype(BF16)
        lows = jnp.concatenate([sums[0, SPLIT + LEFT : ROWS], edge[MAIN:]], axis=0) + sums[1, SPLIT:ROWS]
        lows = [lows[:LEFT] + extra[MAIN:], lows[LEFT:]]
        rest = jnp.zeros((n * share - ROWS, BLK), F32)
        dec[q, SPLIT:, :] = jnp.concatenate(lows + [rest], axis=0).astype(BF16)
        edge[...] = sums[0, last : SPLIT + LEFT]
        for off in range(1, n):
            first(q, off).start()

    def smooth(diff):
        return diff * lax.rsqrt(diff * diff + SMOOTH * SMOOTH)

    def slopes(q):
        for u in range(share // 8):
            seen_copy(q, u).wait()
        for off in range(1, n):
            first(q, off).wait_recv()

        def one(step, carry):
            row = pl.multiple_of(lax.div(step, 2) * 16, 16)
            lanes = pl.ds(pl.multiple_of(lax.rem(step, 2) * HALF, HALF), HALF)
            here = pl.ds(pl.multiple_of(own + row, 16), 16)
            values = [dec[q, here, lanes].astype(F32)]
            values += [recv[q, off, pl.ds(row, 16), lanes].astype(F32) for off in range(1, n)]
            sums = [None] * n
            for a in range(n):
                for b in range(a + 1, n):
                    pair = smooth(values[a] - values[b])
                    sums[a] = pair if sums[a] is None else sums[a] + pair
                    sums[b] = -pair if sums[b] is None else sums[b] - pair
            target = seen[q, pl.ds(row, 16), lanes]
            area = jnp.broadcast_to(lat_row[0:1, lanes], (16, HALF))
            for a in range(n):
                slope = smooth(values[a] - target) - sums[a] * (1.0 / (n - 1))
                result = (slope * area).astype(BF16)
                if a == 0:
                    cot[q, here, lanes] = result
                else:
                    send[q, a, pl.ds(row, 16), lanes] = result
            return carry

        lax.fori_loop(0, share // 16 * 2, one, 0)
        for off in range(1, n):
            second(q, off).start()

    def store_lows(lows, lanes):
        both = jnp.concatenate(lows + [jnp.zeros((USED - K * O, BLK), F32)], axis=0)
        spread[TOPS:USED, lanes] = both.astype(BF16)

    def backward_chunk(b):
        q = lax.rem(b + 1, steps)
        lhs = cot[q, pl.ds(0, ROWS_P), :]
        lows = [[] for _ in range(GROUP)]
        for k in range(K):
            ahead = jnp.dot(lhs, band_back[k, :BLK, :], preferred_element_type=F32)
            here = jnp.dot(lhs, band_back[k, BLK:, :], preferred_element_type=F32)
            for g in range(GROUP):
                low = SPLIT + (GROUP - 1 - g) * LEFT
                top = edge_back[k, :MAIN] if g == 0 else ahead[(g - 1) * MAIN : g * MAIN]
                end = edge_back[k, MAIN:] if g == 0 else ahead[low + LEFT : low + 2 * LEFT]
                lanes = pl.ds(pl.multiple_of(b * WIDE + g * BLK, BLK), BLK)
                spread[k * MAIN : (k + 1) * MAIN, lanes] = (
                    here[g * MAIN : (g + 1) * MAIN] + top
                ).astype(BF16)
                lows[g].append(here[low : low + LEFT] + end)
            edge_back[k] = ahead[SPLIT - MAIN : SPLIT + LEFT]
        for g in range(GROUP):
            store_lows(lows[g], pl.ds(pl.multiple_of(b * WIDE + g * BLK, BLK), BLK))

    def one_grad(t, carry):
        @pl.when(t >= 2)
        def _():
            out_copy(t - 2).wait()

        lanes = pl.ds(pl.multiple_of(t * WIDE + HALF, HALF), WIDE)
        gout[lax.rem(t, 2)] = jnp.dot(
            weight_t[:, :USED], spread[:USED, lanes], preferred_element_type=F32
        ).astype(BF16)
        out_copy(t).start()
        return carry

    def after_scatter(j):
        for off in range(1, n):
            scatter(j, off).wait_recv()
        total = wpart[j, pl.ds(pl.multiple_of(me * prow, 16), prow), :].astype(F32)
        for off in range(1, n):
            total = total + wrecv[j, off].astype(F32)
        wmid[j, at] = total.astype(BF16)
        for off in range(1, nl):
            across(j, off).start()

    def after_across(j):
        for off in range(1, nl):
            across(j, off).wait_recv()
        total = wmid[j, 0].astype(F32)
        for z in range(1, nl):
            total = total + wmid[j, z].astype(F32)
        wfull[j, pl.ds(pl.multiple_of(me * prow, 16), prow), :] = total.astype(BF16)
        for off in range(1, n):
            gather(j, off).start()

    for c in [steps - 1, steps, steps - 2]:
        piece(c).start()
    for c in range(steps - 2):
        piece(c).start()

    def look(q, carry):
        for u in range(share // 8):
            seen_copy(q, u).start()
        return carry

    lax.fori_loop(0, steps, look, 0)
    peers = [{"ens": lax.rem(me + off, n)} for off in range(1, n)]
    peers += [{"lon": lax.rem(at + off, nl)} for off in range(1, nl)]
    barrier = pltpu.get_barrier_semaphore()
    for peer in peers:
        pl.semaphore_signal(barrier, inc=1, device_id=peer, device_id_type=MESH)
    build_band(table, band)
    lane = lax.broadcasted_iota(jnp.int32, (LAT, BLK), 1)
    ones = (lane % LAT == lax.broadcasted_iota(jnp.int32, (LAT, BLK), 0)).astype(F32)
    lat_row[...] = jnp.dot(
        jnp.broadcast_to(lat[...], (8, LAT)), ones, precision=lax.Precision.HIGHEST,
        preferred_element_type=F32,
    )
    wrows[...] = ordered_weight(weight).astype(BF16)
    wide[:, :HALF] = jnp.zeros((chan, HALF), BF16)
    wide[:, cells + HALF :] = jnp.zeros((chan, HALF), BF16)
    extra[...] = jnp.zeros_like(extra)
    for c in [steps - 1, steps, steps - 2]:
        piece(c).wait()
    pl.semaphore_wait(barrier, len(peers))
    project_edges()

    def step(s, carry):
        @pl.when(jnp.logical_and(s >= 1, s < steps - 1))
        def _():
            piece(s - 1).wait()

        @pl.when(s < steps)
        def _():
            forward_chunk(s)

        @pl.when(s >= 2)
        def _():
            slopes(s - 2)

        return carry

    lax.fori_loop(0, steps + 2, step, 0)
    build_band(table_back, band_back)
    for off in range(1, n):
        second(0, off).wait_recv()
    halo(2).start()
    gap = jnp.zeros((PARTS * PART - K * O, chan), F32)
    rows = jnp.concatenate([ordered_weight(weight), gap], axis=0)
    weight_t[...] = rows.T.astype(BF16)
    spread[USED:, :] = jnp.zeros((PARTS * PART - USED, spread.shape[1]), BF16)
    for off in range(1, n):
        second(1, off).wait_recv()
    halo(3).start()
    halo(4).start()
    halo(2).wait()
    for k in range(K):
        got = jnp.dot(rim_left[...], band_back[k, HALF:BLK, :], preferred_element_type=F32)
        edge_back[k] = got[:O]

    def step_back(b, carry):
        @pl.when(jnp.logical_and(b >= 1, b < steps - 1))
        def _():
            for off in range(1, n):
                second(b + 1, off).wait_recv()

        backward_chunk(b)

        @pl.when(jnp.logical_and(b >= 1, b <= EARLY))
        def _():
            one_grad(b - 1, 0)

        return carry

    lax.fori_loop(0, steps, step_back, 0)
    halo(3).wait()
    halo(4).wait()
    rim = jnp.concatenate([rim_top[...].astype(F32), rim_low[...].astype(F32)], axis=0).astype(BF16)
    lows = []
    for k in range(K):
        got = jnp.dot(rim, band_back[k, BLK : BLK + HALF, :], preferred_element_type=F32)
        both = got[:O] + edge_back[k]
        spread[k * MAIN : (k + 1) * MAIN, cells : cells + BLK] = both[:MAIN].astype(BF16)
        lows.append(both[MAIN:])
    store_lows(lows, slice(cells, cells + BLK))

    def one_part(j, carry):
        got = lax.dot_general(
            wide[:, HALF : HALF + cells],
            spread[pl.ds(pl.multiple_of(j * PART, PART), PART), HALF : HALF + cells],
            (((1,), (1,)), ((), ())),
            preferred_element_type=F32,
        )
        wpart[j] = got.T.astype(BF16)
        for off in range(1, n):
            scatter(j, off).start()

        @pl.when(j >= 1)
        def _():
            after_scatter(j - 1)

        @pl.when(j >= 2)
        def _():
            after_across(j - 2)

        return carry

    lax.fori_loop(0, PARTS, one_part, 0)

    def late(t, carry):
        one_grad(t, 0)

        @pl.when(t == 5)
        def _():
            after_scatter(2)
            after_across(1)

        @pl.when(t == 7)
        def _():
            after_across(2)

        return carry

    lax.fori_loop(4, steps, late, 0)
    for j in range(PARTS):
        for off in range(1, n):
            gather(j, off).wait_recv()
        wout[j * PART : (j + 1) * PART, :] = wfull[j]

    def drain(q, carry):
        for off in range(1, n):
            first(q, off).wait_send()
            second(q, off).wait_send()
        return carry

    lax.fori_loop(0, steps, drain, 0)
    for j in range(PARTS):
        for off in range(1, n):
            scatter(j, off).wait_send()
            gather(j, off).wait_send()
        for off in range(1, nl):
            across(j, off).wait_send()
    out_copy(steps - 2).wait()
    out_copy(steps - 1).wait()


def fused(n, nl, feat, weight, table, table_back, obs, lat, share):
    chan, cells = feat.shape
    steps = cells // WIDE
    vmem = pl.BlockSpec(memory_space=pltpu.VMEM)
    anywhere = pl.BlockSpec(memory_space=pl.ANY)
    dma = pltpu.SemaphoreType.DMA
    prow = PART // n
    return pl.pallas_call(
        functools.partial(fused_kernel, n, nl, share, steps),
        out_shape=(
            jax.ShapeDtypeStruct((chan, cells), BF16),
            jax.ShapeDtypeStruct((PARTS * PART, chan), BF16),
        ),
        in_specs=[anywhere, vmem, vmem, vmem, anywhere, vmem],
        out_specs=(anywhere, vmem),
        scratch_shapes=[
            pltpu.VMEM((chan, cells + BLK), BF16),
            pltpu.VMEM((K * O, chan), BF16),
            pltpu.VMEM((K, 2 * BLK, BLK), BF16),
            pltpu.VMEM((K, 2 * BLK, BLK), BF16),
            pltpu.VMEM((chan, PARTS * PART), BF16),
            pltpu.VMEM((8, BLK), F32),
            pltpu.VMEM((K, ROWS_P, BLK), BF16),
            pltpu.VMEM((2, ROWS_P, BLK), F32),
            pltpu.VMEM((O, BLK), F32),
            pltpu.VMEM((O, BLK), F32),
            pltpu.VMEM((O, BLK), F32),
            pltpu.VMEM((K, O, BLK), F32),
            pltpu.VMEM((2, O, HALF), F32),
            pltpu.VMEM((2, O, HALF), F32),
            pltpu.VMEM((steps, n * share, BLK), BF16),
            pltpu.VMEM((steps, n, share, BLK), BF16),
            pltpu.VMEM((steps, n, share, BLK), BF16),
            pltpu.VMEM((steps, n * share, BLK), BF16),
            pltpu.VMEM((steps, share, BLK), F32),
            pltpu.VMEM((MAIN + 16, HALF), BF16),
            pltpu.VMEM((MAIN, HALF), BF16),
            pltpu.VMEM((16, HALF), BF16),
            pltpu.VMEM((PARTS * PART, cells + BLK), BF16),
            pltpu.VMEM((2, chan, WIDE), BF16),
            pltpu.VMEM((PARTS, PART, chan), BF16),
            pltpu.VMEM((PARTS, n, prow, chan), BF16),
            pltpu.VMEM((PARTS, nl, prow, chan), BF16),
            pltpu.VMEM((PARTS, PART, chan), BF16),
            dma((steps + 1,)),
            dma((steps, share // 8)),
            dma((5,)),
            dma((5,)),
            dma((steps, n)),
            dma((steps, n)),
            dma((steps, n)),
            dma((steps, n)),
            dma((steps,)),
            dma((PARTS, n)),
            dma((PARTS, n)),
            dma((PARTS, nl)),
            dma((PARTS, nl)),
            dma((PARTS, n)),
            dma((PARTS, n)),
        ],
        compiler_params=pltpu.CompilerParams(
            collective_id=2, has_side_effects=True, vmem_limit_bytes=VMEM_LIMIT
        ),
        name="fused_decoder",
    )(feat, weight, table, table_back, obs, lat)


def fused_shards(features, proj_weight, basis_vals, row_of, col_off, observed, lat_weight):
    ne = lax.axis_size("ens")
    nl = lax.axis_size("lon")
    feat = features[0]
    chan, cells = feat.shape
    share = pl.cdiv(pl.cdiv(ROWS, ne), 16) * 16
    ahead, back = side_tables(kernel_rows(basis_vals, row_of, col_off))
    grad, part = fused(
        ne, nl, feat, proj_weight, ahead, back, observed, lat_weight.reshape(1, LAT), share
    )
    scale = 1.0 / math.sqrt(ne * (cells // LAT) * nl * LAT)
    tops = part[:TOPS].reshape(K, MAIN, chan)
    lows = part[TOPS : K * O].reshape(K, LEFT, chan)
    part = jnp.concatenate([tops, lows], axis=1).reshape(K * O, chan)
    return (grad[None], part.astype(F32) * scale)


def shards(*args):
    cells = args[0].shape[2]
    sizes = (lax.axis_size("ens"), lax.axis_size("lon"))
    if cells % WIDE == 0 and cells // WIDE >= 8 and PART % (16 * sizes[0]) == 0 and sizes[1] > 1:
        return fused_shards(*args)
    return split_shards(*args)


def solution(mesh):
    in_specs = (P("ens", None, "lon"), P(), P(), P(), P(), P(None, "lon"), P())
    out_specs = (P("ens", None, "lon"), P())
    return jax.shard_map(shards, mesh=mesh, in_specs=in_specs, out_specs=out_specs, check_vma=False)
```

```python
import functools
import math

import jax
import jax.numpy as jnp
from jax import lax
from jax.experimental import pallas as pl
from jax.experimental.pallas import tpu as pltpu
from jax.sharding import PartitionSpec as P

O = 72
OP = 80
K = 9
R = 4
LAT = 32
SMOOTH = 0.25
BLK = 256
HALF = 128
F32 = jnp.float32
BF16 = jnp.bfloat16
MESH = pl.DeviceIdType.MESH
VMEM_LIMIT = 60 * 1024 * 1024


def whole(shape):
    return pl.BlockSpec(shape, lambda s: (0,) * len(shape))


def kernel_rows(basis_vals, row_of, col_off):
    code = (col_off + R) * LAT + row_of
    ids = jnp.arange((2 * R + 1) * LAT, dtype=jnp.int32)
    hit = (code[:, :, None] == ids[None, None, :]).astype(F32)
    table = jnp.einsum("isk,isq->ikq", basis_vals, hit, precision=lax.Precision.HIGHEST)
    return table.astype(BF16)


def side_tables(table):
    taps = 2 * R + 1
    four = table.reshape(LAT, K, taps, LAT)
    ahead = four.transpose(1, 2, 3, 0).reshape(K, taps * LAT, LAT)
    back = four[:, :, ::-1].transpose(1, 2, 0, 3).reshape(K, taps * LAT, LAT)
    return ahead, back


def build_band(table, band):
    lane = lax.broadcasted_iota(jnp.int32, (LAT, BLK), 1)
    spread_lanes = (lane % LAT == lax.broadcasted_iota(jnp.int32, (LAT, BLK), 0)).astype(F32)
    spread_lanes = spread_lanes.astype(BF16)
    place = lane // LAT
    cols = BLK // LAT

    def one(k, carry):
        tiled = jnp.dot(table[k], spread_lanes, preferred_element_type=F32)
        for e in range(2 * cols):
            block = jnp.zeros((LAT, BLK), F32)
            for j in range(cols):
                d = e - j
                if 0 <= d <= 2 * R:
                    block = jnp.where(place == j, tiled[d * LAT : (d + 1) * LAT], block)
            band[k, e * LAT : (e + 1) * LAT, :] = block.astype(BF16)
        return carry

    lax.fori_loop(0, K, one, 0)


def padded_weight(weight):
    wide = weight[...].astype(F32)
    gap = jnp.zeros((OP - O, wide.shape[1]), F32)
    rows = []
    for k in range(K):
        rows += [wide[k * O : (k + 1) * O], gap]
    return jnp.concatenate(rows, axis=0)


def greet(peers):
    barrier = pltpu.get_barrier_semaphore()
    for peer in peers:
        pl.semaphore_signal(barrier, inc=1, device_id=peer, device_id_type=MESH)
    pl.semaphore_wait(barrier, len(peers))


def forward_kernel(
    n, nl, group, steps, share,
    feat, tail, head, weight, table, obs, lat, out, rims,
    wpad, band, proj, dec, flat, recv, send, cot, left, right, rim_left, rim_right,
    ssem1, rsem1, ssem2, rsem2, hsend, hrecv,
):
    s = pl.program_id(0)
    me = lax.axis_index("ens")
    real = group * 2 * O
    own = pl.multiple_of(me * share, 16)
    after = {"lon": lax.rem(lax.axis_index("lon") + 1, nl)}
    before = {"lon": lax.rem(lax.axis_index("lon") + nl - 1, nl)}

    def rim(src, dst, slot, peer):
        return pltpu.make_async_remote_copy(
            src_ref=src,
            dst_ref=dst,
            send_sem=hsend.at[slot],
            recv_sem=hrecv.at[slot],
            device_id=peer,
            device_id_type=MESH,
        )

    def first(q, off):
        peer = lax.rem(me + off, n)
        return pltpu.make_async_remote_copy(
            src_ref=dec.at[q, pl.ds(pl.multiple_of(peer * share, 16), share)],
            dst_ref=recv.at[q, off],
            send_sem=ssem1.at[q, off],
            recv_sem=rsem1.at[q, off],
            device_id={"ens": peer},
            device_id_type=MESH,
        )

    def second(q, off):
        return pltpu.make_async_remote_copy(
            src_ref=send.at[q, off],
            dst_ref=cot.at[q, pl.ds(own, share)],
            send_sem=ssem2.at[q, off],
            recv_sem=rsem2.at[q, off],
            device_id={"ens": lax.rem(me - off + n, n)},
            device_id_type=MESH,
        )

    def put(values, h, lo):
        for k in range(K):
            proj[k, h, :, lo : lo + HALF] = values[k * OP : (k + 1) * OP].astype(BF16)

    @pl.when(s == 0)
    def _():
        greet([{"ens": lax.rem(me + off, n)} for off in range(1, n)] + [after, before])
        rim(tail, left, 0, after).start()
        rim(head, right, 1, before).start()
        wpad[...] = padded_weight(weight).astype(BF16)
        build_band(table, band)
        if n * share > real:
            for q in range(steps):
                dec[q, real:, :] = jnp.zeros((n * share - real, HALF), BF16)
            flat[real:, :] = jnp.zeros((n * share - real, HALF), F32)

    @pl.when(s < steps)
    def _():
        def one(b, carry):
            lanes = pl.ds(pl.multiple_of(b * BLK, BLK), BLK)
            got = jnp.dot(wpad[...], feat[:, lanes], preferred_element_type=F32)
            h = s * group + b
            put(got[:, :HALF], h, HALF)
            put(got[:, HALF:], h + 1, 0)
            return carry

        lax.fori_loop(0, group, one, 0)

    @pl.when(s == 1)
    def _():
        rim(tail, left, 0, after).wait()
        put(jnp.dot(wpad[...], left[...], preferred_element_type=F32), 0, 0)

    @pl.when(s == steps)
    def _():
        rim(head, right, 1, before).wait()
        put(jnp.dot(wpad[...], right[...], preferred_element_type=F32), steps * group, HALF)

    @pl.when(jnp.logical_and(s > 0, s <= steps))
    def _():
        q = s - 1
        g0 = q * group
        acc = jnp.zeros((group * OP, BLK), F32)
        for k in range(K):
            for part in range(2):
                lhs = proj[k, pl.ds(g0 + part, group)].reshape(group * OP, BLK)
                acc = acc + jnp.dot(
                    lhs, band[k, part * BLK : (part + 1) * BLK, :], preferred_element_type=F32
                )
        for g in range(group):
            piece = acc[g * OP : g * OP + O]
            both = jnp.concatenate([piece[:, :HALF], piece[:, HALF:]], axis=0)
            dec[q, g * 2 * O : (g + 1) * 2 * O, :] = both.astype(BF16)
        for off in range(1, n):
            first(q, off).start()

    @pl.when(s > 1)
    def _():
        q = s - 2
        for t in range(2 * group):
            flat[t * O : (t + 1) * O, :] = obs[:, t * HALF : (t + 1) * HALF]
        for off in range(1, n):
            first(q, off).wait_recv()
        lat_row = jnp.broadcast_to(lat[0:1, :], (16, HALF))

        def smooth(diff):
            return diff * lax.rsqrt(diff * diff + SMOOTH * SMOOTH)

        def one(step, carry):
            at = pl.multiple_of(step * 16, 16)
            here = pl.ds(pl.multiple_of(own + at, 16), 16)
            values = [dec[q, here, :].astype(F32)]
            values += [recv[q, off, pl.ds(at, 16), :].astype(F32) for off in range(1, n)]
            sums = [None] * n
            for a in range(n):
                for b in range(a + 1, n):
                    pair = smooth(values[a] - values[b])
                    sums[a] = pair if sums[a] is None else sums[a] + pair
                    sums[b] = -pair if sums[b] is None else sums[b] - pair
            target = flat[here, :]
            for a in range(n):
                slope = smooth(values[a] - target) - sums[a] * (1.0 / (n - 1))
                result = (slope * lat_row).astype(BF16)
                if a == 0:
                    cot[q, here, :] = result
                else:
                    send[q, a, pl.ds(at, 16), :] = result
            return carry

        lax.fori_loop(0, share // 16, one, 0)
        for off in range(1, n):
            second(q, off).start()

    @pl.when(s == steps + 1)
    def _():
        for q in range(steps):
            for off in range(1, n):
                first(q, off).wait_send()
                second(q, off).wait()
        last = rim(cot.at[steps - 1, pl.ds(real - OP, OP)], rim_left, 2, after)
        opening = rim(cot.at[0, pl.ds(0, OP)], rim_right, 3, before)
        last.start()
        opening.start()
        for q in range(steps):
            out[q * n * share : (q + 1) * n * share, :] = cot[q]
        last.wait()
        opening.wait()
        rims[0] = rim_left[...]
        rims[1] = rim_right[...]


def forward(n, nl, feat, tail, head, weight, table, obs, lat, group, steps, share):
    chan = feat.shape[0]
    wide = group * BLK
    rows = n * share
    sem = pltpu.SemaphoreType.DMA((steps, n))
    return pl.pallas_call(
        functools.partial(forward_kernel, n, nl, group, steps, share),
        out_shape=(
            jax.ShapeDtypeStruct((steps * rows, HALF), BF16),
            jax.ShapeDtypeStruct((2, OP, HALF), BF16),
        ),
        grid=(steps + 2,),
        in_specs=[
            pl.BlockSpec((chan, wide), lambda s: (0, jnp.minimum(s, steps - 1))),
            whole(tail.shape),
            whole(head.shape),
            whole(weight.shape),
            whole(table.shape),
            pl.BlockSpec((O, wide), lambda s: (0, jnp.clip(s - 2, 0, steps - 1))),
            whole(lat.shape),
        ],
        out_specs=(whole((steps * rows, HALF)), whole((2, OP, HALF))),
        scratch_shapes=[
            pltpu.VMEM((K * OP, chan), BF16),
            pltpu.VMEM((K, 2 * BLK, BLK), BF16),
            pltpu.VMEM((K, steps * group + 1, OP, BLK), BF16),
            pltpu.VMEM((steps, rows, HALF), BF16),
            pltpu.VMEM((rows, HALF), F32),
            pltpu.VMEM((steps, n, share, HALF), BF16),
            pltpu.VMEM((steps, n, share, HALF), BF16),
            pltpu.VMEM((steps, rows, HALF), BF16),
            pltpu.VMEM((chan, HALF), BF16),
            pltpu.VMEM((chan, HALF), BF16),
            pltpu.VMEM((OP, HALF), BF16),
            pltpu.VMEM((OP, HALF), BF16),
            sem,
            sem,
            sem,
            sem,
            pltpu.SemaphoreType.DMA((4,)),
            pltpu.SemaphoreType.DMA((4,)),
        ],
        compiler_params=pltpu.CompilerParams(
            collective_id=0, has_side_effects=True, vmem_limit_bytes=VMEM_LIMIT
        ),
        name="forward_slopes",
    )(feat, tail, head, weight, table, obs, lat)


WG_ROWS = 2048
WG_PART = 656


def backward_kernel(
    group, steps, piece, share, cells, padded,
    cot, left, right, weight, table, feat, grad, wgrad,
    weight_t, band, ext, spread, acc,
):
    s = pl.program_id(0)
    blocks = steps * group

    @pl.when(s == 0)
    def _():
        ext[:, O:, :] = jnp.zeros((blocks + 1, OP - O, BLK), BF16)
        ext[0, :O, :HALF] = left[...].astype(F32)[OP - O :].astype(BF16)
        ext[blocks, :O, HALF:] = right[:O]

        weight_t[...] = padded_weight(weight).T.astype(BF16)
        build_band(table, band)

        def one(b, carry):
            start = lax.div(b, piece) * share + lax.rem(b, piece) * (2 * O)
            pair = cot[pl.ds(pl.multiple_of(start, 16), 2 * O), :].astype(F32)
            ext[b, :O, HALF:] = pair[:O].astype(BF16)
            ext[b + 1, :O, :HALF] = pair[O:].astype(BF16)
            return carry

        lax.fori_loop(0, blocks, one, 0)
        acc[...] = jnp.zeros_like(acc)

    g0 = s * group
    for k in range(K):
        got = jnp.zeros((group * OP, BLK), F32)
        for part in range(2):
            lhs = ext[pl.ds(g0 + part, group)].reshape(group * OP, BLK)
            got = got + jnp.dot(
                lhs, band[k, part * BLK : (part + 1) * BLK, :], preferred_element_type=F32
            )
        if padded:
            row = lax.broadcasted_iota(jnp.int32, got.shape, 0) // OP
            lane = lax.broadcasted_iota(jnp.int32, got.shape, 1)
            got = jnp.where((g0 + row) * BLK + lane < cells, got, 0.0)
        got = got.astype(BF16)
        for g in range(group):
            spread[k * OP : (k + 1) * OP, g * BLK : (g + 1) * BLK] = got[g * OP : (g + 1) * OP]

    acc[...] += lax.dot_general(
        spread[...], feat[...], (((1,), (1,)), ((), ())), preferred_element_type=F32
    )

    def one_grad(n, carry):
        lanes = pl.ds(pl.multiple_of(n * BLK, BLK), BLK)
        grad[:, lanes] = jnp.dot(
            weight_t[...], spread[:, lanes], preferred_element_type=F32
        ).astype(BF16)
        return carry

    lax.fori_loop(0, group, one_grad, 0)

    @pl.when(s == steps - 1)
    def _():
        parts = acc.shape[1] // HALF
        wgrad[parts * WG_PART - 16 :, :] = jnp.zeros((WG_ROWS - parts * WG_PART + 16, HALF), BF16)
        for t in range(parts):
            rows = [
                acc[k * OP : k * OP + O, t * HALF : (t + 1) * HALF] for k in range(K)
            ] + [jnp.zeros((8, HALF), F32)]
            wgrad[t * WG_PART : (t + 1) * WG_PART, :] = jnp.concatenate(rows, axis=0).astype(BF16)


def backward(cot, left, right, weight, table, feat, group, steps, piece, cells):
    chan = feat.shape[0]
    wide = group * BLK
    blocks = steps * group
    return pl.pallas_call(
        functools.partial(
            backward_kernel,
            group,
            steps,
            piece,
            cot.shape[0] * piece // blocks,
            cells,
            cells != blocks * BLK,
        ),
        out_shape=(
            jax.ShapeDtypeStruct(feat.shape, BF16),
            jax.ShapeDtypeStruct((WG_ROWS, HALF), BF16),
        ),
        grid=(steps,),
        in_specs=[
            whole(cot.shape),
            whole(left.shape),
            whole(right.shape),
            whole(weight.shape),
            whole(table.shape),
            pl.BlockSpec((chan, wide), lambda s: (0, s)),
        ],
        out_specs=(pl.BlockSpec((chan, wide), lambda s: (0, s)), whole((WG_ROWS, HALF))),
        scratch_shapes=[
            pltpu.VMEM((chan, K * OP), BF16),
            pltpu.VMEM((K, 2 * BLK, BLK), BF16),
            pltpu.VMEM((blocks + 1, OP, BLK), BF16),
            pltpu.VMEM((K * OP, wide), BF16),
            pltpu.VMEM((K * OP, chan), F32),
        ],
        compiler_params=pltpu.CompilerParams(vmem_limit_bytes=VMEM_LIMIT),
        name="backward_conv",
    )(cot, left, right, weight, table, feat)


def reduce_kernel(ne, nl, scale, part, out, recv1, mid, recv2, got, *sems):
    (ss1, rs1, ss2, rs2, ss3, rs3, ss4, rs4) = sems
    me = lax.axis_index("ens")
    at = lax.axis_index("lon")
    rows = WG_ROWS // ne
    small = rows // nl
    ens_peers = [{"ens": lax.rem(me + off, ne)} for off in range(1, ne)]
    lon_peers = [{"lon": lax.rem(at + off, nl)} for off in range(1, nl)]
    greet(ens_peers + lon_peers)

    def run(copies):
        for copy in copies:
            copy.start()
        for copy in copies:
            copy.wait()

    def send(src, dst, ssem, rsem, peer):
        return pltpu.make_async_remote_copy(
            src_ref=src, dst_ref=dst, send_sem=ssem, recv_sem=rsem, device_id=peer, device_id_type=MESH
        )

    own = pl.multiple_of(me * rows, 16)
    mine = pl.multiple_of(at * small, 8)
    run(
        [
            send(
                part.at[pl.ds(pl.multiple_of(lax.rem(me + off, ne) * rows, 16), rows)],
                recv1.at[off],
                ss1.at[off],
                rs1.at[off],
                {"ens": lax.rem(me + off, ne)},
            )
            for off in range(1, ne)
        ]
    )
    total = part[pl.ds(own, rows), :].astype(F32)
    for off in range(1, ne):
        total = total + recv1[off].astype(F32)
    mid[...] = total
    run(
        [
            send(
                mid.at[pl.ds(pl.multiple_of(lax.rem(at + off, nl) * small, 8), small)],
                recv2.at[off],
                ss2.at[off],
                rs2.at[off],
                {"lon": lax.rem(at + off, nl)},
            )
            for off in range(1, nl)
        ]
    )
    total = mid[pl.ds(mine, small), :]
    for off in range(1, nl):
        total = total + recv2[off]
    recv2[0] = total
    gat = got[1]
    gat[pl.ds(mine, small), :] = total
    run(
        [
            send(
                recv2.at[0],
                gat.at[pl.ds(mine, small)],
                ss3.at[off],
                rs3.at[off],
                {"lon": lax.rem(at + off, nl)},
            )
            for off in range(1, nl)
        ]
    )
    full = got[0]
    full[pl.ds(own, rows), :] = gat[...].astype(BF16)
    run(
        [
            send(
                full.at[pl.ds(own, rows)],
                full.at[pl.ds(own, rows)],
                ss4.at[off],
                rs4.at[off],
                {"ens": lax.rem(me + off, ne)},
            )
            for off in range(1, ne)
        ]
    )
    for t in range(out.shape[1] // HALF):
        piece = full[t * WG_PART : (t + 1) * WG_PART, :].astype(F32) * scale
        out[:, t * HALF : (t + 1) * HALF] = piece[: K * O]


def reduced(ne, nl, scale, part, chan):
    vmem = pl.BlockSpec(memory_space=pltpu.VMEM)
    rows = WG_ROWS // ne
    small = rows // nl

    def body(part, out, recv1, mid, recv2, full, gat, *sems):
        reduce_kernel(ne, nl, scale, part, out, recv1, mid, recv2, (full, gat), *sems)

    return pl.pallas_call(
        body,
        out_shape=jax.ShapeDtypeStruct((K * O, chan), F32),
        in_specs=[vmem],
        out_specs=vmem,
        scratch_shapes=[
            pltpu.VMEM((ne, rows, HALF), BF16),
            pltpu.VMEM((rows, HALF), F32),
            pltpu.VMEM((nl, small, HALF), F32),
            pltpu.VMEM((WG_ROWS, HALF), BF16),
            pltpu.VMEM((rows, HALF), F32),
        ]
        + [pltpu.SemaphoreType.DMA((n,)) for n in (ne, ne, nl, nl, nl, nl, ne, ne)],
        compiler_params=pltpu.CompilerParams(
            collective_id=1, has_side_effects=True, vmem_limit_bytes=VMEM_LIMIT
        ),
        name="weight_reduce",
    )(part)


def passed_along(value, axis, steps):
    count = lax.axis_size(axis)
    return lax.ppermute(value, axis, [(i, (i + steps) % count) for i in range(count)])


def split_shards(features, proj_weight, basis_vals, row_of, col_off, observed, lat_weight):
    ne = lax.axis_size("ens")
    nl = lax.axis_size("lon")
    assert features.shape[0] == 1
    feat = features[0]
    chan, cells = feat.shape
    aligned = cells % BLK == 0
    blocks = cells // BLK if aligned else pl.cdiv(cells + HALF, BLK)
    group_back = max(g for g in range(1, 10) if blocks % g == 0)
    steps_back = blocks // group_back
    group = max(g for g in range(1, 7) if blocks % g == 0)
    steps = blocks // group
    real = group * 2 * O
    share = pl.cdiv(pl.cdiv(real, ne), 16) * 16
    rows = ne * share
    extra = blocks * BLK - cells

    tail = feat[:, cells - HALF :]
    head = feat[:, :HALF]
    ahead, back = side_tables(kernel_rows(basis_vals, row_of, col_off))
    if not aligned:
        right = passed_along(head, "lon", -1)
        feat = jnp.pad(jnp.concatenate([feat, right], axis=1), ((0, 0), (0, extra - HALF)))
        observed = jnp.pad(observed, ((0, 0), (0, extra)))
    lat = jnp.broadcast_to(jnp.tile(lat_weight, HALF // LAT)[None, :], (8, HALF))
    cot, rims = forward(
        ne, nl, feat, tail, head, proj_weight, ahead, observed, lat, group, steps, share
    )

    if aligned:
        cot_left, cot_right = rims[0], rims[1]
    else:
        flat = cot.reshape(steps, rows, HALF)[:, :real].reshape(2 * blocks, O, HALF)
        flat = flat.transpose(1, 0, 2).reshape(O, blocks * BLK)[:, :cells]
        cot_left = passed_along(flat[:, cells - HALF :], "lon", 1)
        cot_right = passed_along(flat[:, :HALF], "lon", -1)
        flat = jnp.pad(
            jnp.concatenate([flat, cot_right], axis=1), ((0, 0), (0, extra - HALF))
        )
        flat = flat.reshape(O, 2 * blocks, HALF).transpose(1, 0, 2).reshape(steps, real, HALF)
        cot = jnp.pad(flat, ((0, 0), (0, rows - real), (0, 0))).reshape(steps * rows, HALF)
        cot_left = jnp.pad(cot_left, ((OP - O, 0), (0, 0)))
        cot_right = jnp.zeros((OP, HALF), BF16)
    grad, part = backward(
        cot, cot_left, cot_right, proj_weight, back, feat, group_back, steps_back, group, cells
    )
    scale = 1.0 / math.sqrt(ne * (cells // LAT) * nl * LAT)
    weight_grad = reduced(ne, nl, scale, part, chan)
    return (grad[:, :cells][None], weight_grad)


GROUP = 5
WIDE = GROUP * BLK
ROWS = GROUP * O
ROWS_P = ROWS + 8
MAIN = 64
LEFT = O - MAIN
SPLIT = GROUP * MAIN
TOPS = K * MAIN
USED = K * O + 8
LAG = 4
PART = 256
PARTS = 3


def ordered_weight(weight):
    rows = weight[...].astype(F32)
    parts = [rows[k * O : k * O + MAIN] for k in range(K)]
    parts += [rows[k * O + MAIN : (k + 1) * O] for k in range(K)]
    return jnp.concatenate(parts, axis=0)


def fused_kernel(
    n, nl, share, steps,
    feat, weight, table, table_back, obs, lat, grad, wout,
    wide, wrows, band, band_back, weight_t, lat_row, proj, sums, edge, first_edge, extra, edge_back,
    give, take, dec, recv, send, cot, seen, rim_left, rim_top, rim_low, spread, gout,
    wacc, wpart, wrecv, wmid, wfull,
    fsem, osem, hsend, hrecv, ssem1, rsem1, ssem2, rsem2, gsem,
    ws1, wr1, ws2, wr2, ws3, wr3,
):
    me = lax.axis_index("ens")
    at = lax.axis_index("lon")
    cells = steps * WIDE
    chan = feat.shape[0]
    own = pl.multiple_of(me * share, 16)
    after = {"lon": lax.rem(at + 1, nl)}
    before = {"lon": lax.rem(at + nl - 1, nl)}
    prow = PART // n

    def remote(src, dst, ssem, rsem, peer):
        return pltpu.make_async_remote_copy(
            src_ref=src, dst_ref=dst, send_sem=ssem, recv_sem=rsem, device_id=peer, device_id_type=MESH
        )

    def piece(c):
        if isinstance(c, int) and c == steps:
            return pltpu.make_async_copy(
                feat.at[:, pl.ds(0, HALF)], wide.at[:, pl.ds(HALF, HALF)], fsem.at[steps]
            )
        if isinstance(c, int) and c == steps - 1:
            lo, size = c * WIDE, WIDE - HALF
        else:
            lo, size = c * WIDE, WIDE
        return pltpu.make_async_copy(
            feat.at[:, pl.ds(pl.multiple_of(lo + HALF, HALF), size)],
            wide.at[:, pl.ds(pl.multiple_of(lo + 2 * HALF, HALF), size)],
            fsem.at[c],
        )

    def seen_copy(q, u):
        c = lax.rem(q + steps - 1, steps)
        t = jnp.minimum(me * (share // 8) + u, ROWS // 8 - 1)
        low = t // (SPLIT // 8)
        row = pl.multiple_of((1 - low) * (t % (MAIN // 8)) * 8 + low * MAIN, 8)
        block = (1 - low) * (t // (MAIN // 8)) + low * (ROWS // 8 - 1 - t)
        lane = pl.multiple_of(c * WIDE + block * BLK, BLK)
        return pltpu.make_async_copy(
            obs.at[pl.ds(row, 8), pl.ds(lane, BLK)], seen.at[q, pl.ds(u * 8, 8)], osem.at[q, u]
        )

    def first(q, off):
        peer = lax.rem(me + off, n)
        return remote(
            dec.at[q, pl.ds(pl.multiple_of(peer * share, 16), share)],
            recv.at[q, off], ssem1.at[q, off], rsem1.at[q, off], {"ens": peer},
        )

    def second(q, off):
        return remote(
            send.at[q, off], cot.at[q, pl.ds(own, share)],
            ssem2.at[q, off], rsem2.at[q, off], {"ens": lax.rem(me - off + n, n)},
        )

    def halo(slot):
        if slot == 0:
            src, dst, peer = give.at[0], take.at[0], after
        elif slot == 1:
            src, dst, peer = give.at[1], take.at[1], before
        elif slot == 2:
            src = cot.at[0, pl.ds(SPLIT - MAIN, MAIN + 16), pl.ds(HALF, HALF)]
            dst, peer = rim_left, after
        elif slot == 3:
            src, dst, peer = cot.at[1, pl.ds(0, MAIN), pl.ds(0, HALF)], rim_top, before
        else:
            src = cot.at[1, pl.ds(ROWS - LEFT, 16), pl.ds(0, HALF)]
            dst, peer = rim_low, before
        return remote(src, dst, hsend.at[slot], hrecv.at[slot], peer)

    def out_copy(t):
        return pltpu.make_async_copy(
            gout.at[lax.rem(t, 2)], grad.at[:, pl.ds(pl.multiple_of(t * WIDE, WIDE), WIDE)], gsem.at[t]
        )

    def scatter(j, off):
        peer = lax.rem(me + off, n)
        return remote(
            wpart.at[j, pl.ds(pl.multiple_of(peer * prow, 16), prow)], wrecv.at[j, off],
            ws1.at[j, off], wr1.at[j, off], {"ens": peer},
        )

    def across(j, off):
        return remote(
            wmid.at[j, at], wmid.at[j, at], ws2.at[j, off], wr2.at[j, off], {"lon": lax.rem(at + off, nl)}
        )

    def gather(j, off):
        mine = pl.ds(pl.multiple_of(me * prow, 16), prow)
        return remote(
            wfull.at[j, mine], wfull.at[j, mine], ws3.at[j, off], wr3.at[j, off],
            {"ens": lax.rem(me + off, n)},
        )

    def project_edges():
        start = (steps - 1) * WIDE
        lanes = jnp.concatenate(
            [wide[:, HALF:BLK], wide[:, cells : cells + HALF], wide[:, start : start + BLK]], axis=1
        )
        got = jnp.dot(wrows[...], lanes, preferred_element_type=F32)
        acc = jnp.zeros((3 * O, BLK), F32)
        out = jnp.zeros((O, BLK), F32)
        none = jnp.zeros((O, HALF), F32)
        for k in range(K):
            part = jnp.concatenate(
                [got[k * MAIN : (k + 1) * MAIN], got[TOPS + k * LEFT : TOPS + (k + 1) * LEFT]], axis=0
            )
            head = jnp.concatenate([none, part[:, :HALF]], axis=1)
            tail = jnp.concatenate([part[:, HALF:BLK], none], axis=1)
            lhs = jnp.concatenate([head, tail, part[:, BLK:]], axis=0).astype(BF16)
            acc = acc + jnp.dot(lhs, band[k, :BLK, :], preferred_element_type=F32)
            out = out + jnp.dot(head.astype(BF16), band[k, BLK:, :], preferred_element_type=F32)
        first_edge[...] = acc[:O]
        edge[...] = acc[2 * O :]
        give[0] = acc[O : 2 * O, :HALF]
        give[1] = out[:, HALF:]
        halo(0).start()
        halo(1).start()

    def forward_chunk(q):
        c = lax.rem(q + steps - 1, steps)
        got = jnp.dot(
            wrows[...],
            wide[:, pl.ds(pl.multiple_of(c * WIDE + BLK, BLK), WIDE)],
            preferred_element_type=F32,
        )
        gap = jnp.zeros((ROWS_P - ROWS, BLK), F32)
        tops = got[:TOPS].astype(BF16)
        for k in range(K):
            for g in range(GROUP):
                proj[k, g * MAIN : (g + 1) * MAIN, :] = tops[
                    k * MAIN : (k + 1) * MAIN, g * BLK : (g + 1) * BLK
                ]
            lows = [
                got[TOPS + k * LEFT : TOPS + (k + 1) * LEFT, g * BLK : (g + 1) * BLK]
                for g in reversed(range(GROUP))
            ]
            proj[k, SPLIT:, :] = jnp.concatenate(lows + [gap], axis=0).astype(BF16)
        def one_half(half, carry):
            acc = jnp.zeros((ROWS_P, BLK), F32)
            rows = pl.ds(pl.multiple_of(half * BLK, BLK), BLK)
            for k in range(K):
                acc = acc + jnp.dot(proj[k], band[k, rows, :], preferred_element_type=F32)
            sums[half] = acc
            return carry

        lax.fori_loop(0, 2, one_half, 0)

        @pl.when(q == 0)
        def _():
            halo(1).wait()
            extra[:, HALF:] = take[1]

        @pl.when(q == 1)
        def _():
            halo(0).wait()
            extra[...] = jnp.zeros_like(extra)
            edge[...] = first_edge[...]
            edge[:, :HALF] += take[0]

        last = SPLIT - MAIN
        dec[q, :last, :] = (
            jnp.concatenate([edge[:MAIN], sums[0, : last - MAIN]], axis=0) + sums[1, :last]
        ).astype(BF16)
        dec[q, last:SPLIT, :] = (
            sums[0, last - MAIN : last] + sums[1, last:SPLIT] + extra[:MAIN]
        ).astype(BF16)
        lows = jnp.concatenate([sums[0, SPLIT + LEFT : ROWS], edge[MAIN:]], axis=0) + sums[1, SPLIT:ROWS]
        lows = [lows[:LEFT] + extra[MAIN:], lows[LEFT:]]
        rest = jnp.zeros((n * share - ROWS, BLK), F32)
        dec[q, SPLIT:, :] = jnp.concatenate(lows + [rest], axis=0).astype(BF16)
        edge[...] = sums[0, last : SPLIT + LEFT]
        for off in range(1, n):
            first(q, off).start()

    def smooth(diff):
        return diff * lax.rsqrt(diff * diff + SMOOTH * SMOOTH)

    def slopes(q):
        for u in range(share // 8):
            seen_copy(q, u).wait()
        for off in range(1, n):
            first(q, off).wait_recv()

        def one(step, carry):
            row = pl.multiple_of(lax.div(step, 2) * 16, 16)
            lanes = pl.ds(pl.multiple_of(lax.rem(step, 2) * HALF, HALF), HALF)
            here = pl.ds(pl.multiple_of(own + row, 16), 16)
            values = [dec[q, here, lanes].astype(F32)]
            values += [recv[q, off, pl.ds(row, 16), lanes].astype(F32) for off in range(1, n)]
            sums = [None] * n
            for a in range(n):
                for b in range(a + 1, n):
                    pair = smooth(values[a] - values[b])
                    sums[a] = pair if sums[a] is None else sums[a] + pair
                    sums[b] = -pair if sums[b] is None else sums[b] - pair
            target = seen[q, pl.ds(row, 16), lanes]
            area = jnp.broadcast_to(lat_row[0:1, lanes], (16, HALF))
            for a in range(n):
                slope = smooth(values[a] - target) - sums[a] * (1.0 / (n - 1))
                result = (slope * area).astype(BF16)
                if a == 0:
                    cot[q, here, lanes] = result
                else:
                    send[q, a, pl.ds(row, 16), lanes] = result
            return carry

        lax.fori_loop(0, share // 16 * 2, one, 0)
        for off in range(1, n):
            second(q, off).start()

    def store_lows(lows, lanes):
        both = jnp.concatenate(lows + [jnp.zeros((USED - K * O, BLK), F32)], axis=0)
        spread[TOPS:USED, lanes] = both.astype(BF16)

    def backward_chunk(b):
        q = lax.rem(b + 1, steps)
        lhs = cot[q, pl.ds(0, ROWS_P), :]
        lows = [[] for _ in range(GROUP)]
        for k in range(K):
            ahead = jnp.dot(lhs, band_back[k, :BLK, :], preferred_element_type=F32)
            here = jnp.dot(lhs, band_back[k, BLK:, :], preferred_element_type=F32)
            for g in range(GROUP):
                low = SPLIT + (GROUP - 1 - g) * LEFT
                top = edge_back[k, :MAIN] if g == 0 else ahead[(g - 1) * MAIN : g * MAIN]
                end = edge_back[k, MAIN:] if g == 0 else ahead[low + LEFT : low + 2 * LEFT]
                lanes = pl.ds(pl.multiple_of(b * WIDE + g * BLK, BLK), BLK)
                spread[k * MAIN : (k + 1) * MAIN, lanes] = (
                    here[g * MAIN : (g + 1) * MAIN] + top
                ).astype(BF16)
                lows[g].append(here[low : low + LEFT] + end)
            edge_back[k] = ahead[SPLIT - MAIN : SPLIT + LEFT]
        for g in range(GROUP):
            store_lows(lows[g], pl.ds(pl.multiple_of(b * WIDE + g * BLK, BLK), BLK))

    def add_weight(lanes):
        wacc[:, : K * O] += lax.dot_general(
            wide[:, lanes], spread[: K * O, lanes], (((1,), (1,)), ((), ())), preferred_element_type=F32
        )

    def one_grad(t, carry):
        @pl.when(t >= 2)
        def _():
            out_copy(t - 2).wait()

        lanes = pl.ds(pl.multiple_of(t * WIDE + HALF, HALF), WIDE)
        gout[lax.rem(t, 2)] = jnp.dot(
            weight_t[:, :USED], spread[:, lanes], preferred_element_type=F32
        ).astype(BF16)
        out_copy(t).start()
        return carry

    def after_scatter(j):
        for off in range(1, n):
            scatter(j, off).wait_recv()
        total = wpart[j, pl.ds(pl.multiple_of(me * prow, 16), prow), :].astype(F32)
        for off in range(1, n):
            total = total + wrecv[j, off].astype(F32)
        wmid[j, at] = total.astype(BF16)
        for off in range(1, nl):
            across(j, off).start()

    def after_across(j):
        for off in range(1, nl):
            across(j, off).wait_recv()
        total = wmid[j, 0].astype(F32)
        for z in range(1, nl):
            total = total + wmid[j, z].astype(F32)
        wfull[j, pl.ds(pl.multiple_of(me * prow, 16), prow), :] = total.astype(BF16)
        for off in range(1, n):
            gather(j, off).start()

    for c in [steps - 1, steps, steps - 2]:
        piece(c).start()
    for c in range(steps - 2):
        piece(c).start()

    def look(q, carry):
        for u in range(share // 8):
            seen_copy(q, u).start()
        return carry

    lax.fori_loop(0, steps, look, 0)
    peers = [{"ens": lax.rem(me + off, n)} for off in range(1, n)]
    peers += [{"lon": lax.rem(at + off, nl)} for off in range(1, nl)]
    barrier = pltpu.get_barrier_semaphore()
    for peer in peers:
        pl.semaphore_signal(barrier, inc=1, device_id=peer, device_id_type=MESH)
    build_band(table, band)
    lane = lax.broadcasted_iota(jnp.int32, (LAT, BLK), 1)
    ones = (lane % LAT == lax.broadcasted_iota(jnp.int32, (LAT, BLK), 0)).astype(F32)
    lat_row[...] = jnp.dot(
        jnp.broadcast_to(lat[...], (8, LAT)), ones, precision=lax.Precision.HIGHEST,
        preferred_element_type=F32,
    )
    wrows[...] = ordered_weight(weight).astype(BF16)
    wide[:, :HALF] = jnp.zeros((chan, HALF), BF16)
    wide[:, cells + HALF :] = jnp.zeros((chan, HALF), BF16)
    extra[...] = jnp.zeros_like(extra)
    for c in [steps - 1, steps, steps - 2]:
        piece(c).wait()
    pl.semaphore_wait(barrier, len(peers))
    project_edges()

    def step(s, carry):
        @pl.when(jnp.logical_and(s >= 1, s < steps - 1))
        def _():
            piece(s - 1).wait()

        @pl.when(s < steps)
        def _():
            forward_chunk(s)

        @pl.when(s >= LAG)
        def _():
            slopes(s - LAG)

        return carry

    lax.fori_loop(0, steps, step, 0)
    build_band(table_back, band_back)
    for off in range(1, n):
        second(0, off).wait_recv()
    halo(2).start()
    gap = jnp.zeros((PARTS * PART - K * O, chan), F32)
    rows = jnp.concatenate([ordered_weight(weight), gap], axis=0)
    weight_t[...] = rows.T.astype(BF16)
    wacc[...] = jnp.zeros_like(wacc)
    for off in range(1, n):
        second(1, off).wait_recv()
    halo(3).start()
    halo(4).start()
    halo(2).wait()
    for k in range(K):
        got = jnp.dot(rim_left[...], band_back[k, HALF:BLK, :], preferred_element_type=F32)
        edge_back[k] = got[:O]

    def step_back(b, carry):
        @pl.when(b < LAG)
        def _():
            slopes(steps - LAG + b)

        @pl.when(jnp.logical_and(b >= 1, b < steps - 1))
        def _():
            for off in range(1, n):
                second(b + 1, off).wait_recv()

        backward_chunk(b)
        add_weight(pl.ds(pl.multiple_of(b * WIDE, WIDE), WIDE))
        return carry

    lax.fori_loop(0, steps, step_back, 0)
    halo(3).wait()
    halo(4).wait()
    rim = jnp.concatenate([rim_top[...].astype(F32), rim_low[...].astype(F32)], axis=0).astype(BF16)
    lows = []
    for k in range(K):
        got = jnp.dot(rim, band_back[k, BLK : BLK + HALF, :], preferred_element_type=F32)
        both = got[:O] + edge_back[k]
        spread[k * MAIN : (k + 1) * MAIN, cells : cells + BLK] = both[:MAIN].astype(BF16)
        lows.append(both[MAIN:])
    store_lows(lows, slice(cells, cells + BLK))
    add_weight(pl.ds(cells, BLK))

    def one_part(j, carry):
        wpart[j] = wacc[:, pl.ds(pl.multiple_of(j * PART, PART), PART)].T.astype(BF16)
        for off in range(1, n):
            scatter(j, off).start()
        return carry

    lax.fori_loop(0, PARTS, one_part, 0)

    def late(t, carry):
        one_grad(t, 0)

        @pl.when(jnp.logical_and(t >= 2, t < 2 + PARTS))
        def _():
            after_scatter(t - 2)

        @pl.when(jnp.logical_and(t >= 4, t < 4 + PARTS))
        def _():
            after_across(t - 4)

        return carry

    lax.fori_loop(0, steps, late, 0)
    for j in range(PARTS):
        for off in range(1, n):
            gather(j, off).wait_recv()
        wout[j * PART : (j + 1) * PART, :] = wfull[j]

    def drain(q, carry):
        for off in range(1, n):
            first(q, off).wait_send()
            second(q, off).wait_send()
        return carry

    lax.fori_loop(0, steps, drain, 0)
    for j in range(PARTS):
        for off in range(1, n):
            scatter(j, off).wait_send()
            gather(j, off).wait_send()
        for off in range(1, nl):
            across(j, off).wait_send()
    out_copy(steps - 2).wait()
    out_copy(steps - 1).wait()


def fused(n, nl, feat, weight, table, table_back, obs, lat, share):
    chan, cells = feat.shape
    steps = cells // WIDE
    vmem = pl.BlockSpec(memory_space=pltpu.VMEM)
    anywhere = pl.BlockSpec(memory_space=pl.ANY)
    dma = pltpu.SemaphoreType.DMA
    prow = PART // n
    return pl.pallas_call(
        functools.partial(fused_kernel, n, nl, share, steps),
        out_shape=(
            jax.ShapeDtypeStruct((chan, cells), BF16),
            jax.ShapeDtypeStruct((PARTS * PART, chan), BF16),
        ),
        in_specs=[anywhere, vmem, vmem, vmem, anywhere, vmem],
        out_specs=(anywhere, vmem),
        scratch_shapes=[
            pltpu.VMEM((chan, cells + BLK), BF16),
            pltpu.VMEM((K * O, chan), BF16),
            pltpu.VMEM((K, 2 * BLK, BLK), BF16),
            pltpu.VMEM((K, 2 * BLK, BLK), BF16),
            pltpu.VMEM((chan, PARTS * PART), BF16),
            pltpu.VMEM((8, BLK), F32),
            pltpu.VMEM((K, ROWS_P, BLK), BF16),
            pltpu.VMEM((2, ROWS_P, BLK), F32),
            pltpu.VMEM((O, BLK), F32),
            pltpu.VMEM((O, BLK), F32),
            pltpu.VMEM((O, BLK), F32),
            pltpu.VMEM((K, O, BLK), F32),
            pltpu.VMEM((2, O, HALF), F32),
            pltpu.VMEM((2, O, HALF), F32),
            pltpu.VMEM((steps, n * share, BLK), BF16),
            pltpu.VMEM((steps, n, share, BLK), BF16),
            pltpu.VMEM((steps, n, share, BLK), BF16),
            pltpu.VMEM((steps, n * share, BLK), BF16),
            pltpu.VMEM((steps, share, BLK), F32),
            pltpu.VMEM((MAIN + 16, HALF), BF16),
            pltpu.VMEM((MAIN, HALF), BF16),
            pltpu.VMEM((16, HALF), BF16),
            pltpu.VMEM((USED, cells + BLK), BF16),
            pltpu.VMEM((2, chan, WIDE), BF16),
            pltpu.VMEM((chan, PARTS * PART), F32),
            pltpu.VMEM((PARTS, PART, chan), BF16),
            pltpu.VMEM((PARTS, n, prow, chan), BF16),
            pltpu.VMEM((PARTS, nl, prow, chan), BF16),
            pltpu.VMEM((PARTS, PART, chan), BF16),
            dma((steps + 1,)),
            dma((steps, share // 8)),
            dma((5,)),
            dma((5,)),
            dma((steps, n)),
            dma((steps, n)),
            dma((steps, n)),
            dma((steps, n)),
            dma((steps,)),
            dma((PARTS, n)),
            dma((PARTS, n)),
            dma((PARTS, nl)),
            dma((PARTS, nl)),
            dma((PARTS, n)),
            dma((PARTS, n)),
        ],
        compiler_params=pltpu.CompilerParams(
            collective_id=2, has_side_effects=True, vmem_limit_bytes=VMEM_LIMIT
        ),
        name="fused_decoder",
    )(feat, weight, table, table_back, obs, lat)


def fused_shards(features, proj_weight, basis_vals, row_of, col_off, observed, lat_weight):
    ne = lax.axis_size("ens")
    nl = lax.axis_size("lon")
    feat = features[0]
    chan, cells = feat.shape
    share = pl.cdiv(pl.cdiv(ROWS, ne), 16) * 16
    ahead, back = side_tables(kernel_rows(basis_vals, row_of, col_off))
    grad, part = fused(
        ne, nl, feat, proj_weight, ahead, back, observed, lat_weight.reshape(1, LAT), share
    )
    scale = 1.0 / math.sqrt(ne * (cells // LAT) * nl * LAT)
    tops = part[:TOPS].reshape(K, MAIN, chan)
    lows = part[TOPS : K * O].reshape(K, LEFT, chan)
    part = jnp.concatenate([tops, lows], axis=1).reshape(K * O, chan)
    return (grad[None], part.astype(F32) * scale)


def shards(*args):
    cells = args[0].shape[2]
    sizes = (lax.axis_size("ens"), lax.axis_size("lon"))
    if cells % WIDE == 0 and cells // WIDE >= 8 and PART % (16 * sizes[0]) == 0 and sizes[1] > 1:
        return fused_shards(*args)
    return split_shards(*args)


def solution(mesh):
    in_specs = (P("ens", None, "lon"), P(), P(), P(), P(), P(None, "lon"), P())
    out_specs = (P("ens", None, "lon"), P())
    return jax.shard_map(shards, mesh=mesh, in_specs=in_specs, out_specs=out_specs, check_vma=False)
```

```python
import functools
import math

import jax
import jax.numpy as jnp
from jax import lax
from jax.experimental import pallas as pl
from jax.experimental.pallas import tpu as pltpu
from jax.sharding import PartitionSpec as P

O = 72
OP = 80
K = 9
R = 4
LAT = 32
SMOOTH = 0.25
BLK = 256
HALF = 128
F32 = jnp.float32
BF16 = jnp.bfloat16
MESH = pl.DeviceIdType.MESH
VMEM_LIMIT = 60 * 1024 * 1024


def whole(shape):
    return pl.BlockSpec(shape, lambda s: (0,) * len(shape))


def kernel_rows(basis_vals, row_of, col_off):
    code = (col_off + R) * LAT + row_of
    ids = jnp.arange((2 * R + 1) * LAT, dtype=jnp.int32)
    hit = (code[:, :, None] == ids[None, None, :]).astype(F32)
    table = jnp.einsum("isk,isq->ikq", basis_vals, hit, precision=lax.Precision.HIGHEST)
    return table.astype(BF16)


def side_tables(table):
    taps = 2 * R + 1
    four = table.reshape(LAT, K, taps, LAT)
    ahead = four.transpose(1, 2, 3, 0).reshape(K, taps * LAT, LAT)
    back = four[:, :, ::-1].transpose(1, 2, 0, 3).reshape(K, taps * LAT, LAT)
    return ahead, back


def build_band(table, band):
    lane = lax.broadcasted_iota(jnp.int32, (LAT, BLK), 1)
    spread_lanes = (lane % LAT == lax.broadcasted_iota(jnp.int32, (LAT, BLK), 0)).astype(F32)
    spread_lanes = spread_lanes.astype(BF16)
    place = lane // LAT
    cols = BLK // LAT

    def one(k, carry):
        tiled = jnp.dot(table[k], spread_lanes, preferred_element_type=F32)
        for e in range(2 * cols):
            block = jnp.zeros((LAT, BLK), F32)
            for j in range(cols):
                d = e - j
                if 0 <= d <= 2 * R:
                    block = jnp.where(place == j, tiled[d * LAT : (d + 1) * LAT], block)
            band[k, e * LAT : (e + 1) * LAT, :] = block.astype(BF16)
        return carry

    lax.fori_loop(0, K, one, 0)


def padded_weight(weight):
    wide = weight[...].astype(F32)
    gap = jnp.zeros((OP - O, wide.shape[1]), F32)
    rows = []
    for k in range(K):
        rows += [wide[k * O : (k + 1) * O], gap]
    return jnp.concatenate(rows, axis=0)


def greet(peers):
    barrier = pltpu.get_barrier_semaphore()
    for peer in peers:
        pl.semaphore_signal(barrier, inc=1, device_id=peer, device_id_type=MESH)
    pl.semaphore_wait(barrier, len(peers))


def forward_kernel(
    n, nl, group, steps, share,
    feat, tail, head, weight, table, obs, lat, out, rims,
    wpad, band, proj, dec, flat, recv, send, cot, left, right, rim_left, rim_right,
    ssem1, rsem1, ssem2, rsem2, hsend, hrecv,
):
    s = pl.program_id(0)
    me = lax.axis_index("ens")
    real = group * 2 * O
    own = pl.multiple_of(me * share, 16)
    after = {"lon": lax.rem(lax.axis_index("lon") + 1, nl)}
    before = {"lon": lax.rem(lax.axis_index("lon") + nl - 1, nl)}

    def rim(src, dst, slot, peer):
        return pltpu.make_async_remote_copy(
            src_ref=src,
            dst_ref=dst,
            send_sem=hsend.at[slot],
            recv_sem=hrecv.at[slot],
            device_id=peer,
            device_id_type=MESH,
        )

    def first(q, off):
        peer = lax.rem(me + off, n)
        return pltpu.make_async_remote_copy(
            src_ref=dec.at[q, pl.ds(pl.multiple_of(peer * share, 16), share)],
            dst_ref=recv.at[q, off],
            send_sem=ssem1.at[q, off],
            recv_sem=rsem1.at[q, off],
            device_id={"ens": peer},
            device_id_type=MESH,
        )

    def second(q, off):
        return pltpu.make_async_remote_copy(
            src_ref=send.at[q, off],
            dst_ref=cot.at[q, pl.ds(own, share)],
            send_sem=ssem2.at[q, off],
            recv_sem=rsem2.at[q, off],
            device_id={"ens": lax.rem(me - off + n, n)},
            device_id_type=MESH,
        )

    def put(values, h, lo):
        for k in range(K):
            proj[k, h, :, lo : lo + HALF] = values[k * OP : (k + 1) * OP].astype(BF16)

    @pl.when(s == 0)
    def _():
        greet([{"ens": lax.rem(me + off, n)} for off in range(1, n)] + [after, before])
        rim(tail, left, 0, after).start()
        rim(head, right, 1, before).start()
        wpad[...] = padded_weight(weight).astype(BF16)
        build_band(table, band)
        if n * share > real:
            for q in range(steps):
                dec[q, real:, :] = jnp.zeros((n * share - real, HALF), BF16)
            flat[real:, :] = jnp.zeros((n * share - real, HALF), F32)

    @pl.when(s < steps)
    def _():
        def one(b, carry):
            lanes = pl.ds(pl.multiple_of(b * BLK, BLK), BLK)
            got = jnp.dot(wpad[...], feat[:, lanes], preferred_element_type=F32)
            h = s * group + b
            put(got[:, :HALF], h, HALF)
            put(got[:, HALF:], h + 1, 0)
            return carry

        lax.fori_loop(0, group, one, 0)

    @pl.when(s == 1)
    def _():
        rim(tail, left, 0, after).wait()
        put(jnp.dot(wpad[...], left[...], preferred_element_type=F32), 0, 0)

    @pl.when(s == steps)
    def _():
        rim(head, right, 1, before).wait()
        put(jnp.dot(wpad[...], right[...], preferred_element_type=F32), steps * group, HALF)

    @pl.when(jnp.logical_and(s > 0, s <= steps))
    def _():
        q = s - 1
        g0 = q * group
        acc = jnp.zeros((group * OP, BLK), F32)
        for k in range(K):
            for part in range(2):
                lhs = proj[k, pl.ds(g0 + part, group)].reshape(group * OP, BLK)
                acc = acc + jnp.dot(
                    lhs, band[k, part * BLK : (part + 1) * BLK, :], preferred_element_type=F32
                )
        for g in range(group):
            piece = acc[g * OP : g * OP + O]
            both = jnp.concatenate([piece[:, :HALF], piece[:, HALF:]], axis=0)
            dec[q, g * 2 * O : (g + 1) * 2 * O, :] = both.astype(BF16)
        for off in range(1, n):
            first(q, off).start()

    @pl.when(s > 1)
    def _():
        q = s - 2
        for t in range(2 * group):
            flat[t * O : (t + 1) * O, :] = obs[:, t * HALF : (t + 1) * HALF]
        for off in range(1, n):
            first(q, off).wait_recv()
        lat_row = jnp.broadcast_to(lat[0:1, :], (16, HALF))

        def smooth(diff):
            return diff * lax.rsqrt(diff * diff + SMOOTH * SMOOTH)

        def one(step, carry):
            at = pl.multiple_of(step * 16, 16)
            here = pl.ds(pl.multiple_of(own + at, 16), 16)
            values = [dec[q, here, :].astype(F32)]
            values += [recv[q, off, pl.ds(at, 16), :].astype(F32) for off in range(1, n)]
            sums = [None] * n
            for a in range(n):
                for b in range(a + 1, n):
                    pair = smooth(values[a] - values[b])
                    sums[a] = pair if sums[a] is None else sums[a] + pair
                    sums[b] = -pair if sums[b] is None else sums[b] - pair
            target = flat[here, :]
            for a in range(n):
                slope = smooth(values[a] - target) - sums[a] * (1.0 / (n - 1))
                result = (slope * lat_row).astype(BF16)
                if a == 0:
                    cot[q, here, :] = result
                else:
                    send[q, a, pl.ds(at, 16), :] = result
            return carry

        lax.fori_loop(0, share // 16, one, 0)
        for off in range(1, n):
            second(q, off).start()

    @pl.when(s == steps + 1)
    def _():
        for q in range(steps):
            for off in range(1, n):
                first(q, off).wait_send()
                second(q, off).wait()
        last = rim(cot.at[steps - 1, pl.ds(real - OP, OP)], rim_left, 2, after)
        opening = rim(cot.at[0, pl.ds(0, OP)], rim_right, 3, before)
        last.start()
        opening.start()
        for q in range(steps):
            out[q * n * share : (q + 1) * n * share, :] = cot[q]
        last.wait()
        opening.wait()
        rims[0] = rim_left[...]
        rims[1] = rim_right[...]


def forward(n, nl, feat, tail, head, weight, table, obs, lat, group, steps, share):
    chan = feat.shape[0]
    wide = group * BLK
    rows = n * share
    sem = pltpu.SemaphoreType.DMA((steps, n))
    return pl.pallas_call(
        functools.partial(forward_kernel, n, nl, group, steps, share),
        out_shape=(
            jax.ShapeDtypeStruct((steps * rows, HALF), BF16),
            jax.ShapeDtypeStruct((2, OP, HALF), BF16),
        ),
        grid=(steps + 2,),
        in_specs=[
            pl.BlockSpec((chan, wide), lambda s: (0, jnp.minimum(s, steps - 1))),
            whole(tail.shape),
            whole(head.shape),
            whole(weight.shape),
            whole(table.shape),
            pl.BlockSpec((O, wide), lambda s: (0, jnp.clip(s - 2, 0, steps - 1))),
            whole(lat.shape),
        ],
        out_specs=(whole((steps * rows, HALF)), whole((2, OP, HALF))),
        scratch_shapes=[
            pltpu.VMEM((K * OP, chan), BF16),
            pltpu.VMEM((K, 2 * BLK, BLK), BF16),
            pltpu.VMEM((K, steps * group + 1, OP, BLK), BF16),
            pltpu.VMEM((steps, rows, HALF), BF16),
            pltpu.VMEM((rows, HALF), F32),
            pltpu.VMEM((steps, n, share, HALF), BF16),
            pltpu.VMEM((steps, n, share, HALF), BF16),
            pltpu.VMEM((steps, rows, HALF), BF16),
            pltpu.VMEM((chan, HALF), BF16),
            pltpu.VMEM((chan, HALF), BF16),
            pltpu.VMEM((OP, HALF), BF16),
            pltpu.VMEM((OP, HALF), BF16),
            sem,
            sem,
            sem,
            sem,
            pltpu.SemaphoreType.DMA((4,)),
            pltpu.SemaphoreType.DMA((4,)),
        ],
        compiler_params=pltpu.CompilerParams(
            collective_id=0, has_side_effects=True, vmem_limit_bytes=VMEM_LIMIT
        ),
        name="forward_slopes",
    )(feat, tail, head, weight, table, obs, lat)


WG_ROWS = 2048
WG_PART = 656


def backward_kernel(
    group, steps, piece, share, cells, padded,
    cot, left, right, weight, table, feat, grad, wgrad,
    weight_t, band, ext, spread, acc,
):
    s = pl.program_id(0)
    blocks = steps * group

    @pl.when(s == 0)
    def _():
        ext[:, O:, :] = jnp.zeros((blocks + 1, OP - O, BLK), BF16)
        ext[0, :O, :HALF] = left[...].astype(F32)[OP - O :].astype(BF16)
        ext[blocks, :O, HALF:] = right[:O]

        weight_t[...] = padded_weight(weight).T.astype(BF16)
        build_band(table, band)

        def one(b, carry):
            start = lax.div(b, piece) * share + lax.rem(b, piece) * (2 * O)
            pair = cot[pl.ds(pl.multiple_of(start, 16), 2 * O), :].astype(F32)
            ext[b, :O, HALF:] = pair[:O].astype(BF16)
            ext[b + 1, :O, :HALF] = pair[O:].astype(BF16)
            return carry

        lax.fori_loop(0, blocks, one, 0)
        acc[...] = jnp.zeros_like(acc)

    g0 = s * group
    for k in range(K):
        got = jnp.zeros((group * OP, BLK), F32)
        for part in range(2):
            lhs = ext[pl.ds(g0 + part, group)].reshape(group * OP, BLK)
            got = got + jnp.dot(
                lhs, band[k, part * BLK : (part + 1) * BLK, :], preferred_element_type=F32
            )
        if padded:
            row = lax.broadcasted_iota(jnp.int32, got.shape, 0) // OP
            lane = lax.broadcasted_iota(jnp.int32, got.shape, 1)
            got = jnp.where((g0 + row) * BLK + lane < cells, got, 0.0)
        got = got.astype(BF16)
        for g in range(group):
            spread[k * OP : (k + 1) * OP, g * BLK : (g + 1) * BLK] = got[g * OP : (g + 1) * OP]

    acc[...] += lax.dot_general(
        spread[...], feat[...], (((1,), (1,)), ((), ())), preferred_element_type=F32
    )

    def one_grad(n, carry):
        lanes = pl.ds(pl.multiple_of(n * BLK, BLK), BLK)
        grad[:, lanes] = jnp.dot(
            weight_t[...], spread[:, lanes], preferred_element_type=F32
        ).astype(BF16)
        return carry

    lax.fori_loop(0, group, one_grad, 0)

    @pl.when(s == steps - 1)
    def _():
        parts = acc.shape[1] // HALF
        wgrad[parts * WG_PART - 16 :, :] = jnp.zeros((WG_ROWS - parts * WG_PART + 16, HALF), BF16)
        for t in range(parts):
            rows = [
                acc[k * OP : k * OP + O, t * HALF : (t + 1) * HALF] for k in range(K)
            ] + [jnp.zeros((8, HALF), F32)]
            wgrad[t * WG_PART : (t + 1) * WG_PART, :] = jnp.concatenate(rows, axis=0).astype(BF16)


def backward(cot, left, right, weight, table, feat, group, steps, piece, cells):
    chan = feat.shape[0]
    wide = group * BLK
    blocks = steps * group
    return pl.pallas_call(
        functools.partial(
            backward_kernel,
            group,
            steps,
            piece,
            cot.shape[0] * piece // blocks,
            cells,
            cells != blocks * BLK,
        ),
        out_shape=(
            jax.ShapeDtypeStruct(feat.shape, BF16),
            jax.ShapeDtypeStruct((WG_ROWS, HALF), BF16),
        ),
        grid=(steps,),
        in_specs=[
            whole(cot.shape),
            whole(left.shape),
            whole(right.shape),
            whole(weight.shape),
            whole(table.shape),
            pl.BlockSpec((chan, wide), lambda s: (0, s)),
        ],
        out_specs=(pl.BlockSpec((chan, wide), lambda s: (0, s)), whole((WG_ROWS, HALF))),
        scratch_shapes=[
            pltpu.VMEM((chan, K * OP), BF16),
            pltpu.VMEM((K, 2 * BLK, BLK), BF16),
            pltpu.VMEM((blocks + 1, OP, BLK), BF16),
            pltpu.VMEM((K * OP, wide), BF16),
            pltpu.VMEM((K * OP, chan), F32),
        ],
        compiler_params=pltpu.CompilerParams(vmem_limit_bytes=VMEM_LIMIT),
        name="backward_conv",
    )(cot, left, right, weight, table, feat)


def reduce_kernel(ne, nl, scale, part, out, recv1, mid, recv2, got, *sems):
    (ss1, rs1, ss2, rs2, ss3, rs3, ss4, rs4) = sems
    me = lax.axis_index("ens")
    at = lax.axis_index("lon")
    rows = WG_ROWS // ne
    small = rows // nl
    ens_peers = [{"ens": lax.rem(me + off, ne)} for off in range(1, ne)]
    lon_peers = [{"lon": lax.rem(at + off, nl)} for off in range(1, nl)]
    greet(ens_peers + lon_peers)

    def run(copies):
        for copy in copies:
            copy.start()
        for copy in copies:
            copy.wait()

    def send(src, dst, ssem, rsem, peer):
        return pltpu.make_async_remote_copy(
            src_ref=src, dst_ref=dst, send_sem=ssem, recv_sem=rsem, device_id=peer, device_id_type=MESH
        )

    own = pl.multiple_of(me * rows, 16)
    mine = pl.multiple_of(at * small, 8)
    run(
        [
            send(
                part.at[pl.ds(pl.multiple_of(lax.rem(me + off, ne) * rows, 16), rows)],
                recv1.at[off],
                ss1.at[off],
                rs1.at[off],
                {"ens": lax.rem(me + off, ne)},
            )
            for off in range(1, ne)
        ]
    )
    total = part[pl.ds(own, rows), :].astype(F32)
    for off in range(1, ne):
        total = total + recv1[off].astype(F32)
    mid[...] = total
    run(
        [
            send(
                mid.at[pl.ds(pl.multiple_of(lax.rem(at + off, nl) * small, 8), small)],
                recv2.at[off],
                ss2.at[off],
                rs2.at[off],
                {"lon": lax.rem(at + off, nl)},
            )
            for off in range(1, nl)
        ]
    )
    total = mid[pl.ds(mine, small), :]
    for off in range(1, nl):
        total = total + recv2[off]
    recv2[0] = total
    gat = got[1]
    gat[pl.ds(mine, small), :] = total
    run(
        [
            send(
                recv2.at[0],
                gat.at[pl.ds(mine, small)],
                ss3.at[off],
                rs3.at[off],
                {"lon": lax.rem(at + off, nl)},
            )
            for off in range(1, nl)
        ]
    )
    full = got[0]
    full[pl.ds(own, rows), :] = gat[...].astype(BF16)
    run(
        [
            send(
                full.at[pl.ds(own, rows)],
                full.at[pl.ds(own, rows)],
                ss4.at[off],
                rs4.at[off],
                {"ens": lax.rem(me + off, ne)},
            )
            for off in range(1, ne)
        ]
    )
    for t in range(out.shape[1] // HALF):
        piece = full[t * WG_PART : (t + 1) * WG_PART, :].astype(F32) * scale
        out[:, t * HALF : (t + 1) * HALF] = piece[: K * O]


def reduced(ne, nl, scale, part, chan):
    vmem = pl.BlockSpec(memory_space=pltpu.VMEM)
    rows = WG_ROWS // ne
    small = rows // nl

    def body(part, out, recv1, mid, recv2, full, gat, *sems):
        reduce_kernel(ne, nl, scale, part, out, recv1, mid, recv2, (full, gat), *sems)

    return pl.pallas_call(
        body,
        out_shape=jax.ShapeDtypeStruct((K * O, chan), F32),
        in_specs=[vmem],
        out_specs=vmem,
        scratch_shapes=[
            pltpu.VMEM((ne, rows, HALF), BF16),
            pltpu.VMEM((rows, HALF), F32),
            pltpu.VMEM((nl, small, HALF), F32),
            pltpu.VMEM((WG_ROWS, HALF), BF16),
            pltpu.VMEM((rows, HALF), F32),
        ]
        + [pltpu.SemaphoreType.DMA((n,)) for n in (ne, ne, nl, nl, nl, nl, ne, ne)],
        compiler_params=pltpu.CompilerParams(
            collective_id=1, has_side_effects=True, vmem_limit_bytes=VMEM_LIMIT
        ),
        name="weight_reduce",
    )(part)


def passed_along(value, axis, steps):
    count = lax.axis_size(axis)
    return lax.ppermute(value, axis, [(i, (i + steps) % count) for i in range(count)])


def split_shards(features, proj_weight, basis_vals, row_of, col_off, observed, lat_weight):
    ne = lax.axis_size("ens")
    nl = lax.axis_size("lon")
    assert features.shape[0] == 1
    feat = features[0]
    chan, cells = feat.shape
    aligned = cells % BLK == 0
    blocks = cells // BLK if aligned else pl.cdiv(cells + HALF, BLK)
    group_back = max(g for g in range(1, 10) if blocks % g == 0)
    steps_back = blocks // group_back
    group = max(g for g in range(1, 7) if blocks % g == 0)
    steps = blocks // group
    real = group * 2 * O
    share = pl.cdiv(pl.cdiv(real, ne), 16) * 16
    rows = ne * share
    extra = blocks * BLK - cells

    tail = feat[:, cells - HALF :]
    head = feat[:, :HALF]
    ahead, back = side_tables(kernel_rows(basis_vals, row_of, col_off))
    if not aligned:
        right = passed_along(head, "lon", -1)
        feat = jnp.pad(jnp.concatenate([feat, right], axis=1), ((0, 0), (0, extra - HALF)))
        observed = jnp.pad(observed, ((0, 0), (0, extra)))
    lat = jnp.broadcast_to(jnp.tile(lat_weight, HALF // LAT)[None, :], (8, HALF))
    cot, rims = forward(
        ne, nl, feat, tail, head, proj_weight, ahead, observed, lat, group, steps, share
    )

    if aligned:
        cot_left, cot_right = rims[0], rims[1]
    else:
        flat = cot.reshape(steps, rows, HALF)[:, :real].reshape(2 * blocks, O, HALF)
        flat = flat.transpose(1, 0, 2).reshape(O, blocks * BLK)[:, :cells]
        cot_left = passed_along(flat[:, cells - HALF :], "lon", 1)
        cot_right = passed_along(flat[:, :HALF], "lon", -1)
        flat = jnp.pad(
            jnp.concatenate([flat, cot_right], axis=1), ((0, 0), (0, extra - HALF))
        )
        flat = flat.reshape(O, 2 * blocks, HALF).transpose(1, 0, 2).reshape(steps, real, HALF)
        cot = jnp.pad(flat, ((0, 0), (0, rows - real), (0, 0))).reshape(steps * rows, HALF)
        cot_left = jnp.pad(cot_left, ((OP - O, 0), (0, 0)))
        cot_right = jnp.zeros((OP, HALF), BF16)
    grad, part = backward(
        cot, cot_left, cot_right, proj_weight, back, feat, group_back, steps_back, group, cells
    )
    scale = 1.0 / math.sqrt(ne * (cells // LAT) * nl * LAT)
    weight_grad = reduced(ne, nl, scale, part, chan)
    return (grad[:, :cells][None], weight_grad)


GROUP = 5
WIDE = GROUP * BLK
ROWS = GROUP * O
ROWS_P = ROWS + 8
MAIN = 64
LEFT = O - MAIN
SPLIT = GROUP * MAIN
TOPS = K * MAIN
USED = K * O + 8
LAG = 4
PART = 256
PARTS = 3


def ordered_weight(weight):
    rows = weight[...].astype(F32)
    parts = [rows[k * O : k * O + MAIN] for k in range(K)]
    parts += [rows[k * O + MAIN : (k + 1) * O] for k in range(K)]
    return jnp.concatenate(parts, axis=0)


def dot_lanes(left, right):
    return lax.dot_general(left, right, (((1,), (1,)), ((), ())), preferred_element_type=F32)


def table_columns(basis_vals, row_of, col_off):
    code = (col_off + R) * LAT + row_of
    ids = jnp.arange((2 * R + 1) * LAT, dtype=jnp.int32)
    hit = (code[:, :, None] == ids[None, None, :]).astype(F32)
    table = jnp.einsum("isk,isq->kqi", basis_vals, hit, precision=lax.Precision.HIGHEST)
    return table.astype(BF16)


def fused_kernel(
    n, nl, share, steps,
    feat, weight, table, obs, lat, grad, wout,
    wide, wrows, band, weight_t, lat_row, proj, sums, edge, first_edge, extra, edge_back,
    give, take, dec, recv, send, cot, seen, rim_left, rim_top, rim_low, spread, gout,
    wacc, wpart, wrecv, wmid, wfull,
    fsem, osem, hsend, hrecv, ssem1, rsem1, ssem2, rsem2, gsem,
    ws1, wr1, ws2, wr2, ws3, wr3,
):
    me = lax.axis_index("ens")
    at = lax.axis_index("lon")
    cells = steps * WIDE
    chan = feat.shape[0]
    own = pl.multiple_of(me * share, 16)
    after = {"lon": lax.rem(at + 1, nl)}
    before = {"lon": lax.rem(at + nl - 1, nl)}
    prow = PART // n

    def remote(src, dst, ssem, rsem, peer):
        return pltpu.make_async_remote_copy(
            src_ref=src, dst_ref=dst, send_sem=ssem, recv_sem=rsem, device_id=peer, device_id_type=MESH
        )

    def piece(c):
        if isinstance(c, int) and c == steps:
            return pltpu.make_async_copy(
                feat.at[:, pl.ds(0, HALF)], wide.at[:, pl.ds(HALF, HALF)], fsem.at[steps]
            )
        if isinstance(c, int) and c == steps - 1:
            lo, size = c * WIDE, WIDE - HALF
        else:
            lo, size = c * WIDE, WIDE
        return pltpu.make_async_copy(
            feat.at[:, pl.ds(pl.multiple_of(lo + HALF, HALF), size)],
            wide.at[:, pl.ds(pl.multiple_of(lo + 2 * HALF, HALF), size)],
            fsem.at[c],
        )

    def seen_copy(q, u):
        c = lax.rem(q + steps - 2, steps)
        t = jnp.minimum(me * (share // 8) + u, ROWS // 8 - 1)
        low = t // (SPLIT // 8)
        row = pl.multiple_of((1 - low) * (t % (MAIN // 8)) * 8 + low * MAIN, 8)
        block = (1 - low) * (t // (MAIN // 8)) + low * (ROWS // 8 - 1 - t)
        lane = pl.multiple_of(c * WIDE + block * BLK, BLK)
        return pltpu.make_async_copy(
            obs.at[pl.ds(row, 8), pl.ds(lane, BLK)], seen.at[q, pl.ds(u * 8, 8)], osem.at[q, u]
        )

    def first(q, off):
        peer = lax.rem(me + off, n)
        return remote(
            dec.at[q, pl.ds(pl.multiple_of(peer * share, 16), share)],
            recv.at[q, off], ssem1.at[q, off], rsem1.at[q, off], {"ens": peer},
        )

    def second(q, off):
        return remote(
            send.at[q, off], cot.at[q, pl.ds(own, share)],
            ssem2.at[q, off], rsem2.at[q, off], {"ens": lax.rem(me - off + n, n)},
        )

    def halo(slot):
        if slot == 0:
            src, dst, peer = give.at[0], take.at[0], after
        elif slot == 1:
            src, dst, peer = give.at[1], take.at[1], before
        elif slot == 2:
            src = cot.at[1, pl.ds(SPLIT - MAIN, MAIN + 16), pl.ds(HALF, HALF)]
            dst, peer = rim_left, after
        elif slot == 3:
            src, dst, peer = cot.at[2, pl.ds(0, MAIN), pl.ds(0, HALF)], rim_top, before
        else:
            src = cot.at[2, pl.ds(ROWS - LEFT, 16), pl.ds(0, HALF)]
            dst, peer = rim_low, before
        return remote(src, dst, hsend.at[slot], hrecv.at[slot], peer)

    def out_copy(t):
        return pltpu.make_async_copy(
            gout.at[lax.rem(t, 2)], grad.at[:, pl.ds(pl.multiple_of(t * WIDE, WIDE), WIDE)], gsem.at[t]
        )

    def scatter(j, off):
        peer = lax.rem(me + off, n)
        return remote(
            wpart.at[j, pl.ds(pl.multiple_of(peer * prow, 16), prow)], wrecv.at[j, off],
            ws1.at[j, off], wr1.at[j, off], {"ens": peer},
        )

    def across(j, off):
        return remote(
            wmid.at[j, at], wmid.at[j, at], ws2.at[j, off], wr2.at[j, off], {"lon": lax.rem(at + off, nl)}
        )

    def gather(j, off):
        mine = pl.ds(pl.multiple_of(me * prow, 16), prow)
        return remote(
            wfull.at[j, mine], wfull.at[j, mine], ws3.at[j, off], wr3.at[j, off],
            {"ens": lax.rem(me + off, n)},
        )

    def project_edges():
        start = (steps - 2) * WIDE
        lanes = jnp.concatenate(
            [wide[:, HALF:BLK], wide[:, cells : cells + HALF], wide[:, start : start + BLK]], axis=1
        )
        got = jnp.dot(wrows[...], lanes, preferred_element_type=F32)
        acc = jnp.zeros((3 * O, BLK), F32)
        out = jnp.zeros((O, BLK), F32)
        none = jnp.zeros((O, HALF), F32)
        for k in range(K):
            part = jnp.concatenate(
                [got[k * MAIN : (k + 1) * MAIN], got[TOPS + k * LEFT : TOPS + (k + 1) * LEFT]], axis=0
            )
            head = jnp.concatenate([none, part[:, :HALF]], axis=1)
            tail = jnp.concatenate([part[:, HALF:BLK], none], axis=1)
            lhs = jnp.concatenate([head, tail, part[:, BLK:]], axis=0).astype(BF16)
            acc = acc + jnp.dot(lhs, band[k, :BLK, :], preferred_element_type=F32)
            out = out + jnp.dot(head.astype(BF16), band[k, BLK:, :], preferred_element_type=F32)
        first_edge[...] = acc[:O]
        edge[...] = acc[2 * O :]
        give[0] = acc[O : 2 * O, :HALF]
        give[1] = out[:, HALF:]
        halo(0).start()
        halo(1).start()

    def forward_chunk(q):
        c = lax.rem(q + steps - 2, steps)
        got = jnp.dot(
            wrows[...],
            wide[:, pl.ds(pl.multiple_of(c * WIDE + BLK, BLK), WIDE)],
            preferred_element_type=F32,
        )
        gap = jnp.zeros((ROWS_P - ROWS, BLK), F32)
        tops = got[:TOPS].astype(BF16)
        for k in range(K):
            for g in range(GROUP):
                proj[k, g * MAIN : (g + 1) * MAIN, :] = tops[
                    k * MAIN : (k + 1) * MAIN, g * BLK : (g + 1) * BLK
                ]
            lows = [
                got[TOPS + k * LEFT : TOPS + (k + 1) * LEFT, g * BLK : (g + 1) * BLK]
                for g in reversed(range(GROUP))
            ]
            proj[k, SPLIT:, :] = jnp.concatenate(lows + [gap], axis=0).astype(BF16)
        def one_half(half, carry):
            acc = jnp.zeros((ROWS_P, BLK), F32)
            rows = pl.ds(pl.multiple_of(half * BLK, BLK), BLK)
            for k in range(K):
                acc = acc + jnp.dot(proj[k], band[k, rows, :], preferred_element_type=F32)
            sums[half] = acc
            return carry

        lax.fori_loop(0, 2, one_half, 0)

        @pl.when(q == 1)
        def _():
            halo(1).wait()
            extra[:, HALF:] = take[1]

        @pl.when(q == 2)
        def _():
            halo(0).wait()
            extra[...] = jnp.zeros_like(extra)
            edge[...] = first_edge[...]
            edge[:, :HALF] += take[0]

        last = SPLIT - MAIN
        dec[q, :last, :] = (
            jnp.concatenate([edge[:MAIN], sums[0, : last - MAIN]], axis=0) + sums[1, :last]
        ).astype(BF16)
        dec[q, last:SPLIT, :] = (
            sums[0, last - MAIN : last] + sums[1, last:SPLIT] + extra[:MAIN]
        ).astype(BF16)
        lows = jnp.concatenate([sums[0, SPLIT + LEFT : ROWS], edge[MAIN:]], axis=0) + sums[1, SPLIT:ROWS]
        lows = [lows[:LEFT] + extra[MAIN:], lows[LEFT:]]
        rest = jnp.zeros((n * share - ROWS, BLK), F32)
        dec[q, SPLIT:, :] = jnp.concatenate(lows + [rest], axis=0).astype(BF16)
        edge[...] = sums[0, last : SPLIT + LEFT]
        for off in range(1, n):
            first(q, off).start()

    def smooth(diff):
        return diff * lax.rsqrt(diff * diff + SMOOTH * SMOOTH)

    def slopes(q):
        for u in range(share // 8):
            seen_copy(q, u).wait()
        for off in range(1, n):
            first(q, off).wait_recv()

        def one(step, carry):
            row = pl.multiple_of(lax.div(step, 2) * 16, 16)
            lanes = pl.ds(pl.multiple_of(lax.rem(step, 2) * HALF, HALF), HALF)
            here = pl.ds(pl.multiple_of(own + row, 16), 16)
            values = [dec[q, here, lanes].astype(F32)]
            values += [recv[q, off, pl.ds(row, 16), lanes].astype(F32) for off in range(1, n)]
            sums = [None] * n
            for a in range(n):
                for b in range(a + 1, n):
                    pair = smooth(values[a] - values[b])
                    sums[a] = pair if sums[a] is None else sums[a] + pair
                    sums[b] = -pair if sums[b] is None else sums[b] - pair
            target = seen[q, pl.ds(row, 16), lanes]
            area = jnp.broadcast_to(lat_row[0:1, lanes], (16, HALF))
            for a in range(n):
                slope = smooth(values[a] - target) - sums[a] * (1.0 / (n - 1))
                result = (slope * area).astype(BF16)
                if a == 0:
                    cot[q, here, lanes] = result
                else:
                    send[q, a, pl.ds(row, 16), lanes] = result
            return carry

        lax.fori_loop(0, share // 16 * 2, one, 0)
        for off in range(1, n):
            second(q, off).start()

    def store_lows(lows, lanes):
        both = jnp.concatenate(lows + [jnp.zeros((USED - K * O, BLK), F32)], axis=0)
        spread[TOPS:USED, lanes] = both.astype(BF16)

    def backward_chunk(b):
        q = lax.rem(b + 2, steps)
        lhs = cot[q, pl.ds(0, ROWS_P), :]
        lows = [[] for _ in range(GROUP)]
        for k in range(K):
            ahead = dot_lanes(lhs, band[k, BLK:, :])
            here = dot_lanes(lhs, band[k, :BLK, :])
            for g in range(GROUP):
                low = SPLIT + (GROUP - 1 - g) * LEFT
                top = edge_back[k, :MAIN] if g == 0 else ahead[(g - 1) * MAIN : g * MAIN]
                end = edge_back[k, MAIN:] if g == 0 else ahead[low + LEFT : low + 2 * LEFT]
                lanes = pl.ds(pl.multiple_of(b * WIDE + g * BLK, BLK), BLK)
                spread[k * MAIN : (k + 1) * MAIN, lanes] = (
                    here[g * MAIN : (g + 1) * MAIN] + top
                ).astype(BF16)
                lows[g].append(here[low : low + LEFT] + end)
            edge_back[k] = ahead[SPLIT - MAIN : SPLIT + LEFT]
        for g in range(GROUP):
            store_lows(lows[g], pl.ds(pl.multiple_of(b * WIDE + g * BLK, BLK), BLK))

    def add_weight(lanes):
        wacc[:, : K * O] += lax.dot_general(
            wide[:, lanes], spread[: K * O, lanes], (((1,), (1,)), ((), ())), preferred_element_type=F32
        )

    def one_grad(t, carry):
        @pl.when(t >= 2)
        def _():
            out_copy(t - 2).wait()

        lanes = pl.ds(pl.multiple_of(t * WIDE + HALF, HALF), WIDE)
        gout[lax.rem(t, 2)] = jnp.dot(
            weight_t[:, :USED], spread[:, lanes], preferred_element_type=F32
        ).astype(BF16)
        out_copy(t).start()
        return carry

    def after_scatter(j):
        for off in range(1, n):
            scatter(j, off).wait_recv()
        total = wpart[j, pl.ds(pl.multiple_of(me * prow, 16), prow), :].astype(F32)
        for off in range(1, n):
            total = total + wrecv[j, off].astype(F32)
        wmid[j, at] = total.astype(BF16)
        for off in range(1, nl):
            across(j, off).start()

    def after_across(j):
        for off in range(1, nl):
            across(j, off).wait_recv()
        total = wmid[j, 0].astype(F32)
        for z in range(1, nl):
            total = total + wmid[j, z].astype(F32)
        wfull[j, pl.ds(pl.multiple_of(me * prow, 16), prow), :] = total.astype(BF16)
        for off in range(1, n):
            gather(j, off).start()

    for c in [steps - 1, steps, steps - 3, steps - 2]:
        piece(c).start()
    for c in range(steps - 3):
        piece(c).start()

    def look(q, carry):
        for u in range(share // 8):
            seen_copy(q, u).start()
        return carry

    lax.fori_loop(0, steps, look, 0)
    peers = [{"ens": lax.rem(me + off, n)} for off in range(1, n)]
    peers += [{"lon": lax.rem(at + off, nl)} for off in range(1, nl)]
    barrier = pltpu.get_barrier_semaphore()
    for peer in peers:
        pl.semaphore_signal(barrier, inc=1, device_id=peer, device_id_type=MESH)
    build_band(table, band)
    lane = lax.broadcasted_iota(jnp.int32, (LAT, BLK), 1)
    ones = (lane % LAT == lax.broadcasted_iota(jnp.int32, (LAT, BLK), 0)).astype(F32)
    lat_row[...] = jnp.dot(
        jnp.broadcast_to(lat[...], (8, LAT)), ones, precision=lax.Precision.HIGHEST,
        preferred_element_type=F32,
    )
    wrows[...] = ordered_weight(weight).astype(BF16)
    wide[:, :HALF] = jnp.zeros((chan, HALF), BF16)
    wide[:, cells + HALF :] = jnp.zeros((chan, HALF), BF16)
    extra[...] = jnp.zeros_like(extra)
    for c in [steps - 1, steps, steps - 3, steps - 2]:
        piece(c).wait()
    pl.semaphore_wait(barrier, len(peers))
    project_edges()

    def step(s, carry):
        @pl.when(jnp.logical_and(s >= 2, s < steps - 1))
        def _():
            piece(s - 2).wait()

        @pl.when(s < steps)
        def _():
            forward_chunk(s)

        @pl.when(s >= LAG)
        def _():
            slopes(s - LAG)

        return carry

    lax.fori_loop(0, steps, step, 0)
    for q in (1, 2, 0):
        for off in range(1, n):
            second(q, off).wait_recv()
        if q == 1:
            halo(2).start()
        if q == 2:
            halo(3).start()
            halo(4).start()
    gap = jnp.zeros((PARTS * PART - K * O, chan), F32)
    rows = jnp.concatenate([ordered_weight(weight), gap], axis=0)
    weight_t[...] = rows.T.astype(BF16)
    wacc[...] = jnp.zeros_like(wacc)
    halo(2).wait()
    for k in range(K):
        got = dot_lanes(rim_left[...], band[k, BLK:, HALF:])
        edge_back[k] = got[:O]

    def step_back(b, carry):
        @pl.when(b < LAG)
        def _():
            slopes(steps - LAG + b)

        @pl.when(jnp.logical_and(b >= 1, b < steps - 2))
        def _():
            for off in range(1, n):
                second(b + 2, off).wait_recv()

        backward_chunk(b)
        add_weight(pl.ds(pl.multiple_of(b * WIDE, WIDE), WIDE))
        return carry

    lax.fori_loop(0, steps, step_back, 0)
    halo(3).wait()
    halo(4).wait()
    rim = jnp.concatenate([rim_top[...].astype(F32), rim_low[...].astype(F32)], axis=0).astype(BF16)
    lows = []
    for k in range(K):
        got = dot_lanes(rim, band[k, :BLK, :HALF])
        both = got[:O] + edge_back[k]
        spread[k * MAIN : (k + 1) * MAIN, cells : cells + BLK] = both[:MAIN].astype(BF16)
        lows.append(both[MAIN:])
    store_lows(lows, slice(cells, cells + BLK))
    add_weight(pl.ds(cells, BLK))

    def one_part(j, carry):
        wpart[j] = wacc[:, pl.ds(pl.multiple_of(j * PART, PART), PART)].T.astype(BF16)
        for off in range(1, n):
            scatter(j, off).start()
        return carry

    lax.fori_loop(0, PARTS, one_part, 0)

    def late(t, carry):
        one_grad(t, 0)

        @pl.when(jnp.logical_and(t >= 2, t < 2 + PARTS))
        def _():
            after_scatter(t - 2)

        @pl.when(jnp.logical_and(t >= 4, t < 4 + PARTS))
        def _():
            after_across(t - 4)

        return carry

    lax.fori_loop(0, steps, late, 0)
    for j in range(PARTS):
        for off in range(1, n):
            gather(j, off).wait_recv()

    def drain(q, carry):
        for off in range(1, n):
            first(q, off).wait_send()
            second(q, off).wait_send()
        return carry

    rows = [wfull[j].astype(F32) for j in range(PARTS)]
    rows = jnp.concatenate(rows, axis=0)
    parts = []
    for k in range(K):
        parts += [rows[k * MAIN : (k + 1) * MAIN], rows[TOPS + k * LEFT : TOPS + (k + 1) * LEFT]]
    wout[...] = jnp.concatenate(parts, axis=0).astype(BF16)
    lax.fori_loop(0, steps, drain, 0)
    for j in range(PARTS):
        for off in range(1, n):
            scatter(j, off).wait_send()
            gather(j, off).wait_send()
        for off in range(1, nl):
            across(j, off).wait_send()
    out_copy(steps - 2).wait()
    out_copy(steps - 1).wait()


def fused(n, nl, feat, weight, table, obs, lat, share):
    chan, cells = feat.shape
    steps = cells // WIDE
    vmem = pl.BlockSpec(memory_space=pltpu.VMEM)
    anywhere = pl.BlockSpec(memory_space=pl.ANY)
    dma = pltpu.SemaphoreType.DMA
    prow = PART // n
    return pl.pallas_call(
        functools.partial(fused_kernel, n, nl, share, steps),
        out_shape=(
            jax.ShapeDtypeStruct((chan, cells), BF16),
            jax.ShapeDtypeStruct((K * O, chan), BF16),
        ),
        in_specs=[anywhere, vmem, vmem, anywhere, vmem],
        out_specs=(anywhere, vmem),
        scratch_shapes=[
            pltpu.VMEM((chan, cells + BLK), BF16),
            pltpu.VMEM((K * O, chan), BF16),
            pltpu.VMEM((K, 2 * BLK, BLK), BF16),
            pltpu.VMEM((chan, PARTS * PART), BF16),
            pltpu.VMEM((8, BLK), F32),
            pltpu.VMEM((K, ROWS_P, BLK), BF16),
            pltpu.VMEM((2, ROWS_P, BLK), F32),
            pltpu.VMEM((O, BLK), F32),
            pltpu.VMEM((O, BLK), F32),
            pltpu.VMEM((O, BLK), F32),
            pltpu.VMEM((K, O, BLK), F32),
            pltpu.VMEM((2, O, HALF), F32),
            pltpu.VMEM((2, O, HALF), F32),
            pltpu.VMEM((steps, n * share, BLK), BF16),
            pltpu.VMEM((steps, n, share, BLK), BF16),
            pltpu.VMEM((steps, n, share, BLK), BF16),
            pltpu.VMEM((steps, n * share, BLK), BF16),
            pltpu.VMEM((steps, share, BLK), F32),
            pltpu.VMEM((MAIN + 16, HALF), BF16),
            pltpu.VMEM((MAIN, HALF), BF16),
            pltpu.VMEM((16, HALF), BF16),
            pltpu.VMEM((USED, cells + BLK), BF16),
            pltpu.VMEM((2, chan, WIDE), BF16),
            pltpu.VMEM((chan, PARTS * PART), F32),
            pltpu.VMEM((PARTS, PART, chan), BF16),
            pltpu.VMEM((PARTS, n, prow, chan), BF16),
            pltpu.VMEM((PARTS, nl, prow, chan), BF16),
            pltpu.VMEM((PARTS, PART, chan), BF16),
            dma((steps + 1,)),
            dma((steps, share // 8)),
            dma((5,)),
            dma((5,)),
            dma((steps, n)),
            dma((steps, n)),
            dma((steps, n)),
            dma((steps, n)),
            dma((steps,)),
            dma((PARTS, n)),
            dma((PARTS, n)),
            dma((PARTS, nl)),
            dma((PARTS, nl)),
            dma((PARTS, n)),
            dma((PARTS, n)),
        ],
        compiler_params=pltpu.CompilerParams(
            collective_id=2, has_side_effects=True, vmem_limit_bytes=VMEM_LIMIT
        ),
        name="fused_decoder",
    )(feat, weight, table, obs, lat)


def fused_shards(features, proj_weight, basis_vals, row_of, col_off, observed, lat_weight):
    ne = lax.axis_size("ens")
    nl = lax.axis_size("lon")
    feat = features[0]
    chan, cells = feat.shape
    share = pl.cdiv(pl.cdiv(ROWS, ne), 16) * 16
    table = table_columns(basis_vals, row_of, col_off)
    grad, part = fused(
        ne, nl, feat, proj_weight, table, observed, lat_weight.reshape(1, LAT), share
    )
    scale = 1.0 / math.sqrt(ne * (cells // LAT) * nl * LAT)
    return (grad[None], part.astype(F32) * scale)


def shards(*args):
    cells = args[0].shape[2]
    sizes = (lax.axis_size("ens"), lax.axis_size("lon"))
    if cells % WIDE == 0 and cells // WIDE >= 8 and PART % (16 * sizes[0]) == 0 and sizes[1] > 1:
        return fused_shards(*args)
    return split_shards(*args)


def solution(mesh):
    in_specs = (P("ens", None, "lon"), P(), P(), P(), P(), P(None, "lon"), P())
    out_specs = (P("ens", None, "lon"), P())
    return jax.shard_map(shards, mesh=mesh, in_specs=in_specs, out_specs=out_specs, check_vma=False)
```

```python
import functools
import math

import jax
import jax.numpy as jnp
from jax import lax
from jax.experimental import pallas as pl
from jax.experimental.pallas import tpu as pltpu
from jax.sharding import PartitionSpec as P

O = 72
OP = 80
K = 9
R = 4
LAT = 32
SMOOTH = 0.25
BLK = 256
HALF = 128
F32 = jnp.float32
BF16 = jnp.bfloat16
MESH = pl.DeviceIdType.MESH
VMEM_LIMIT = 60 * 1024 * 1024


def whole(shape):
    return pl.BlockSpec(shape, lambda s: (0,) * len(shape))


def kernel_rows(basis_vals, row_of, col_off):
    code = (col_off + R) * LAT + row_of
    ids = jnp.arange((2 * R + 1) * LAT, dtype=jnp.int32)
    hit = (code[:, :, None] == ids[None, None, :]).astype(F32)
    table = jnp.einsum("isk,isq->ikq", basis_vals, hit, precision=lax.Precision.HIGHEST)
    return table.astype(BF16)


def side_tables(table):
    taps = 2 * R + 1
    four = table.reshape(LAT, K, taps, LAT)
    ahead = four.transpose(1, 2, 3, 0).reshape(K, taps * LAT, LAT)
    back = four[:, :, ::-1].transpose(1, 2, 0, 3).reshape(K, taps * LAT, LAT)
    return ahead, back


def build_band(table, band):
    lane = lax.broadcasted_iota(jnp.int32, (LAT, BLK), 1)
    spread_lanes = (lane % LAT == lax.broadcasted_iota(jnp.int32, (LAT, BLK), 0)).astype(F32)
    spread_lanes = spread_lanes.astype(BF16)
    place = lane // LAT
    cols = BLK // LAT

    def one(k, carry):
        tiled = jnp.dot(table[k], spread_lanes, preferred_element_type=F32)
        for e in range(2 * cols):
            block = jnp.zeros((LAT, BLK), F32)
            for j in range(cols):
                d = e - j
                if 0 <= d <= 2 * R:
                    block = jnp.where(place == j, tiled[d * LAT : (d + 1) * LAT], block)
            band[k, e * LAT : (e + 1) * LAT, :] = block.astype(BF16)
        return carry

    lax.fori_loop(0, K, one, 0)


def padded_weight(weight):
    wide = weight[...].astype(F32)
    gap = jnp.zeros((OP - O, wide.shape[1]), F32)
    rows = []
    for k in range(K):
        rows += [wide[k * O : (k + 1) * O], gap]
    return jnp.concatenate(rows, axis=0)


def greet(peers):
    barrier = pltpu.get_barrier_semaphore()
    for peer in peers:
        pl.semaphore_signal(barrier, inc=1, device_id=peer, device_id_type=MESH)
    pl.semaphore_wait(barrier, len(peers))


def forward_kernel(
    n, nl, group, steps, share,
    feat, tail, head, weight, table, obs, lat, out, rims,
    wpad, band, proj, dec, flat, recv, send, cot, left, right, rim_left, rim_right,
    ssem1, rsem1, ssem2, rsem2, hsend, hrecv,
):
    s = pl.program_id(0)
    me = lax.axis_index("ens")
    real = group * 2 * O
    own = pl.multiple_of(me * share, 16)
    after = {"lon": lax.rem(lax.axis_index("lon") + 1, nl)}
    before = {"lon": lax.rem(lax.axis_index("lon") + nl - 1, nl)}

    def rim(src, dst, slot, peer):
        return pltpu.make_async_remote_copy(
            src_ref=src,
            dst_ref=dst,
            send_sem=hsend.at[slot],
            recv_sem=hrecv.at[slot],
            device_id=peer,
            device_id_type=MESH,
        )

    def first(q, off):
        peer = lax.rem(me + off, n)
        return pltpu.make_async_remote_copy(
            src_ref=dec.at[q, pl.ds(pl.multiple_of(peer * share, 16), share)],
            dst_ref=recv.at[q, off],
            send_sem=ssem1.at[q, off],
            recv_sem=rsem1.at[q, off],
            device_id={"ens": peer},
            device_id_type=MESH,
        )

    def second(q, off):
        return pltpu.make_async_remote_copy(
            src_ref=send.at[q, off],
            dst_ref=cot.at[q, pl.ds(own, share)],
            send_sem=ssem2.at[q, off],
            recv_sem=rsem2.at[q, off],
            device_id={"ens": lax.rem(me - off + n, n)},
            device_id_type=MESH,
        )

    def put(values, h, lo):
        for k in range(K):
            proj[k, h, :, lo : lo + HALF] = values[k * OP : (k + 1) * OP].astype(BF16)

    @pl.when(s == 0)
    def _():
        greet([{"ens": lax.rem(me + off, n)} for off in range(1, n)] + [after, before])
        rim(tail, left, 0, after).start()
        rim(head, right, 1, before).start()
        wpad[...] = padded_weight(weight).astype(BF16)
        build_band(table, band)
        if n * share > real:
            for q in range(steps):
                dec[q, real:, :] = jnp.zeros((n * share - real, HALF), BF16)
            flat[real:, :] = jnp.zeros((n * share - real, HALF), F32)

    @pl.when(s < steps)
    def _():
        def one(b, carry):
            lanes = pl.ds(pl.multiple_of(b * BLK, BLK), BLK)
            got = jnp.dot(wpad[...], feat[:, lanes], preferred_element_type=F32)
            h = s * group + b
            put(got[:, :HALF], h, HALF)
            put(got[:, HALF:], h + 1, 0)
            return carry

        lax.fori_loop(0, group, one, 0)

    @pl.when(s == 1)
    def _():
        rim(tail, left, 0, after).wait()
        put(jnp.dot(wpad[...], left[...], preferred_element_type=F32), 0, 0)

    @pl.when(s == steps)
    def _():
        rim(head, right, 1, before).wait()
        put(jnp.dot(wpad[...], right[...], preferred_element_type=F32), steps * group, HALF)

    @pl.when(jnp.logical_and(s > 0, s <= steps))
    def _():
        q = s - 1
        g0 = q * group
        acc = jnp.zeros((group * OP, BLK), F32)
        for k in range(K):
            for part in range(2):
                lhs = proj[k, pl.ds(g0 + part, group)].reshape(group * OP, BLK)
                acc = acc + jnp.dot(
                    lhs, band[k, part * BLK : (part + 1) * BLK, :], preferred_element_type=F32
                )
        for g in range(group):
            piece = acc[g * OP : g * OP + O]
            both = jnp.concatenate([piece[:, :HALF], piece[:, HALF:]], axis=0)
            dec[q, g * 2 * O : (g + 1) * 2 * O, :] = both.astype(BF16)
        for off in range(1, n):
            first(q, off).start()

    @pl.when(s > 1)
    def _():
        q = s - 2
        for t in range(2 * group):
            flat[t * O : (t + 1) * O, :] = obs[:, t * HALF : (t + 1) * HALF]
        for off in range(1, n):
            first(q, off).wait_recv()
        lat_row = jnp.broadcast_to(lat[0:1, :], (16, HALF))

        def smooth(diff):
            return diff * lax.rsqrt(diff * diff + SMOOTH * SMOOTH)

        def one(step, carry):
            at = pl.multiple_of(step * 16, 16)
            here = pl.ds(pl.multiple_of(own + at, 16), 16)
            values = [dec[q, here, :].astype(F32)]
            values += [recv[q, off, pl.ds(at, 16), :].astype(F32) for off in range(1, n)]
            sums = [None] * n
            for a in range(n):
                for b in range(a + 1, n):
                    pair = smooth(values[a] - values[b])
                    sums[a] = pair if sums[a] is None else sums[a] + pair
                    sums[b] = -pair if sums[b] is None else sums[b] - pair
            target = flat[here, :]
            for a in range(n):
                slope = smooth(values[a] - target) - sums[a] * (1.0 / (n - 1))
                result = (slope * lat_row).astype(BF16)
                if a == 0:
                    cot[q, here, :] = result
                else:
                    send[q, a, pl.ds(at, 16), :] = result
            return carry

        lax.fori_loop(0, share // 16, one, 0)
        for off in range(1, n):
            second(q, off).start()

    @pl.when(s == steps + 1)
    def _():
        for q in range(steps):
            for off in range(1, n):
                first(q, off).wait_send()
                second(q, off).wait()
        last = rim(cot.at[steps - 1, pl.ds(real - OP, OP)], rim_left, 2, after)
        opening = rim(cot.at[0, pl.ds(0, OP)], rim_right, 3, before)
        last.start()
        opening.start()
        for q in range(steps):
            out[q * n * share : (q + 1) * n * share, :] = cot[q]
        last.wait()
        opening.wait()
        rims[0] = rim_left[...]
        rims[1] = rim_right[...]


def forward(n, nl, feat, tail, head, weight, table, obs, lat, group, steps, share):
    chan = feat.shape[0]
    wide = group * BLK
    rows = n * share
    sem = pltpu.SemaphoreType.DMA((steps, n))
    return pl.pallas_call(
        functools.partial(forward_kernel, n, nl, group, steps, share),
        out_shape=(
            jax.ShapeDtypeStruct((steps * rows, HALF), BF16),
            jax.ShapeDtypeStruct((2, OP, HALF), BF16),
        ),
        grid=(steps + 2,),
        in_specs=[
            pl.BlockSpec((chan, wide), lambda s: (0, jnp.minimum(s, steps - 1))),
            whole(tail.shape),
            whole(head.shape),
            whole(weight.shape),
            whole(table.shape),
            pl.BlockSpec((O, wide), lambda s: (0, jnp.clip(s - 2, 0, steps - 1))),
            whole(lat.shape),
        ],
        out_specs=(whole((steps * rows, HALF)), whole((2, OP, HALF))),
        scratch_shapes=[
            pltpu.VMEM((K * OP, chan), BF16),
            pltpu.VMEM((K, 2 * BLK, BLK), BF16),
            pltpu.VMEM((K, steps * group + 1, OP, BLK), BF16),
            pltpu.VMEM((steps, rows, HALF), BF16),
            pltpu.VMEM((rows, HALF), F32),
            pltpu.VMEM((steps, n, share, HALF), BF16),
            pltpu.VMEM((steps, n, share, HALF), BF16),
            pltpu.VMEM((steps, rows, HALF), BF16),
            pltpu.VMEM((chan, HALF), BF16),
            pltpu.VMEM((chan, HALF), BF16),
            pltpu.VMEM((OP, HALF), BF16),
            pltpu.VMEM((OP, HALF), BF16),
            sem,
            sem,
            sem,
            sem,
            pltpu.SemaphoreType.DMA((4,)),
            pltpu.SemaphoreType.DMA((4,)),
        ],
        compiler_params=pltpu.CompilerParams(
            collective_id=0, has_side_effects=True, vmem_limit_bytes=VMEM_LIMIT
        ),
        name="forward_slopes",
    )(feat, tail, head, weight, table, obs, lat)


WG_ROWS = 2048
WG_PART = 656


def backward_kernel(
    group, steps, piece, share, cells, padded,
    cot, left, right, weight, table, feat, grad, wgrad,
    weight_t, band, ext, spread, acc,
):
    s = pl.program_id(0)
    blocks = steps * group

    @pl.when(s == 0)
    def _():
        ext[:, O:, :] = jnp.zeros((blocks + 1, OP - O, BLK), BF16)
        ext[0, :O, :HALF] = left[...].astype(F32)[OP - O :].astype(BF16)
        ext[blocks, :O, HALF:] = right[:O]

        weight_t[...] = padded_weight(weight).T.astype(BF16)
        build_band(table, band)

        def one(b, carry):
            start = lax.div(b, piece) * share + lax.rem(b, piece) * (2 * O)
            pair = cot[pl.ds(pl.multiple_of(start, 16), 2 * O), :].astype(F32)
            ext[b, :O, HALF:] = pair[:O].astype(BF16)
            ext[b + 1, :O, :HALF] = pair[O:].astype(BF16)
            return carry

        lax.fori_loop(0, blocks, one, 0)
        acc[...] = jnp.zeros_like(acc)

    g0 = s * group
    for k in range(K):
        got = jnp.zeros((group * OP, BLK), F32)
        for part in range(2):
            lhs = ext[pl.ds(g0 + part, group)].reshape(group * OP, BLK)
            got = got + jnp.dot(
                lhs, band[k, part * BLK : (part + 1) * BLK, :], preferred_element_type=F32
            )
        if padded:
            row = lax.broadcasted_iota(jnp.int32, got.shape, 0) // OP
            lane = lax.broadcasted_iota(jnp.int32, got.shape, 1)
            got = jnp.where((g0 + row) * BLK + lane < cells, got, 0.0)
        got = got.astype(BF16)
        for g in range(group):
            spread[k * OP : (k + 1) * OP, g * BLK : (g + 1) * BLK] = got[g * OP : (g + 1) * OP]

    acc[...] += lax.dot_general(
        spread[...], feat[...], (((1,), (1,)), ((), ())), preferred_element_type=F32
    )

    def one_grad(n, carry):
        lanes = pl.ds(pl.multiple_of(n * BLK, BLK), BLK)
        grad[:, lanes] = jnp.dot(
            weight_t[...], spread[:, lanes], preferred_element_type=F32
        ).astype(BF16)
        return carry

    lax.fori_loop(0, group, one_grad, 0)

    @pl.when(s == steps - 1)
    def _():
        parts = acc.shape[1] // HALF
        wgrad[parts * WG_PART - 16 :, :] = jnp.zeros((WG_ROWS - parts * WG_PART + 16, HALF), BF16)
        for t in range(parts):
            rows = [
                acc[k * OP : k * OP + O, t * HALF : (t + 1) * HALF] for k in range(K)
            ] + [jnp.zeros((8, HALF), F32)]
            wgrad[t * WG_PART : (t + 1) * WG_PART, :] = jnp.concatenate(rows, axis=0).astype(BF16)


def backward(cot, left, right, weight, table, feat, group, steps, piece, cells):
    chan = feat.shape[0]
    wide = group * BLK
    blocks = steps * group
    return pl.pallas_call(
        functools.partial(
            backward_kernel,
            group,
            steps,
            piece,
            cot.shape[0] * piece // blocks,
            cells,
            cells != blocks * BLK,
        ),
        out_shape=(
            jax.ShapeDtypeStruct(feat.shape, BF16),
            jax.ShapeDtypeStruct((WG_ROWS, HALF), BF16),
        ),
        grid=(steps,),
        in_specs=[
            whole(cot.shape),
            whole(left.shape),
            whole(right.shape),
            whole(weight.shape),
            whole(table.shape),
            pl.BlockSpec((chan, wide), lambda s: (0, s)),
        ],
        out_specs=(pl.BlockSpec((chan, wide), lambda s: (0, s)), whole((WG_ROWS, HALF))),
        scratch_shapes=[
            pltpu.VMEM((chan, K * OP), BF16),
            pltpu.VMEM((K, 2 * BLK, BLK), BF16),
            pltpu.VMEM((blocks + 1, OP, BLK), BF16),
            pltpu.VMEM((K * OP, wide), BF16),
            pltpu.VMEM((K * OP, chan), F32),
        ],
        compiler_params=pltpu.CompilerParams(vmem_limit_bytes=VMEM_LIMIT),
        name="backward_conv",
    )(cot, left, right, weight, table, feat)


def reduce_kernel(ne, nl, scale, part, out, recv1, mid, recv2, got, *sems):
    (ss1, rs1, ss2, rs2, ss3, rs3, ss4, rs4) = sems
    me = lax.axis_index("ens")
    at = lax.axis_index("lon")
    rows = WG_ROWS // ne
    small = rows // nl
    ens_peers = [{"ens": lax.rem(me + off, ne)} for off in range(1, ne)]
    lon_peers = [{"lon": lax.rem(at + off, nl)} for off in range(1, nl)]
    greet(ens_peers + lon_peers)

    def run(copies):
        for copy in copies:
            copy.start()
        for copy in copies:
            copy.wait()

    def send(src, dst, ssem, rsem, peer):
        return pltpu.make_async_remote_copy(
            src_ref=src, dst_ref=dst, send_sem=ssem, recv_sem=rsem, device_id=peer, device_id_type=MESH
        )

    own = pl.multiple_of(me * rows, 16)
    mine = pl.multiple_of(at * small, 8)
    run(
        [
            send(
                part.at[pl.ds(pl.multiple_of(lax.rem(me + off, ne) * rows, 16), rows)],
                recv1.at[off],
                ss1.at[off],
                rs1.at[off],
                {"ens": lax.rem(me + off, ne)},
            )
            for off in range(1, ne)
        ]
    )
    total = part[pl.ds(own, rows), :].astype(F32)
    for off in range(1, ne):
        total = total + recv1[off].astype(F32)
    mid[...] = total
    run(
        [
            send(
                mid.at[pl.ds(pl.multiple_of(lax.rem(at + off, nl) * small, 8), small)],
                recv2.at[off],
                ss2.at[off],
                rs2.at[off],
                {"lon": lax.rem(at + off, nl)},
            )
            for off in range(1, nl)
        ]
    )
    total = mid[pl.ds(mine, small), :]
    for off in range(1, nl):
        total = total + recv2[off]
    recv2[0] = total
    gat = got[1]
    gat[pl.ds(mine, small), :] = total
    run(
        [
            send(
                recv2.at[0],
                gat.at[pl.ds(mine, small)],
                ss3.at[off],
                rs3.at[off],
                {"lon": lax.rem(at + off, nl)},
            )
            for off in range(1, nl)
        ]
    )
    full = got[0]
    full[pl.ds(own, rows), :] = gat[...].astype(BF16)
    run(
        [
            send(
                full.at[pl.ds(own, rows)],
                full.at[pl.ds(own, rows)],
                ss4.at[off],
                rs4.at[off],
                {"ens": lax.rem(me + off, ne)},
            )
            for off in range(1, ne)
        ]
    )
    for t in range(out.shape[1] // HALF):
        piece = full[t * WG_PART : (t + 1) * WG_PART, :].astype(F32) * scale
        out[:, t * HALF : (t + 1) * HALF] = piece[: K * O]


def reduced(ne, nl, scale, part, chan):
    vmem = pl.BlockSpec(memory_space=pltpu.VMEM)
    rows = WG_ROWS // ne
    small = rows // nl

    def body(part, out, recv1, mid, recv2, full, gat, *sems):
        reduce_kernel(ne, nl, scale, part, out, recv1, mid, recv2, (full, gat), *sems)

    return pl.pallas_call(
        body,
        out_shape=jax.ShapeDtypeStruct((K * O, chan), F32),
        in_specs=[vmem],
        out_specs=vmem,
        scratch_shapes=[
            pltpu.VMEM((ne, rows, HALF), BF16),
            pltpu.VMEM((rows, HALF), F32),
            pltpu.VMEM((nl, small, HALF), F32),
            pltpu.VMEM((WG_ROWS, HALF), BF16),
            pltpu.VMEM((rows, HALF), F32),
        ]
        + [pltpu.SemaphoreType.DMA((n,)) for n in (ne, ne, nl, nl, nl, nl, ne, ne)],
        compiler_params=pltpu.CompilerParams(
            collective_id=1, has_side_effects=True, vmem_limit_bytes=VMEM_LIMIT
        ),
        name="weight_reduce",
    )(part)


def passed_along(value, axis, steps):
    count = lax.axis_size(axis)
    return lax.ppermute(value, axis, [(i, (i + steps) % count) for i in range(count)])


def split_shards(features, proj_weight, basis_vals, row_of, col_off, observed, lat_weight):
    ne = lax.axis_size("ens")
    nl = lax.axis_size("lon")
    assert features.shape[0] == 1
    feat = features[0]
    chan, cells = feat.shape
    aligned = cells % BLK == 0
    blocks = cells // BLK if aligned else pl.cdiv(cells + HALF, BLK)
    group_back = max(g for g in range(1, 10) if blocks % g == 0)
    steps_back = blocks // group_back
    group = max(g for g in range(1, 7) if blocks % g == 0)
    steps = blocks // group
    real = group * 2 * O
    share = pl.cdiv(pl.cdiv(real, ne), 16) * 16
    rows = ne * share
    extra = blocks * BLK - cells

    tail = feat[:, cells - HALF :]
    head = feat[:, :HALF]
    ahead, back = side_tables(kernel_rows(basis_vals, row_of, col_off))
    if not aligned:
        right = passed_along(head, "lon", -1)
        feat = jnp.pad(jnp.concatenate([feat, right], axis=1), ((0, 0), (0, extra - HALF)))
        observed = jnp.pad(observed, ((0, 0), (0, extra)))
    lat = jnp.broadcast_to(jnp.tile(lat_weight, HALF // LAT)[None, :], (8, HALF))
    cot, rims = forward(
        ne, nl, feat, tail, head, proj_weight, ahead, observed, lat, group, steps, share
    )

    if aligned:
        cot_left, cot_right = rims[0], rims[1]
    else:
        flat = cot.reshape(steps, rows, HALF)[:, :real].reshape(2 * blocks, O, HALF)
        flat = flat.transpose(1, 0, 2).reshape(O, blocks * BLK)[:, :cells]
        cot_left = passed_along(flat[:, cells - HALF :], "lon", 1)
        cot_right = passed_along(flat[:, :HALF], "lon", -1)
        flat = jnp.pad(
            jnp.concatenate([flat, cot_right], axis=1), ((0, 0), (0, extra - HALF))
        )
        flat = flat.reshape(O, 2 * blocks, HALF).transpose(1, 0, 2).reshape(steps, real, HALF)
        cot = jnp.pad(flat, ((0, 0), (0, rows - real), (0, 0))).reshape(steps * rows, HALF)
        cot_left = jnp.pad(cot_left, ((OP - O, 0), (0, 0)))
        cot_right = jnp.zeros((OP, HALF), BF16)
    grad, part = backward(
        cot, cot_left, cot_right, proj_weight, back, feat, group_back, steps_back, group, cells
    )
    scale = 1.0 / math.sqrt(ne * (cells // LAT) * nl * LAT)
    weight_grad = reduced(ne, nl, scale, part, chan)
    return (grad[:, :cells][None], weight_grad)


GROUP = 5
WIDE = GROUP * BLK
ROWS = GROUP * O
ROWS_P = ROWS + 8
MAIN = 64
LEFT = O - MAIN
SPLIT = GROUP * MAIN
TOPS = K * MAIN
USED = K * O + 8
LAG = 3
PART = 256
PARTS = 3


def ordered_weight(weight):
    rows = weight[...].astype(F32)
    parts = [rows[k * O : k * O + MAIN] for k in range(K)]
    parts += [rows[k * O + MAIN : (k + 1) * O] for k in range(K)]
    return jnp.concatenate(parts, axis=0)


def dot_lanes(left, right):
    return lax.dot_general(left, right, (((1,), (1,)), ((), ())), preferred_element_type=F32)


def table_columns(basis_vals, row_of, col_off):
    code = (col_off + R) * LAT + row_of
    ids = jnp.arange((2 * R + 1) * LAT, dtype=jnp.int32)
    hit = (code[:, :, None] == ids[None, None, :]).astype(F32)
    table = jnp.einsum("isk,isq->kqi", basis_vals, hit, precision=lax.Precision.HIGHEST)
    return table.astype(BF16)


def fused_kernel(
    n, nl, share, steps,
    feat, weight, table, obs, lat, grad, wout,
    wide, wrows, band, weight_t, lat_row, proj, sums, edge, first_edge, extra, edge_back,
    give, take, dec, recv, send, cot, seen, rim_left, rim_top, rim_low, spread, gout,
    wacc, wpart, wrecv, wmid, wfull,
    fsem, osem, hsend, hrecv, ssem1, rsem1, ssem2, rsem2, gsem,
    ws1, wr1, ws2, wr2, ws3, wr3,
):
    me = lax.axis_index("ens")
    at = lax.axis_index("lon")
    cells = steps * WIDE
    chan = feat.shape[0]
    own = pl.multiple_of(me * share, 16)
    after = {"lon": lax.rem(at + 1, nl)}
    before = {"lon": lax.rem(at + nl - 1, nl)}
    prow = PART // n

    def remote(src, dst, ssem, rsem, peer):
        return pltpu.make_async_remote_copy(
            src_ref=src, dst_ref=dst, send_sem=ssem, recv_sem=rsem, device_id=peer, device_id_type=MESH
        )

    def piece(c):
        if isinstance(c, int) and c == steps:
            return pltpu.make_async_copy(
                feat.at[:, pl.ds(0, HALF)], wide.at[:, pl.ds(HALF, HALF)], fsem.at[steps]
            )
        if isinstance(c, int) and c == steps - 1:
            lo, size = c * WIDE, WIDE - HALF
        else:
            lo, size = c * WIDE, WIDE
        return pltpu.make_async_copy(
            feat.at[:, pl.ds(pl.multiple_of(lo + HALF, HALF), size)],
            wide.at[:, pl.ds(pl.multiple_of(lo + 2 * HALF, HALF), size)],
            fsem.at[c],
        )

    def seen_copy(q, u):
        c = lax.rem(q + steps - 2, steps)
        t = jnp.minimum(me * (share // 8) + u, ROWS // 8 - 1)
        low = t // (SPLIT // 8)
        row = pl.multiple_of((1 - low) * (t % (MAIN // 8)) * 8 + low * MAIN, 8)
        block = (1 - low) * (t // (MAIN // 8)) + low * (ROWS // 8 - 1 - t)
        lane = pl.multiple_of(c * WIDE + block * BLK, BLK)
        return pltpu.make_async_copy(
            obs.at[pl.ds(row, 8), pl.ds(lane, BLK)], seen.at[q, pl.ds(u * 8, 8)], osem.at[q, u]
        )

    def first(q, off):
        peer = lax.rem(me + off, n)
        return remote(
            dec.at[q, pl.ds(pl.multiple_of(peer * share, 16), share)],
            recv.at[q, off], ssem1.at[q, off], rsem1.at[q, off], {"ens": peer},
        )

    def second(q, off):
        return remote(
            send.at[q, off], cot.at[q, pl.ds(own, share)],
            ssem2.at[q, off], rsem2.at[q, off], {"ens": lax.rem(me - off + n, n)},
        )

    def halo(slot):
        if slot == 0:
            src, dst, peer = give.at[0], take.at[0], after
        elif slot == 1:
            src, dst, peer = give.at[1], take.at[1], before
        elif slot == 2:
            src = cot.at[1, pl.ds(SPLIT - MAIN, MAIN + 16), pl.ds(HALF, HALF)]
            dst, peer = rim_left, after
        elif slot == 3:
            src, dst, peer = cot.at[2, pl.ds(0, MAIN), pl.ds(0, HALF)], rim_top, before
        else:
            src = cot.at[2, pl.ds(ROWS - LEFT, 16), pl.ds(0, HALF)]
            dst, peer = rim_low, before
        return remote(src, dst, hsend.at[slot], hrecv.at[slot], peer)

    def out_copy(t):
        return pltpu.make_async_copy(
            gout.at[lax.rem(t, 2)], grad.at[:, pl.ds(pl.multiple_of(t * WIDE, WIDE), WIDE)], gsem.at[t]
        )

    def scatter(j, off):
        peer = lax.rem(me + off, n)
        return remote(
            wpart.at[j, pl.ds(pl.multiple_of(peer * prow, 16), prow)], wrecv.at[j, off],
            ws1.at[j, off], wr1.at[j, off], {"ens": peer},
        )

    def across(j, off):
        return remote(
            wmid.at[j, at], wmid.at[j, at], ws2.at[j, off], wr2.at[j, off], {"lon": lax.rem(at + off, nl)}
        )

    def gather(j, off):
        mine = pl.ds(pl.multiple_of(me * prow, 16), prow)
        return remote(
            wfull.at[j, mine], wfull.at[j, mine], ws3.at[j, off], wr3.at[j, off],
            {"ens": lax.rem(me + off, n)},
        )

    def project_edges():
        start = (steps - 2) * WIDE
        lanes = jnp.concatenate(
            [wide[:, HALF:BLK], wide[:, cells : cells + HALF], wide[:, start : start + BLK]], axis=1
        )
        got = jnp.dot(wrows[...], lanes, preferred_element_type=F32)
        acc = jnp.zeros((3 * O, BLK), F32)
        out = jnp.zeros((O, BLK), F32)
        none = jnp.zeros((O, HALF), F32)
        for k in range(K):
            part = jnp.concatenate(
                [got[k * MAIN : (k + 1) * MAIN], got[TOPS + k * LEFT : TOPS + (k + 1) * LEFT]], axis=0
            )
            head = jnp.concatenate([none, part[:, :HALF]], axis=1)
            tail = jnp.concatenate([part[:, HALF:BLK], none], axis=1)
            lhs = jnp.concatenate([head, tail, part[:, BLK:]], axis=0).astype(BF16)
            acc = acc + jnp.dot(lhs, band[k, :BLK, :], preferred_element_type=F32)
            out = out + jnp.dot(head.astype(BF16), band[k, BLK:, :], preferred_element_type=F32)
        first_edge[...] = acc[:O]
        edge[...] = acc[2 * O :]
        give[0] = acc[O : 2 * O, :HALF]
        give[1] = out[:, HALF:]
        halo(0).start()
        halo(1).start()

    def forward_chunk(q):
        c = lax.rem(q + steps - 2, steps)
        got = jnp.dot(
            wrows[...],
            wide[:, pl.ds(pl.multiple_of(c * WIDE + BLK, BLK), WIDE)],
            preferred_element_type=F32,
        )
        gap = jnp.zeros((ROWS_P - ROWS, BLK), F32)
        tops = got[:TOPS].astype(BF16)
        for k in range(K):
            for g in range(GROUP):
                proj[k, g * MAIN : (g + 1) * MAIN, :] = tops[
                    k * MAIN : (k + 1) * MAIN, g * BLK : (g + 1) * BLK
                ]
            lows = [
                got[TOPS + k * LEFT : TOPS + (k + 1) * LEFT, g * BLK : (g + 1) * BLK]
                for g in reversed(range(GROUP))
            ]
            proj[k, SPLIT:, :] = jnp.concatenate(lows + [gap], axis=0).astype(BF16)
        def one_half(half, carry):
            acc = jnp.zeros((ROWS_P, BLK), F32)
            rows = pl.ds(pl.multiple_of(half * BLK, BLK), BLK)
            for k in range(K):
                acc = acc + jnp.dot(proj[k], band[k, rows, :], preferred_element_type=F32)
            sums[half] = acc
            return carry

        lax.fori_loop(0, 2, one_half, 0)

        @pl.when(q == 1)
        def _():
            halo(1).wait()
            extra[:, HALF:] = take[1]

        @pl.when(q == 2)
        def _():
            halo(0).wait()
            extra[...] = jnp.zeros_like(extra)
            edge[...] = first_edge[...]
            edge[:, :HALF] += take[0]

        last = SPLIT - MAIN
        dec[q, :last, :] = (
            jnp.concatenate([edge[:MAIN], sums[0, : last - MAIN]], axis=0) + sums[1, :last]
        ).astype(BF16)
        dec[q, last:SPLIT, :] = (
            sums[0, last - MAIN : last] + sums[1, last:SPLIT] + extra[:MAIN]
        ).astype(BF16)
        lows = jnp.concatenate([sums[0, SPLIT + LEFT : ROWS], edge[MAIN:]], axis=0) + sums[1, SPLIT:ROWS]
        lows = [lows[:LEFT] + extra[MAIN:], lows[LEFT:]]
        rest = jnp.zeros((n * share - ROWS, BLK), F32)
        dec[q, SPLIT:, :] = jnp.concatenate(lows + [rest], axis=0).astype(BF16)
        edge[...] = sums[0, last : SPLIT + LEFT]
        for off in range(1, n):
            first(q, off).start()

    def smooth(diff):
        return diff * lax.rsqrt(diff * diff + SMOOTH * SMOOTH)

    def slopes(q):
        for u in range(share // 8):
            seen_copy(q, u).wait()
        for off in range(1, n):
            first(q, off).wait_recv()

        def one(step, carry):
            row = pl.multiple_of(lax.div(step, 2) * 16, 16)
            lanes = pl.ds(pl.multiple_of(lax.rem(step, 2) * HALF, HALF), HALF)
            here = pl.ds(pl.multiple_of(own + row, 16), 16)
            values = [dec[q, here, lanes].astype(F32)]
            values += [recv[q, off, pl.ds(row, 16), lanes].astype(F32) for off in range(1, n)]
            sums = [None] * n
            for a in range(n):
                for b in range(a + 1, n):
                    pair = smooth(values[a] - values[b])
                    sums[a] = pair if sums[a] is None else sums[a] + pair
                    sums[b] = -pair if sums[b] is None else sums[b] - pair
            target = seen[q, pl.ds(row, 16), lanes]
            area = jnp.broadcast_to(lat_row[0:1, lanes], (16, HALF))
            for a in range(n):
                slope = smooth(values[a] - target) - sums[a] * (1.0 / (n - 1))
                result = (slope * area).astype(BF16)
                if a == 0:
                    cot[q, here, lanes] = result
                else:
                    send[q, a, pl.ds(row, 16), lanes] = result
            return carry

        lax.fori_loop(0, share // 16 * 2, one, 0)
        for off in range(1, n):
            second(q, off).start()

    def store_lows(lows, lanes):
        both = jnp.concatenate(lows + [jnp.zeros((USED - K * O, BLK), F32)], axis=0)
        spread[TOPS:USED, lanes] = both.astype(BF16)

    def backward_chunk(b):
        q = lax.rem(b + 2, steps)
        lhs = cot[q, pl.ds(0, ROWS_P), :]
        lows = [[] for _ in range(GROUP)]
        for k in range(K):
            ahead = dot_lanes(lhs, band[k, BLK:, :])
            here = dot_lanes(lhs, band[k, :BLK, :])
            for g in range(GROUP):
                low = SPLIT + (GROUP - 1 - g) * LEFT
                top = edge_back[k, :MAIN] if g == 0 else ahead[(g - 1) * MAIN : g * MAIN]
                end = edge_back[k, MAIN:] if g == 0 else ahead[low + LEFT : low + 2 * LEFT]
                lanes = pl.ds(pl.multiple_of(b * WIDE + g * BLK, BLK), BLK)
                spread[k * MAIN : (k + 1) * MAIN, lanes] = (
                    here[g * MAIN : (g + 1) * MAIN] + top
                ).astype(BF16)
                lows[g].append(here[low : low + LEFT] + end)
            edge_back[k] = ahead[SPLIT - MAIN : SPLIT + LEFT]
        for g in range(GROUP):
            store_lows(lows[g], pl.ds(pl.multiple_of(b * WIDE + g * BLK, BLK), BLK))

    def add_weight(lanes):
        wacc[:, : K * O] += lax.dot_general(
            wide[:, lanes], spread[: K * O, lanes], (((1,), (1,)), ((), ())), preferred_element_type=F32
        )

    def one_grad(t, carry):
        @pl.when(t >= 2)
        def _():
            out_copy(t - 2).wait()

        lanes = pl.ds(pl.multiple_of(t * WIDE + HALF, HALF), WIDE)
        gout[lax.rem(t, 2)] = jnp.dot(
            weight_t[:, :USED], spread[:, lanes], preferred_element_type=F32
        ).astype(BF16)
        out_copy(t).start()
        return carry

    def after_scatter(j):
        for off in range(1, n):
            scatter(j, off).wait_recv()
        total = wpart[j, pl.ds(pl.multiple_of(me * prow, 16), prow), :].astype(F32)
        for off in range(1, n):
            total = total + wrecv[j, off].astype(F32)
        wmid[j, at] = total.astype(BF16)
        for off in range(1, nl):
            across(j, off).start()

    def after_across(j):
        for off in range(1, nl):
            across(j, off).wait_recv()
        total = wmid[j, 0].astype(F32)
        for z in range(1, nl):
            total = total + wmid[j, z].astype(F32)
        wfull[j, pl.ds(pl.multiple_of(me * prow, 16), prow), :] = total.astype(BF16)
        for off in range(1, n):
            gather(j, off).start()

    for c in [steps - 1, steps, steps - 3, steps - 2]:
        piece(c).start()
    for c in range(steps - 3):
        piece(c).start()

    def look(q, carry):
        for u in range(share // 8):
            seen_copy(q, u).start()
        return carry

    lax.fori_loop(0, steps, look, 0)
    peers = [{"ens": lax.rem(me + off, n)} for off in range(1, n)]
    peers += [{"lon": lax.rem(at + off, nl)} for off in range(1, nl)]
    barrier = pltpu.get_barrier_semaphore()
    for peer in peers:
        pl.semaphore_signal(barrier, inc=1, device_id=peer, device_id_type=MESH)
    build_band(table, band)
    lane = lax.broadcasted_iota(jnp.int32, (LAT, BLK), 1)
    ones = (lane % LAT == lax.broadcasted_iota(jnp.int32, (LAT, BLK), 0)).astype(F32)
    lat_row[...] = jnp.dot(
        jnp.broadcast_to(lat[...], (8, LAT)), ones, precision=lax.Precision.HIGHEST,
        preferred_element_type=F32,
    )
    wrows[...] = ordered_weight(weight).astype(BF16)
    wide[:, :HALF] = jnp.zeros((chan, HALF), BF16)
    wide[:, cells + HALF :] = jnp.zeros((chan, HALF), BF16)
    extra[...] = jnp.zeros_like(extra)
    for c in [steps - 1, steps, steps - 3, steps - 2]:
        piece(c).wait()
    pl.semaphore_wait(barrier, len(peers))
    project_edges()

    def step(s, carry):
        @pl.when(jnp.logical_and(s >= 2, s < steps - 1))
        def _():
            piece(s - 2).wait()

        @pl.when(s < steps)
        def _():
            forward_chunk(s)

        @pl.when(s >= LAG)
        def _():
            slopes(s - LAG)

        return carry

    lax.fori_loop(0, steps, step, 0)
    for q in (1, 2, 0):
        for off in range(1, n):
            second(q, off).wait_recv()
        if q == 1:
            halo(2).start()
        if q == 2:
            halo(3).start()
            halo(4).start()
    gap = jnp.zeros((PARTS * PART - K * O, chan), F32)
    rows = jnp.concatenate([ordered_weight(weight), gap], axis=0)
    weight_t[...] = rows.T.astype(BF16)
    wacc[...] = jnp.zeros_like(wacc)
    halo(2).wait()
    for k in range(K):
        got = dot_lanes(rim_left[...], band[k, BLK:, HALF:])
        edge_back[k] = got[:O]

    def step_back(b, carry):
        @pl.when(b < LAG)
        def _():
            slopes(steps - LAG + b)

        @pl.when(jnp.logical_and(b >= 1, b < steps - 2))
        def _():
            for off in range(1, n):
                second(b + 2, off).wait_recv()

        backward_chunk(b)
        add_weight(pl.ds(pl.multiple_of(b * WIDE, WIDE), WIDE))
        return carry

    lax.fori_loop(0, steps, step_back, 0)
    halo(3).wait()
    halo(4).wait()
    rim = jnp.concatenate([rim_top[...].astype(F32), rim_low[...].astype(F32)], axis=0).astype(BF16)
    lows = []
    for k in range(K):
        got = dot_lanes(rim, band[k, :BLK, :HALF])
        both = got[:O] + edge_back[k]
        spread[k * MAIN : (k + 1) * MAIN, cells : cells + BLK] = both[:MAIN].astype(BF16)
        lows.append(both[MAIN:])
    store_lows(lows, slice(cells, cells + BLK))
    add_weight(pl.ds(cells, BLK))

    def one_part(j, carry):
        wpart[j] = wacc[:, pl.ds(pl.multiple_of(j * PART, PART), PART)].T.astype(BF16)
        for off in range(1, n):
            scatter(j, off).start()
        return carry

    lax.fori_loop(0, PARTS, one_part, 0)

    def late(t, carry):
        one_grad(t, 0)

        @pl.when(jnp.logical_and(t >= 2, t < 2 + PARTS))
        def _():
            after_scatter(t - 2)

        @pl.when(jnp.logical_and(t >= 4, t < 4 + PARTS))
        def _():
            after_across(t - 4)

        return carry

    lax.fori_loop(0, steps, late, 0)
    for j in range(PARTS):
        for off in range(1, n):
            gather(j, off).wait_recv()

    def drain(q, carry):
        for off in range(1, n):
            first(q, off).wait_send()
            second(q, off).wait_send()
        return carry

    rows = [wfull[j].astype(F32) for j in range(PARTS)]
    rows = jnp.concatenate(rows, axis=0)
    parts = []
    for k in range(K):
        parts += [rows[k * MAIN : (k + 1) * MAIN], rows[TOPS + k * LEFT : TOPS + (k + 1) * LEFT]]
    wout[...] = jnp.concatenate(parts, axis=0).astype(BF16)
    lax.fori_loop(0, steps, drain, 0)
    for j in range(PARTS):
        for off in range(1, n):
            scatter(j, off).wait_send()
            gather(j, off).wait_send()
        for off in range(1, nl):
            across(j, off).wait_send()
    out_copy(steps - 2).wait()
    out_copy(steps - 1).wait()


def fused(n, nl, feat, weight, table, obs, lat, share):
    chan, cells = feat.shape
    steps = cells // WIDE
    vmem = pl.BlockSpec(memory_space=pltpu.VMEM)
    anywhere = pl.BlockSpec(memory_space=pl.ANY)
    dma = pltpu.SemaphoreType.DMA
    prow = PART // n
    return pl.pallas_call(
        functools.partial(fused_kernel, n, nl, share, steps),
        out_shape=(
            jax.ShapeDtypeStruct((chan, cells), BF16),
            jax.ShapeDtypeStruct((K * O, chan), BF16),
        ),
        in_specs=[anywhere, vmem, vmem, anywhere, vmem],
        out_specs=(anywhere, vmem),
        scratch_shapes=[
            pltpu.VMEM((chan, cells + BLK), BF16),
            pltpu.VMEM((K * O, chan), BF16),
            pltpu.VMEM((K, 2 * BLK, BLK), BF16),
            pltpu.VMEM((chan, PARTS * PART), BF16),
            pltpu.VMEM((8, BLK), F32),
            pltpu.VMEM((K, ROWS_P, BLK), BF16),
            pltpu.VMEM((2, ROWS_P, BLK), F32),
            pltpu.VMEM((O, BLK), F32),
            pltpu.VMEM((O, BLK), F32),
            pltpu.VMEM((O, BLK), F32),
            pltpu.VMEM((K, O, BLK), F32),
            pltpu.VMEM((2, O, HALF), F32),
            pltpu.VMEM((2, O, HALF), F32),
            pltpu.VMEM((steps, n * share, BLK), BF16),
            pltpu.VMEM((steps, n, share, BLK), BF16),
            pltpu.VMEM((steps, n, share, BLK), BF16),
            pltpu.VMEM((steps, n * share, BLK), BF16),
            pltpu.VMEM((steps, share, BLK), F32),
            pltpu.VMEM((MAIN + 16, HALF), BF16),
            pltpu.VMEM((MAIN, HALF), BF16),
            pltpu.VMEM((16, HALF), BF16),
            pltpu.VMEM((USED, cells + BLK), BF16),
            pltpu.VMEM((2, chan, WIDE), BF16),
            pltpu.VMEM((chan, PARTS * PART), F32),
            pltpu.VMEM((PARTS, PART, chan), BF16),
            pltpu.VMEM((PARTS, n, prow, chan), BF16),
            pltpu.VMEM((PARTS, nl, prow, chan), BF16),
            pltpu.VMEM((PARTS, PART, chan), BF16),
            dma((steps + 1,)),
            dma((steps, share // 8)),
            dma((5,)),
            dma((5,)),
            dma((steps, n)),
            dma((steps, n)),
            dma((steps, n)),
            dma((steps, n)),
            dma((steps,)),
            dma((PARTS, n)),
            dma((PARTS, n)),
            dma((PARTS, nl)),
            dma((PARTS, nl)),
            dma((PARTS, n)),
            dma((PARTS, n)),
        ],
        compiler_params=pltpu.CompilerParams(
            collective_id=2, has_side_effects=True, vmem_limit_bytes=VMEM_LIMIT
        ),
        name="fused_decoder",
    )(feat, weight, table, obs, lat)


def write_kernel(scale, grad, part, out, wout):
    out[...] = grad[...]

    @pl.when(pl.program_id(0) == 0)
    def _():
        wout[...] = part[...].astype(F32) * scale


def written(grad, part, scale, size):
    chan, cells = grad.shape
    block = pl.BlockSpec((size, cells), lambda s: (s, 0))
    return pl.pallas_call(
        functools.partial(write_kernel, scale),
        out_shape=(
            jax.ShapeDtypeStruct(grad.shape, BF16),
            jax.ShapeDtypeStruct(part.shape, F32),
        ),
        grid=(chan // size,),
        in_specs=[block, whole(part.shape)],
        out_specs=(block, whole(part.shape)),
        compiler_params=pltpu.CompilerParams(vmem_limit_bytes=VMEM_LIMIT),
        name="write_results",
    )(grad, part)


def fused_shards(features, proj_weight, basis_vals, row_of, col_off, observed, lat_weight):
    ne = lax.axis_size("ens")
    nl = lax.axis_size("lon")
    feat = features[0]
    chan, cells = feat.shape
    share = pl.cdiv(pl.cdiv(ROWS, ne), 16) * 16
    table = table_columns(basis_vals, row_of, col_off)
    grad, part = fused(
        ne, nl, feat, proj_weight, table, observed, lat_weight.reshape(1, LAT), share
    )
    scale = 1.0 / math.sqrt(ne * (cells // LAT) * nl * LAT)
    grad, weight_grad = written(grad, part, scale, 96)
    return (grad[None], weight_grad)


def shards(*args):
    cells = args[0].shape[2]
    sizes = (lax.axis_size("ens"), lax.axis_size("lon"))
    if cells % WIDE == 0 and cells // WIDE >= 8 and PART % (16 * sizes[0]) == 0 and sizes[1] > 1:
        return fused_shards(*args)
    return split_shards(*args)


def solution(mesh):
    in_specs = (P("ens", None, "lon"), P(), P(), P(), P(), P(None, "lon"), P())
    out_specs = (P("ens", None, "lon"), P())
    return jax.shard_map(shards, mesh=mesh, in_specs=in_specs, out_specs=out_specs, check_vma=False)
```

```python
import functools
import math

import jax
import jax.numpy as jnp
from jax import lax
from jax.experimental import pallas as pl
from jax.experimental.pallas import tpu as pltpu
from jax.sharding import PartitionSpec as P

O = 72
OP = 80
K = 9
R = 4
LAT = 32
SMOOTH = 0.25
BLK = 256
HALF = 128
F32 = jnp.float32
BF16 = jnp.bfloat16
MESH = pl.DeviceIdType.MESH
VMEM_LIMIT = 60 * 1024 * 1024


def whole(shape):
    return pl.BlockSpec(shape, lambda s: (0,) * len(shape))


def kernel_rows(basis_vals, row_of, col_off):
    code = (col_off + R) * LAT + row_of
    ids = jnp.arange((2 * R + 1) * LAT, dtype=jnp.int32)
    hit = (code[:, :, None] == ids[None, None, :]).astype(F32)
    table = jnp.einsum("isk,isq->ikq", basis_vals, hit, precision=lax.Precision.HIGHEST)
    return table.astype(BF16)


def side_tables(table):
    taps = 2 * R + 1
    four = table.reshape(LAT, K, taps, LAT)
    ahead = four.transpose(1, 2, 3, 0).reshape(K, taps * LAT, LAT)
    back = four[:, :, ::-1].transpose(1, 2, 0, 3).reshape(K, taps * LAT, LAT)
    return ahead, back


def build_band(table, band):
    lane = lax.broadcasted_iota(jnp.int32, (LAT, BLK), 1)
    spread_lanes = (lane % LAT == lax.broadcasted_iota(jnp.int32, (LAT, BLK), 0)).astype(F32)
    spread_lanes = spread_lanes.astype(BF16)
    place = lane // LAT
    cols = BLK // LAT

    def one(k, carry):
        tiled = jnp.dot(table[k], spread_lanes, preferred_element_type=F32)
        for e in range(2 * cols):
            block = jnp.zeros((LAT, BLK), F32)
            for j in range(cols):
                d = e - j
                if 0 <= d <= 2 * R:
                    block = jnp.where(place == j, tiled[d * LAT : (d + 1) * LAT], block)
            band[k, e * LAT : (e + 1) * LAT, :] = block.astype(BF16)
        return carry

    lax.fori_loop(0, K, one, 0)


def padded_weight(weight):
    wide = weight[...].astype(F32)
    gap = jnp.zeros((OP - O, wide.shape[1]), F32)
    rows = []
    for k in range(K):
        rows += [wide[k * O : (k + 1) * O], gap]
    return jnp.concatenate(rows, axis=0)


def greet(peers):
    barrier = pltpu.get_barrier_semaphore()
    for peer in peers:
        pl.semaphore_signal(barrier, inc=1, device_id=peer, device_id_type=MESH)
    pl.semaphore_wait(barrier, len(peers))


def forward_kernel(
    n, nl, group, steps, share,
    feat, tail, head, weight, table, obs, lat, out, rims,
    wpad, band, proj, dec, flat, recv, send, cot, left, right, rim_left, rim_right,
    ssem1, rsem1, ssem2, rsem2, hsend, hrecv,
):
    s = pl.program_id(0)
    me = lax.axis_index("ens")
    real = group * 2 * O
    own = pl.multiple_of(me * share, 16)
    after = {"lon": lax.rem(lax.axis_index("lon") + 1, nl)}
    before = {"lon": lax.rem(lax.axis_index("lon") + nl - 1, nl)}

    def rim(src, dst, slot, peer):
        return pltpu.make_async_remote_copy(
            src_ref=src,
            dst_ref=dst,
            send_sem=hsend.at[slot],
            recv_sem=hrecv.at[slot],
            device_id=peer,
            device_id_type=MESH,
        )

    def first(q, off):
        peer = lax.rem(me + off, n)
        return pltpu.make_async_remote_copy(
            src_ref=dec.at[q, pl.ds(pl.multiple_of(peer * share, 16), share)],
            dst_ref=recv.at[q, off],
            send_sem=ssem1.at[q, off],
            recv_sem=rsem1.at[q, off],
            device_id={"ens": peer},
            device_id_type=MESH,
        )

    def second(q, off):
        return pltpu.make_async_remote_copy(
            src_ref=send.at[q, off],
            dst_ref=cot.at[q, pl.ds(own, share)],
            send_sem=ssem2.at[q, off],
            recv_sem=rsem2.at[q, off],
            device_id={"ens": lax.rem(me - off + n, n)},
            device_id_type=MESH,
        )

    def put(values, h, lo):
        for k in range(K):
            proj[k, h, :, lo : lo + HALF] = values[k * OP : (k + 1) * OP].astype(BF16)

    @pl.when(s == 0)
    def _():
        greet([{"ens": lax.rem(me + off, n)} for off in range(1, n)] + [after, before])
        rim(tail, left, 0, after).start()
        rim(head, right, 1, before).start()
        wpad[...] = padded_weight(weight).astype(BF16)
        build_band(table, band)
        if n * share > real:
            for q in range(steps):
                dec[q, real:, :] = jnp.zeros((n * share - real, HALF), BF16)
            flat[real:, :] = jnp.zeros((n * share - real, HALF), F32)

    @pl.when(s < steps)
    def _():
        def one(b, carry):
            lanes = pl.ds(pl.multiple_of(b * BLK, BLK), BLK)
            got = jnp.dot(wpad[...], feat[:, lanes], preferred_element_type=F32)
            h = s * group + b
            put(got[:, :HALF], h, HALF)
            put(got[:, HALF:], h + 1, 0)
            return carry

        lax.fori_loop(0, group, one, 0)

    @pl.when(s == 1)
    def _():
        rim(tail, left, 0, after).wait()
        put(jnp.dot(wpad[...], left[...], preferred_element_type=F32), 0, 0)

    @pl.when(s == steps)
    def _():
        rim(head, right, 1, before).wait()
        put(jnp.dot(wpad[...], right[...], preferred_element_type=F32), steps * group, HALF)

    @pl.when(jnp.logical_and(s > 0, s <= steps))
    def _():
        q = s - 1
        g0 = q * group
        acc = jnp.zeros((group * OP, BLK), F32)
        for k in range(K):
            for part in range(2):
                lhs = proj[k, pl.ds(g0 + part, group)].reshape(group * OP, BLK)
                acc = acc + jnp.dot(
                    lhs, band[k, part * BLK : (part + 1) * BLK, :], preferred_element_type=F32
                )
        for g in range(group):
            piece = acc[g * OP : g * OP + O]
            both = jnp.concatenate([piece[:, :HALF], piece[:, HALF:]], axis=0)
            dec[q, g * 2 * O : (g + 1) * 2 * O, :] = both.astype(BF16)
        for off in range(1, n):
            first(q, off).start()

    @pl.when(s > 1)
    def _():
        q = s - 2
        for t in range(2 * group):
            flat[t * O : (t + 1) * O, :] = obs[:, t * HALF : (t + 1) * HALF]
        for off in range(1, n):
            first(q, off).wait_recv()
        lat_row = jnp.broadcast_to(lat[0:1, :], (16, HALF))

        def smooth(diff):
            return diff * lax.rsqrt(diff * diff + SMOOTH * SMOOTH)

        def one(step, carry):
            at = pl.multiple_of(step * 16, 16)
            here = pl.ds(pl.multiple_of(own + at, 16), 16)
            values = [dec[q, here, :].astype(F32)]
            values += [recv[q, off, pl.ds(at, 16), :].astype(F32) for off in range(1, n)]
            sums = [None] * n
            for a in range(n):
                for b in range(a + 1, n):
                    pair = smooth(values[a] - values[b])
                    sums[a] = pair if sums[a] is None else sums[a] + pair
                    sums[b] = -pair if sums[b] is None else sums[b] - pair
            target = flat[here, :]
            for a in range(n):
                slope = smooth(values[a] - target) - sums[a] * (1.0 / (n - 1))
                result = (slope * lat_row).astype(BF16)
                if a == 0:
                    cot[q, here, :] = result
                else:
                    send[q, a, pl.ds(at, 16), :] = result
            return carry

        lax.fori_loop(0, share // 16, one, 0)
        for off in range(1, n):
            second(q, off).start()

    @pl.when(s == steps + 1)
    def _():
        for q in range(steps):
            for off in range(1, n):
                first(q, off).wait_send()
                second(q, off).wait()
        last = rim(cot.at[steps - 1, pl.ds(real - OP, OP)], rim_left, 2, after)
        opening = rim(cot.at[0, pl.ds(0, OP)], rim_right, 3, before)
        last.start()
        opening.start()
        for q in range(steps):
            out[q * n * share : (q + 1) * n * share, :] = cot[q]
        last.wait()
        opening.wait()
        rims[0] = rim_left[...]
        rims[1] = rim_right[...]


def forward(n, nl, feat, tail, head, weight, table, obs, lat, group, steps, share):
    chan = feat.shape[0]
    wide = group * BLK
    rows = n * share
    sem = pltpu.SemaphoreType.DMA((steps, n))
    return pl.pallas_call(
        functools.partial(forward_kernel, n, nl, group, steps, share),
        out_shape=(
            jax.ShapeDtypeStruct((steps * rows, HALF), BF16),
            jax.ShapeDtypeStruct((2, OP, HALF), BF16),
        ),
        grid=(steps + 2,),
        in_specs=[
            pl.BlockSpec((chan, wide), lambda s: (0, jnp.minimum(s, steps - 1))),
            whole(tail.shape),
            whole(head.shape),
            whole(weight.shape),
            whole(table.shape),
            pl.BlockSpec((O, wide), lambda s: (0, jnp.clip(s - 2, 0, steps - 1))),
            whole(lat.shape),
        ],
        out_specs=(whole((steps * rows, HALF)), whole((2, OP, HALF))),
        scratch_shapes=[
            pltpu.VMEM((K * OP, chan), BF16),
            pltpu.VMEM((K, 2 * BLK, BLK), BF16),
            pltpu.VMEM((K, steps * group + 1, OP, BLK), BF16),
            pltpu.VMEM((steps, rows, HALF), BF16),
            pltpu.VMEM((rows, HALF), F32),
            pltpu.VMEM((steps, n, share, HALF), BF16),
            pltpu.VMEM((steps, n, share, HALF), BF16),
            pltpu.VMEM((steps, rows, HALF), BF16),
            pltpu.VMEM((chan, HALF), BF16),
            pltpu.VMEM((chan, HALF), BF16),
            pltpu.VMEM((OP, HALF), BF16),
            pltpu.VMEM((OP, HALF), BF16),
            sem,
            sem,
            sem,
            sem,
            pltpu.SemaphoreType.DMA((4,)),
            pltpu.SemaphoreType.DMA((4,)),
        ],
        compiler_params=pltpu.CompilerParams(
            collective_id=0, has_side_effects=True, vmem_limit_bytes=VMEM_LIMIT
        ),
        name="forward_slopes",
    )(feat, tail, head, weight, table, obs, lat)


WG_ROWS = 2048
WG_PART = 656


def backward_kernel(
    group, steps, piece, share, cells, padded,
    cot, left, right, weight, table, feat, grad, wgrad,
    weight_t, band, ext, spread, acc,
):
    s = pl.program_id(0)
    blocks = steps * group

    @pl.when(s == 0)
    def _():
        ext[:, O:, :] = jnp.zeros((blocks + 1, OP - O, BLK), BF16)
        ext[0, :O, :HALF] = left[...].astype(F32)[OP - O :].astype(BF16)
        ext[blocks, :O, HALF:] = right[:O]

        weight_t[...] = padded_weight(weight).T.astype(BF16)
        build_band(table, band)

        def one(b, carry):
            start = lax.div(b, piece) * share + lax.rem(b, piece) * (2 * O)
            pair = cot[pl.ds(pl.multiple_of(start, 16), 2 * O), :].astype(F32)
            ext[b, :O, HALF:] = pair[:O].astype(BF16)
            ext[b + 1, :O, :HALF] = pair[O:].astype(BF16)
            return carry

        lax.fori_loop(0, blocks, one, 0)
        acc[...] = jnp.zeros_like(acc)

    g0 = s * group
    for k in range(K):
        got = jnp.zeros((group * OP, BLK), F32)
        for part in range(2):
            lhs = ext[pl.ds(g0 + part, group)].reshape(group * OP, BLK)
            got = got + jnp.dot(
                lhs, band[k, part * BLK : (part + 1) * BLK, :], preferred_element_type=F32
            )
        if padded:
            row = lax.broadcasted_iota(jnp.int32, got.shape, 0) // OP
            lane = lax.broadcasted_iota(jnp.int32, got.shape, 1)
            got = jnp.where((g0 + row) * BLK + lane < cells, got, 0.0)
        got = got.astype(BF16)
        for g in range(group):
            spread[k * OP : (k + 1) * OP, g * BLK : (g + 1) * BLK] = got[g * OP : (g + 1) * OP]

    acc[...] += lax.dot_general(
        spread[...], feat[...], (((1,), (1,)), ((), ())), preferred_element_type=F32
    )

    def one_grad(n, carry):
        lanes = pl.ds(pl.multiple_of(n * BLK, BLK), BLK)
        grad[:, lanes] = jnp.dot(
            weight_t[...], spread[:, lanes], preferred_element_type=F32
        ).astype(BF16)
        return carry

    lax.fori_loop(0, group, one_grad, 0)

    @pl.when(s == steps - 1)
    def _():
        parts = acc.shape[1] // HALF
        wgrad[parts * WG_PART - 16 :, :] = jnp.zeros((WG_ROWS - parts * WG_PART + 16, HALF), BF16)
        for t in range(parts):
            rows = [
                acc[k * OP : k * OP + O, t * HALF : (t + 1) * HALF] for k in range(K)
            ] + [jnp.zeros((8, HALF), F32)]
            wgrad[t * WG_PART : (t + 1) * WG_PART, :] = jnp.concatenate(rows, axis=0).astype(BF16)


def backward(cot, left, right, weight, table, feat, group, steps, piece, cells):
    chan = feat.shape[0]
    wide = group * BLK
    blocks = steps * group
    return pl.pallas_call(
        functools.partial(
            backward_kernel,
            group,
            steps,
            piece,
            cot.shape[0] * piece // blocks,
            cells,
            cells != blocks * BLK,
        ),
        out_shape=(
            jax.ShapeDtypeStruct(feat.shape, BF16),
            jax.ShapeDtypeStruct((WG_ROWS, HALF), BF16),
        ),
        grid=(steps,),
        in_specs=[
            whole(cot.shape),
            whole(left.shape),
            whole(right.shape),
            whole(weight.shape),
            whole(table.shape),
            pl.BlockSpec((chan, wide), lambda s: (0, s)),
        ],
        out_specs=(pl.BlockSpec((chan, wide), lambda s: (0, s)), whole((WG_ROWS, HALF))),
        scratch_shapes=[
            pltpu.VMEM((chan, K * OP), BF16),
            pltpu.VMEM((K, 2 * BLK, BLK), BF16),
            pltpu.VMEM((blocks + 1, OP, BLK), BF16),
            pltpu.VMEM((K * OP, wide), BF16),
            pltpu.VMEM((K * OP, chan), F32),
        ],
        compiler_params=pltpu.CompilerParams(vmem_limit_bytes=VMEM_LIMIT),
        name="backward_conv",
    )(cot, left, right, weight, table, feat)


def reduce_kernel(ne, nl, scale, part, out, recv1, mid, recv2, got, *sems):
    (ss1, rs1, ss2, rs2, ss3, rs3, ss4, rs4) = sems
    me = lax.axis_index("ens")
    at = lax.axis_index("lon")
    rows = WG_ROWS // ne
    small = rows // nl
    ens_peers = [{"ens": lax.rem(me + off, ne)} for off in range(1, ne)]
    lon_peers = [{"lon": lax.rem(at + off, nl)} for off in range(1, nl)]
    greet(ens_peers + lon_peers)

    def run(copies):
        for copy in copies:
            copy.start()
        for copy in copies:
            copy.wait()

    def send(src, dst, ssem, rsem, peer):
        return pltpu.make_async_remote_copy(
            src_ref=src, dst_ref=dst, send_sem=ssem, recv_sem=rsem, device_id=peer, device_id_type=MESH
        )

    own = pl.multiple_of(me * rows, 16)
    mine = pl.multiple_of(at * small, 8)
    run(
        [
            send(
                part.at[pl.ds(pl.multiple_of(lax.rem(me + off, ne) * rows, 16), rows)],
                recv1.at[off],
                ss1.at[off],
                rs1.at[off],
                {"ens": lax.rem(me + off, ne)},
            )
            for off in range(1, ne)
        ]
    )
    total = part[pl.ds(own, rows), :].astype(F32)
    for off in range(1, ne):
        total = total + recv1[off].astype(F32)
    mid[...] = total
    run(
        [
            send(
                mid.at[pl.ds(pl.multiple_of(lax.rem(at + off, nl) * small, 8), small)],
                recv2.at[off],
                ss2.at[off],
                rs2.at[off],
                {"lon": lax.rem(at + off, nl)},
            )
            for off in range(1, nl)
        ]
    )
    total = mid[pl.ds(mine, small), :]
    for off in range(1, nl):
        total = total + recv2[off]
    recv2[0] = total
    gat = got[1]
    gat[pl.ds(mine, small), :] = total
    run(
        [
            send(
                recv2.at[0],
                gat.at[pl.ds(mine, small)],
                ss3.at[off],
                rs3.at[off],
                {"lon": lax.rem(at + off, nl)},
            )
            for off in range(1, nl)
        ]
    )
    full = got[0]
    full[pl.ds(own, rows), :] = gat[...].astype(BF16)
    run(
        [
            send(
                full.at[pl.ds(own, rows)],
                full.at[pl.ds(own, rows)],
                ss4.at[off],
                rs4.at[off],
                {"ens": lax.rem(me + off, ne)},
            )
            for off in range(1, ne)
        ]
    )
    for t in range(out.shape[1] // HALF):
        piece = full[t * WG_PART : (t + 1) * WG_PART, :].astype(F32) * scale
        out[:, t * HALF : (t + 1) * HALF] = piece[: K * O]


def reduced(ne, nl, scale, part, chan):
    vmem = pl.BlockSpec(memory_space=pltpu.VMEM)
    rows = WG_ROWS // ne
    small = rows // nl

    def body(part, out, recv1, mid, recv2, full, gat, *sems):
        reduce_kernel(ne, nl, scale, part, out, recv1, mid, recv2, (full, gat), *sems)

    return pl.pallas_call(
        body,
        out_shape=jax.ShapeDtypeStruct((K * O, chan), F32),
        in_specs=[vmem],
        out_specs=vmem,
        scratch_shapes=[
            pltpu.VMEM((ne, rows, HALF), BF16),
            pltpu.VMEM((rows, HALF), F32),
            pltpu.VMEM((nl, small, HALF), F32),
            pltpu.VMEM((WG_ROWS, HALF), BF16),
            pltpu.VMEM((rows, HALF), F32),
        ]
        + [pltpu.SemaphoreType.DMA((n,)) for n in (ne, ne, nl, nl, nl, nl, ne, ne)],
        compiler_params=pltpu.CompilerParams(
            collective_id=1, has_side_effects=True, vmem_limit_bytes=VMEM_LIMIT
        ),
        name="weight_reduce",
    )(part)


def passed_along(value, axis, steps):
    count = lax.axis_size(axis)
    return lax.ppermute(value, axis, [(i, (i + steps) % count) for i in range(count)])


def split_shards(features, proj_weight, basis_vals, row_of, col_off, observed, lat_weight):
    ne = lax.axis_size("ens")
    nl = lax.axis_size("lon")
    assert features.shape[0] == 1
    feat = features[0]
    chan, cells = feat.shape
    aligned = cells % BLK == 0
    blocks = cells // BLK if aligned else pl.cdiv(cells + HALF, BLK)
    group_back = max(g for g in range(1, 10) if blocks % g == 0)
    steps_back = blocks // group_back
    group = max(g for g in range(1, 7) if blocks % g == 0)
    steps = blocks // group
    real = group * 2 * O
    share = pl.cdiv(pl.cdiv(real, ne), 16) * 16
    rows = ne * share
    extra = blocks * BLK - cells

    tail = feat[:, cells - HALF :]
    head = feat[:, :HALF]
    ahead, back = side_tables(kernel_rows(basis_vals, row_of, col_off))
    if not aligned:
        right = passed_along(head, "lon", -1)
        feat = jnp.pad(jnp.concatenate([feat, right], axis=1), ((0, 0), (0, extra - HALF)))
        observed = jnp.pad(observed, ((0, 0), (0, extra)))
    lat = jnp.broadcast_to(jnp.tile(lat_weight, HALF // LAT)[None, :], (8, HALF))
    cot, rims = forward(
        ne, nl, feat, tail, head, proj_weight, ahead, observed, lat, group, steps, share
    )

    if aligned:
        cot_left, cot_right = rims[0], rims[1]
    else:
        flat = cot.reshape(steps, rows, HALF)[:, :real].reshape(2 * blocks, O, HALF)
        flat = flat.transpose(1, 0, 2).reshape(O, blocks * BLK)[:, :cells]
        cot_left = passed_along(flat[:, cells - HALF :], "lon", 1)
        cot_right = passed_along(flat[:, :HALF], "lon", -1)
        flat = jnp.pad(
            jnp.concatenate([flat, cot_right], axis=1), ((0, 0), (0, extra - HALF))
        )
        flat = flat.reshape(O, 2 * blocks, HALF).transpose(1, 0, 2).reshape(steps, real, HALF)
        cot = jnp.pad(flat, ((0, 0), (0, rows - real), (0, 0))).reshape(steps * rows, HALF)
        cot_left = jnp.pad(cot_left, ((OP - O, 0), (0, 0)))
        cot_right = jnp.zeros((OP, HALF), BF16)
    grad, part = backward(
        cot, cot_left, cot_right, proj_weight, back, feat, group_back, steps_back, group, cells
    )
    scale = 1.0 / math.sqrt(ne * (cells // LAT) * nl * LAT)
    weight_grad = reduced(ne, nl, scale, part, chan)
    return (grad[:, :cells][None], weight_grad)


GROUP = 5
WIDE = GROUP * BLK
ROWS = GROUP * O
ROWS_P = ROWS + 8
MAIN = 64
LEFT = O - MAIN
SPLIT = GROUP * MAIN
TOPS = K * MAIN
USED = K * O + 8
LAG = 3
PART = 256
PARTS = 3


def ordered_weight(weight):
    rows = weight[...].astype(F32)
    parts = [rows[k * O : k * O + MAIN] for k in range(K)]
    parts += [rows[k * O + MAIN : (k + 1) * O] for k in range(K)]
    return jnp.concatenate(parts, axis=0)


def dot_lanes(left, right):
    return lax.dot_general(left, right, (((1,), (1,)), ((), ())), preferred_element_type=F32)


def table_columns(basis_vals, row_of, col_off):
    code = (col_off + R) * LAT + row_of
    ids = jnp.arange((2 * R + 1) * LAT, dtype=jnp.int32)
    hit = (code[:, :, None] == ids[None, None, :]).astype(F32)
    table = jnp.einsum("isk,isq->kqi", basis_vals, hit, precision=lax.Precision.HIGHEST)
    return table.astype(BF16)


def fused_kernel(
    n, nl, share, steps,
    feat, weight, table, obs, lat, grad, wout,
    wide, wrows, band, weight_t, lat_row, proj, sums, edge, first_edge, extra, edge_back,
    give, take, dec, recv, send, cot, seen, rim_left, rim_top, rim_low, spread, gout,
    wacc, wpart, wrecv, wmid, wfull,
    fsem, osem, hsend, hrecv, ssem1, rsem1, ssem2, rsem2, gsem,
    ws1, wr1, ws2, wr2, ws3, wr3,
):
    me = lax.axis_index("ens")
    at = lax.axis_index("lon")
    cells = steps * WIDE
    chan = feat.shape[0]
    own = pl.multiple_of(me * share, 16)
    after = {"lon": lax.rem(at + 1, nl)}
    before = {"lon": lax.rem(at + nl - 1, nl)}
    prow = PART // n

    def remote(src, dst, ssem, rsem, peer):
        return pltpu.make_async_remote_copy(
            src_ref=src, dst_ref=dst, send_sem=ssem, recv_sem=rsem, device_id=peer, device_id_type=MESH
        )

    def piece(c):
        if isinstance(c, int) and c == steps:
            return pltpu.make_async_copy(
                feat.at[:, pl.ds(0, HALF)], wide.at[:, pl.ds(HALF, HALF)], fsem.at[steps]
            )
        if isinstance(c, int) and c == steps - 1:
            lo, size = c * WIDE, WIDE - HALF
        else:
            lo, size = c * WIDE, WIDE
        return pltpu.make_async_copy(
            feat.at[:, pl.ds(pl.multiple_of(lo + HALF, HALF), size)],
            wide.at[:, pl.ds(pl.multiple_of(lo + 2 * HALF, HALF), size)],
            fsem.at[c],
        )

    def seen_copy(q, u):
        c = lax.rem(q + steps - 2, steps)
        t = jnp.minimum(me * (share // 8) + u, ROWS // 8 - 1)
        low = t // (SPLIT // 8)
        row = pl.multiple_of((1 - low) * (t % (MAIN // 8)) * 8 + low * MAIN, 8)
        block = (1 - low) * (t // (MAIN // 8)) + low * (ROWS // 8 - 1 - t)
        lane = pl.multiple_of(c * WIDE + block * BLK, BLK)
        return pltpu.make_async_copy(
            obs.at[pl.ds(row, 8), pl.ds(lane, BLK)], seen.at[q, pl.ds(u * 8, 8)], osem.at[q, u]
        )

    def first(q, off):
        peer = lax.rem(me + off, n)
        return remote(
            dec.at[q, pl.ds(pl.multiple_of(peer * share, 16), share)],
            recv.at[q, off], ssem1.at[q, off], rsem1.at[q, off], {"ens": peer},
        )

    def second(q, off):
        return remote(
            send.at[q, off], cot.at[q, pl.ds(own, share)],
            ssem2.at[q, off], rsem2.at[q, off], {"ens": lax.rem(me - off + n, n)},
        )

    def halo(slot):
        if slot == 0:
            src, dst, peer = give.at[0], take.at[0], after
        elif slot == 1:
            src, dst, peer = give.at[1], take.at[1], before
        elif slot == 2:
            src = cot.at[1, pl.ds(SPLIT - MAIN, MAIN + 16), pl.ds(HALF, HALF)]
            dst, peer = rim_left, after
        elif slot == 3:
            src, dst, peer = cot.at[2, pl.ds(0, MAIN), pl.ds(0, HALF)], rim_top, before
        else:
            src = cot.at[2, pl.ds(ROWS - LEFT, 16), pl.ds(0, HALF)]
            dst, peer = rim_low, before
        return remote(src, dst, hsend.at[slot], hrecv.at[slot], peer)

    def out_copy(t):
        return pltpu.make_async_copy(
            gout.at[lax.rem(t, 2)], grad.at[:, pl.ds(pl.multiple_of(t * WIDE, WIDE), WIDE)], gsem.at[t]
        )

    def scatter(j, off):
        peer = lax.rem(me + off, n)
        return remote(
            wpart.at[j, pl.ds(pl.multiple_of(peer * prow, 16), prow)], wrecv.at[j, off],
            ws1.at[j, off], wr1.at[j, off], {"ens": peer},
        )

    def across(j, off):
        return remote(
            wmid.at[j, at], wmid.at[j, at], ws2.at[j, off], wr2.at[j, off], {"lon": lax.rem(at + off, nl)}
        )

    def gather(j, off):
        mine = pl.ds(pl.multiple_of(me * prow, 16), prow)
        return remote(
            wfull.at[j, mine], wfull.at[j, mine], ws3.at[j, off], wr3.at[j, off],
            {"ens": lax.rem(me + off, n)},
        )

    def project_edges():
        start = (steps - 2) * WIDE
        lanes = jnp.concatenate(
            [wide[:, HALF:BLK], wide[:, cells : cells + HALF], wide[:, start : start + BLK]], axis=1
        )
        got = jnp.dot(wrows[...], lanes, preferred_element_type=F32)
        acc = jnp.zeros((3 * O, BLK), F32)
        out = jnp.zeros((O, BLK), F32)
        none = jnp.zeros((O, HALF), F32)
        for k in range(K):
            part = jnp.concatenate(
                [got[k * MAIN : (k + 1) * MAIN], got[TOPS + k * LEFT : TOPS + (k + 1) * LEFT]], axis=0
            )
            head = jnp.concatenate([none, part[:, :HALF]], axis=1)
            tail = jnp.concatenate([part[:, HALF:BLK], none], axis=1)
            lhs = jnp.concatenate([head, tail, part[:, BLK:]], axis=0).astype(BF16)
            acc = acc + jnp.dot(lhs, band[k, :BLK, :], preferred_element_type=F32)
            out = out + jnp.dot(head.astype(BF16), band[k, BLK:, :], preferred_element_type=F32)
        first_edge[...] = acc[:O]
        edge[...] = acc[2 * O :]
        give[0] = acc[O : 2 * O, :HALF]
        give[1] = out[:, HALF:]
        halo(0).start()
        halo(1).start()

    def forward_chunk(q):
        c = lax.rem(q + steps - 2, steps)
        got = jnp.dot(
            wrows[...],
            wide[:, pl.ds(pl.multiple_of(c * WIDE + BLK, BLK), WIDE)],
            preferred_element_type=F32,
        )
        gap = jnp.zeros((ROWS_P - ROWS, BLK), F32)
        tops = got[:TOPS].astype(BF16)
        for k in range(K):
            for g in range(GROUP):
                proj[k, g * MAIN : (g + 1) * MAIN, :] = tops[
                    k * MAIN : (k + 1) * MAIN, g * BLK : (g + 1) * BLK
                ]
            lows = [
                got[TOPS + k * LEFT : TOPS + (k + 1) * LEFT, g * BLK : (g + 1) * BLK]
                for g in reversed(range(GROUP))
            ]
            proj[k, SPLIT:, :] = jnp.concatenate(lows + [gap], axis=0).astype(BF16)
        def one_half(half, carry):
            acc = jnp.zeros((ROWS_P, BLK), F32)
            rows = pl.ds(pl.multiple_of(half * BLK, BLK), BLK)
            for k in range(K):
                acc = acc + jnp.dot(proj[k], band[k, rows, :], preferred_element_type=F32)
            sums[half] = acc
            return carry

        lax.fori_loop(0, 2, one_half, 0)

        @pl.when(q == 1)
        def _():
            halo(1).wait()
            extra[:, HALF:] = take[1]

        @pl.when(q == 2)
        def _():
            halo(0).wait()
            extra[...] = jnp.zeros_like(extra)
            edge[...] = first_edge[...]
            edge[:, :HALF] += take[0]

        last = SPLIT - MAIN
        dec[q, :last, :] = (
            jnp.concatenate([edge[:MAIN], sums[0, : last - MAIN]], axis=0) + sums[1, :last]
        ).astype(BF16)
        dec[q, last:SPLIT, :] = (
            sums[0, last - MAIN : last] + sums[1, last:SPLIT] + extra[:MAIN]
        ).astype(BF16)
        lows = jnp.concatenate([sums[0, SPLIT + LEFT : ROWS], edge[MAIN:]], axis=0) + sums[1, SPLIT:ROWS]
        lows = [lows[:LEFT] + extra[MAIN:], lows[LEFT:]]
        rest = jnp.zeros((n * share - ROWS, BLK), F32)
        dec[q, SPLIT:, :] = jnp.concatenate(lows + [rest], axis=0).astype(BF16)
        edge[...] = sums[0, last : SPLIT + LEFT]
        for off in range(1, n):
            first(q, off).start()

    def smooth(diff):
        return diff * lax.rsqrt(diff * diff + SMOOTH * SMOOTH)

    def slopes(q):
        for u in range(share // 8):
            seen_copy(q, u).wait()
        for off in range(1, n):
            first(q, off).wait_recv()

        def one(step, carry):
            row = pl.multiple_of(lax.div(step, 2) * 16, 16)
            lanes = pl.ds(pl.multiple_of(lax.rem(step, 2) * HALF, HALF), HALF)
            here = pl.ds(pl.multiple_of(own + row, 16), 16)
            values = [dec[q, here, lanes].astype(F32)]
            values += [recv[q, off, pl.ds(row, 16), lanes].astype(F32) for off in range(1, n)]
            sums = [None] * n
            for a in range(n):
                for b in range(a + 1, n):
                    pair = smooth(values[a] - values[b])
                    sums[a] = pair if sums[a] is None else sums[a] + pair
                    sums[b] = -pair if sums[b] is None else sums[b] - pair
            target = seen[q, pl.ds(row, 16), lanes]
            area = jnp.broadcast_to(lat_row[0:1, lanes], (16, HALF))
            for a in range(n):
                slope = smooth(values[a] - target) - sums[a] * (1.0 / (n - 1))
                result = (slope * area).astype(BF16)
                if a == 0:
                    cot[q, here, lanes] = result
                else:
                    send[q, a, pl.ds(row, 16), lanes] = result
            return carry

        lax.fori_loop(0, share // 16 * 2, one, 0)
        for off in range(1, n):
            second(q, off).start()

    def store_lows(lows, lanes):
        both = jnp.concatenate(lows + [jnp.zeros((USED - K * O, BLK), F32)], axis=0)
        spread[TOPS:USED, lanes] = both.astype(BF16)

    def backward_chunk(b):
        q = lax.rem(b + 2, steps)
        lhs = cot[q, pl.ds(0, ROWS_P), :]
        lows = [[] for _ in range(GROUP)]
        for k in range(K):
            ahead = dot_lanes(lhs, band[k, BLK:, :])
            here = dot_lanes(lhs, band[k, :BLK, :])
            for g in range(GROUP):
                low = SPLIT + (GROUP - 1 - g) * LEFT
                top = edge_back[k, :MAIN] if g == 0 else ahead[(g - 1) * MAIN : g * MAIN]
                end = edge_back[k, MAIN:] if g == 0 else ahead[low + LEFT : low + 2 * LEFT]
                lanes = pl.ds(pl.multiple_of(b * WIDE + g * BLK, BLK), BLK)
                spread[k * MAIN : (k + 1) * MAIN, lanes] = (
                    here[g * MAIN : (g + 1) * MAIN] + top
                ).astype(BF16)
                lows[g].append(here[low : low + LEFT] + end)
            edge_back[k] = ahead[SPLIT - MAIN : SPLIT + LEFT]
        for g in range(GROUP):
            store_lows(lows[g], pl.ds(pl.multiple_of(b * WIDE + g * BLK, BLK), BLK))

    def add_weight(lanes):
        wacc[:, : K * O] += lax.dot_general(
            wide[:, lanes], spread[: K * O, lanes], (((1,), (1,)), ((), ())), preferred_element_type=F32
        )

    def one_grad(t, carry):
        @pl.when(t >= 2)
        def _():
            out_copy(t - 2).wait()

        lanes = pl.ds(pl.multiple_of(t * WIDE + HALF, HALF), WIDE)
        gout[lax.rem(t, 2)] = jnp.dot(
            weight_t[:, :USED], spread[:, lanes], preferred_element_type=F32
        ).astype(BF16)
        out_copy(t).start()
        return carry

    def after_scatter(j):
        for off in range(1, n):
            scatter(j, off).wait_recv()
        total = wpart[j, pl.ds(pl.multiple_of(me * prow, 16), prow), :].astype(F32)
        for off in range(1, n):
            total = total + wrecv[j, off].astype(F32)
        wmid[j, at] = total.astype(BF16)
        for off in range(1, nl):
            across(j, off).start()

    def after_across(j):
        for off in range(1, nl):
            across(j, off).wait_recv()
        total = wmid[j, 0].astype(F32)
        for z in range(1, nl):
            total = total + wmid[j, z].astype(F32)
        wfull[j, pl.ds(pl.multiple_of(me * prow, 16), prow), :] = total.astype(BF16)
        for off in range(1, n):
            gather(j, off).start()

    for c in [steps - 1, steps, steps - 3, steps - 2]:
        piece(c).start()
    for c in range(steps - 3):
        piece(c).start()

    def look(q, carry):
        for u in range(share // 8):
            seen_copy(q, u).start()
        return carry

    lax.fori_loop(0, steps, look, 0)
    peers = [{"ens": lax.rem(me + off, n)} for off in range(1, n)]
    peers += [{"lon": lax.rem(at + off, nl)} for off in range(1, nl)]
    barrier = pltpu.get_barrier_semaphore()
    for peer in peers:
        pl.semaphore_signal(barrier, inc=1, device_id=peer, device_id_type=MESH)
    build_band(table, band)
    lane = lax.broadcasted_iota(jnp.int32, (LAT, BLK), 1)
    ones = (lane % LAT == lax.broadcasted_iota(jnp.int32, (LAT, BLK), 0)).astype(F32)
    lat_row[...] = jnp.dot(
        jnp.broadcast_to(lat[...], (8, LAT)), ones, precision=lax.Precision.HIGHEST,
        preferred_element_type=F32,
    )
    wrows[...] = ordered_weight(weight).astype(BF16)
    wide[:, :HALF] = jnp.zeros((chan, HALF), BF16)
    wide[:, cells + HALF :] = jnp.zeros((chan, HALF), BF16)
    extra[...] = jnp.zeros_like(extra)
    for c in [steps - 1, steps, steps - 3, steps - 2]:
        piece(c).wait()
    pl.semaphore_wait(barrier, len(peers))
    project_edges()

    def step(s, carry):
        @pl.when(jnp.logical_and(s >= 2, s < steps - 1))
        def _():
            piece(s - 2).wait()

        @pl.when(s < steps)
        def _():
            forward_chunk(s)

        @pl.when(s >= LAG)
        def _():
            slopes(s - LAG)

        return carry

    lax.fori_loop(0, steps, step, 0)
    for q in (1, 2, 0):
        for off in range(1, n):
            second(q, off).wait_recv()
        if q == 1:
            halo(2).start()
        if q == 2:
            halo(3).start()
            halo(4).start()
    gap = jnp.zeros((PARTS * PART - K * O, chan), F32)
    rows = jnp.concatenate([ordered_weight(weight), gap], axis=0)
    weight_t[...] = rows.T.astype(BF16)
    wacc[...] = jnp.zeros_like(wacc)
    halo(2).wait()
    for k in range(K):
        got = dot_lanes(rim_left[...], band[k, BLK:, HALF:])
        edge_back[k] = got[:O]

    def step_back(b, carry):
        @pl.when(b < LAG)
        def _():
            slopes(steps - LAG + b)

        @pl.when(jnp.logical_and(b >= 1, b < steps - 2))
        def _():
            for off in range(1, n):
                second(b + 2, off).wait_recv()

        backward_chunk(b)

        @pl.when(b % 2 == 1)
        def _():
            add_weight(pl.ds(pl.multiple_of((b - 1) * WIDE, WIDE), 2 * WIDE))

        return carry

    lax.fori_loop(0, steps, step_back, 0)
    halo(3).wait()
    halo(4).wait()
    rim = jnp.concatenate([rim_top[...].astype(F32), rim_low[...].astype(F32)], axis=0).astype(BF16)
    lows = []
    for k in range(K):
        got = dot_lanes(rim, band[k, :BLK, :HALF])
        both = got[:O] + edge_back[k]
        spread[k * MAIN : (k + 1) * MAIN, cells : cells + BLK] = both[:MAIN].astype(BF16)
        lows.append(both[MAIN:])
    store_lows(lows, slice(cells, cells + BLK))
    rest = steps % 2 * WIDE
    add_weight(pl.ds(cells - rest, rest + BLK))

    def one_part(j, carry):
        wpart[j] = wacc[:, pl.ds(pl.multiple_of(j * PART, PART), PART)].T.astype(BF16)
        for off in range(1, n):
            scatter(j, off).start()
        return carry

    lax.fori_loop(0, PARTS, one_part, 0)

    def late(t, carry):
        one_grad(t, 0)

        @pl.when(jnp.logical_and(t >= 2, t < 2 + PARTS))
        def _():
            after_scatter(t - 2)

        @pl.when(jnp.logical_and(t >= 4, t < 4 + PARTS))
        def _():
            after_across(t - 4)

        return carry

    lax.fori_loop(0, steps, late, 0)
    for j in range(PARTS):
        for off in range(1, n):
            gather(j, off).wait_recv()

    def drain(q, carry):
        for off in range(1, n):
            first(q, off).wait_send()
            second(q, off).wait_send()
        return carry

    rows = [wfull[j].astype(F32) for j in range(PARTS)]
    rows = jnp.concatenate(rows, axis=0)
    parts = []
    for k in range(K):
        parts += [rows[k * MAIN : (k + 1) * MAIN], rows[TOPS + k * LEFT : TOPS + (k + 1) * LEFT]]
    wout[...] = jnp.concatenate(parts, axis=0).astype(BF16)
    lax.fori_loop(0, steps, drain, 0)
    for j in range(PARTS):
        for off in range(1, n):
            scatter(j, off).wait_send()
            gather(j, off).wait_send()
        for off in range(1, nl):
            across(j, off).wait_send()
    out_copy(steps - 2).wait()
    out_copy(steps - 1).wait()


def fused(n, nl, feat, weight, table, obs, lat, share):
    chan, cells = feat.shape
    steps = cells // WIDE
    vmem = pl.BlockSpec(memory_space=pltpu.VMEM)
    anywhere = pl.BlockSpec(memory_space=pl.ANY)
    dma = pltpu.SemaphoreType.DMA
    prow = PART // n
    return pl.pallas_call(
        functools.partial(fused_kernel, n, nl, share, steps),
        out_shape=(
            jax.ShapeDtypeStruct((chan, cells), BF16),
            jax.ShapeDtypeStruct((K * O, chan), BF16),
        ),
        in_specs=[anywhere, vmem, vmem, anywhere, vmem],
        out_specs=(anywhere, vmem),
        scratch_shapes=[
            pltpu.VMEM((chan, cells + BLK), BF16),
            pltpu.VMEM((K * O, chan), BF16),
            pltpu.VMEM((K, 2 * BLK, BLK), BF16),
            pltpu.VMEM((chan, PARTS * PART), BF16),
            pltpu.VMEM((8, BLK), F32),
            pltpu.VMEM((K, ROWS_P, BLK), BF16),
            pltpu.VMEM((2, ROWS_P, BLK), F32),
            pltpu.VMEM((O, BLK), F32),
            pltpu.VMEM((O, BLK), F32),
            pltpu.VMEM((O, BLK), F32),
            pltpu.VMEM((K, O, BLK), F32),
            pltpu.VMEM((2, O, HALF), F32),
            pltpu.VMEM((2, O, HALF), F32),
            pltpu.VMEM((steps, n * share, BLK), BF16),
            pltpu.VMEM((steps, n, share, BLK), BF16),
            pltpu.VMEM((steps, n, share, BLK), BF16),
            pltpu.VMEM((steps, n * share, BLK), BF16),
            pltpu.VMEM((steps, share, BLK), F32),
            pltpu.VMEM((MAIN + 16, HALF), BF16),
            pltpu.VMEM((MAIN, HALF), BF16),
            pltpu.VMEM((16, HALF), BF16),
            pltpu.VMEM((USED, cells + BLK), BF16),
            pltpu.VMEM((2, chan, WIDE), BF16),
            pltpu.VMEM((chan, PARTS * PART), F32),
            pltpu.VMEM((PARTS, PART, chan), BF16),
            pltpu.VMEM((PARTS, n, prow, chan), BF16),
            pltpu.VMEM((PARTS, nl, prow, chan), BF16),
            pltpu.VMEM((PARTS, PART, chan), BF16),
            dma((steps + 1,)),
            dma((steps, share // 8)),
            dma((5,)),
            dma((5,)),
            dma((steps, n)),
            dma((steps, n)),
            dma((steps, n)),
            dma((steps, n)),
            dma((steps,)),
            dma((PARTS, n)),
            dma((PARTS, n)),
            dma((PARTS, nl)),
            dma((PARTS, nl)),
            dma((PARTS, n)),
            dma((PARTS, n)),
        ],
        compiler_params=pltpu.CompilerParams(
            collective_id=2, has_side_effects=True, vmem_limit_bytes=VMEM_LIMIT
        ),
        name="fused_decoder",
    )(feat, weight, table, obs, lat)


def write_kernel(scale, grad, part, out, wout):
    out[...] = grad[...]

    @pl.when(pl.program_id(0) == 0)
    def _():
        wout[...] = part[...].astype(F32) * scale


def written(grad, part, scale, size):
    chan, cells = grad.shape
    block = pl.BlockSpec((size, cells), lambda s: (s, 0))
    return pl.pallas_call(
        functools.partial(write_kernel, scale),
        out_shape=(
            jax.ShapeDtypeStruct(grad.shape, BF16),
            jax.ShapeDtypeStruct(part.shape, F32),
        ),
        grid=(chan // size,),
        in_specs=[block, whole(part.shape)],
        out_specs=(block, whole(part.shape)),
        compiler_params=pltpu.CompilerParams(vmem_limit_bytes=VMEM_LIMIT),
        name="write_results",
    )(grad, part)


def fused_shards(features, proj_weight, basis_vals, row_of, col_off, observed, lat_weight):
    ne = lax.axis_size("ens")
    nl = lax.axis_size("lon")
    feat = features[0]
    chan, cells = feat.shape
    share = pl.cdiv(pl.cdiv(ROWS, ne), 16) * 16
    table = table_columns(basis_vals, row_of, col_off)
    grad, part = fused(
        ne, nl, feat, proj_weight, table, observed, lat_weight.reshape(1, LAT), share
    )
    scale = 1.0 / math.sqrt(ne * (cells // LAT) * nl * LAT)
    grad, weight_grad = written(grad, part, scale, 96)
    return (grad[None], weight_grad)


def shards(*args):
    cells = args[0].shape[2]
    sizes = (lax.axis_size("ens"), lax.axis_size("lon"))
    if cells % WIDE == 0 and cells // WIDE >= 8 and PART % (16 * sizes[0]) == 0 and sizes[1] > 1:
        return fused_shards(*args)
    return split_shards(*args)


def solution(mesh):
    in_specs = (P("ens", None, "lon"), P(), P(), P(), P(), P(None, "lon"), P())
    out_specs = (P("ens", None, "lon"), P())
    return jax.shard_map(shards, mesh=mesh, in_specs=in_specs, out_specs=out_specs, check_vma=False)
```

```python
import functools
import math

import jax
import jax.numpy as jnp
from jax import lax
from jax.experimental import pallas as pl
from jax.experimental.pallas import tpu as pltpu
from jax.sharding import PartitionSpec as P

O = 72
OP = 80
K = 9
R = 4
LAT = 32
SMOOTH = 0.25
BLK = 256
HALF = 128
F32 = jnp.float32
BF16 = jnp.bfloat16
MESH = pl.DeviceIdType.MESH
VMEM_LIMIT = 60 * 1024 * 1024


def whole(shape):
    return pl.BlockSpec(shape, lambda s: (0,) * len(shape))


def kernel_rows(basis_vals, row_of, col_off):
    code = (col_off + R) * LAT + row_of
    ids = jnp.arange((2 * R + 1) * LAT, dtype=jnp.int32)
    hit = (code[:, :, None] == ids[None, None, :]).astype(F32)
    table = jnp.einsum("isk,isq->ikq", basis_vals, hit, precision=lax.Precision.HIGHEST)
    return table.astype(BF16)


def side_tables(table):
    taps = 2 * R + 1
    four = table.reshape(LAT, K, taps, LAT)
    ahead = four.transpose(1, 2, 3, 0).reshape(K, taps * LAT, LAT)
    back = four[:, :, ::-1].transpose(1, 2, 0, 3).reshape(K, taps * LAT, LAT)
    return ahead, back


def build_band(table, band):
    lane = lax.broadcasted_iota(jnp.int32, (LAT, BLK), 1)
    spread_lanes = (lane % LAT == lax.broadcasted_iota(jnp.int32, (LAT, BLK), 0)).astype(F32)
    spread_lanes = spread_lanes.astype(BF16)
    place = lane // LAT
    cols = BLK // LAT

    def one(k, carry):
        tiled = jnp.dot(table[k], spread_lanes, preferred_element_type=F32)
        for e in range(2 * cols):
            block = jnp.zeros((LAT, BLK), F32)
            for j in range(cols):
                d = e - j
                if 0 <= d <= 2 * R:
                    block = jnp.where(place == j, tiled[d * LAT : (d + 1) * LAT], block)
            band[k, e * LAT : (e + 1) * LAT, :] = block.astype(BF16)
        return carry

    lax.fori_loop(0, K, one, 0)


def build_band_rows(table, band):
    lane = lax.broadcasted_iota(jnp.int32, (LAT, BLK), 1)
    spread_lanes = (lane % LAT == lax.broadcasted_iota(jnp.int32, (LAT, BLK), 0)).astype(F32)
    spread_lanes = spread_lanes.astype(BF16)
    place = lane // LAT
    cols = BLK // LAT

    def one(k, carry):
        tiled = lax.dot_general(
            table[k], spread_lanes, (((0,), (0,)), ((), ())), preferred_element_type=F32
        )
        for e in range(2 * cols):
            block = jnp.zeros((LAT, BLK), F32)
            for j in range(cols):
                d = e - j
                if 0 <= d <= 2 * R:
                    block = jnp.where(place == j, tiled[d * LAT : (d + 1) * LAT], block)
            band[k, e * LAT : (e + 1) * LAT, :] = block.astype(BF16)
        return carry

    lax.fori_loop(0, K, one, 0)


def padded_weight(weight):
    wide = weight[...].astype(F32)
    gap = jnp.zeros((OP - O, wide.shape[1]), F32)
    rows = []
    for k in range(K):
        rows += [wide[k * O : (k + 1) * O], gap]
    return jnp.concatenate(rows, axis=0)


def greet(peers):
    barrier = pltpu.get_barrier_semaphore()
    for peer in peers:
        pl.semaphore_signal(barrier, inc=1, device_id=peer, device_id_type=MESH)
    pl.semaphore_wait(barrier, len(peers))


def forward_kernel(
    n, nl, group, steps, share,
    feat, tail, head, weight, table, obs, lat, out, rims,
    wpad, band, proj, dec, flat, recv, send, cot, left, right, rim_left, rim_right,
    ssem1, rsem1, ssem2, rsem2, hsend, hrecv,
):
    s = pl.program_id(0)
    me = lax.axis_index("ens")
    real = group * 2 * O
    own = pl.multiple_of(me * share, 16)
    after = {"lon": lax.rem(lax.axis_index("lon") + 1, nl)}
    before = {"lon": lax.rem(lax.axis_index("lon") + nl - 1, nl)}

    def rim(src, dst, slot, peer):
        return pltpu.make_async_remote_copy(
            src_ref=src,
            dst_ref=dst,
            send_sem=hsend.at[slot],
            recv_sem=hrecv.at[slot],
            device_id=peer,
            device_id_type=MESH,
        )

    def first(q, off):
        peer = lax.rem(me + off, n)
        return pltpu.make_async_remote_copy(
            src_ref=dec.at[q, pl.ds(pl.multiple_of(peer * share, 16), share)],
            dst_ref=recv.at[q, off],
            send_sem=ssem1.at[q, off],
            recv_sem=rsem1.at[q, off],
            device_id={"ens": peer},
            device_id_type=MESH,
        )

    def second(q, off):
        return pltpu.make_async_remote_copy(
            src_ref=send.at[q, off],
            dst_ref=cot.at[q, pl.ds(own, share)],
            send_sem=ssem2.at[q, off],
            recv_sem=rsem2.at[q, off],
            device_id={"ens": lax.rem(me - off + n, n)},
            device_id_type=MESH,
        )

    def put(values, h, lo):
        for k in range(K):
            proj[k, h, :, lo : lo + HALF] = values[k * OP : (k + 1) * OP].astype(BF16)

    @pl.when(s == 0)
    def _():
        greet([{"ens": lax.rem(me + off, n)} for off in range(1, n)] + [after, before])
        rim(tail, left, 0, after).start()
        rim(head, right, 1, before).start()
        wpad[...] = padded_weight(weight).astype(BF16)
        build_band(table, band)
        if n * share > real:
            for q in range(steps):
                dec[q, real:, :] = jnp.zeros((n * share - real, HALF), BF16)
            flat[real:, :] = jnp.zeros((n * share - real, HALF), F32)

    @pl.when(s < steps)
    def _():
        def one(b, carry):
            lanes = pl.ds(pl.multiple_of(b * BLK, BLK), BLK)
            got = jnp.dot(wpad[...], feat[:, lanes], preferred_element_type=F32)
            h = s * group + b
            put(got[:, :HALF], h, HALF)
            put(got[:, HALF:], h + 1, 0)
            return carry

        lax.fori_loop(0, group, one, 0)

    @pl.when(s == 1)
    def _():
        rim(tail, left, 0, after).wait()
        put(jnp.dot(wpad[...], left[...], preferred_element_type=F32), 0, 0)

    @pl.when(s == steps)
    def _():
        rim(head, right, 1, before).wait()
        put(jnp.dot(wpad[...], right[...], preferred_element_type=F32), steps * group, HALF)

    @pl.when(jnp.logical_and(s > 0, s <= steps))
    def _():
        q = s - 1
        g0 = q * group
        acc = jnp.zeros((group * OP, BLK), F32)
        for k in range(K):
            for part in range(2):
                lhs = proj[k, pl.ds(g0 + part, group)].reshape(group * OP, BLK)
                acc = acc + jnp.dot(
                    lhs, band[k, part * BLK : (part + 1) * BLK, :], preferred_element_type=F32
                )
        for g in range(group):
            piece = acc[g * OP : g * OP + O]
            both = jnp.concatenate([piece[:, :HALF], piece[:, HALF:]], axis=0)
            dec[q, g * 2 * O : (g + 1) * 2 * O, :] = both.astype(BF16)
        for off in range(1, n):
            first(q, off).start()

    @pl.when(s > 1)
    def _():
        q = s - 2
        for t in range(2 * group):
            flat[t * O : (t + 1) * O, :] = obs[:, t * HALF : (t + 1) * HALF]
        for off in range(1, n):
            first(q, off).wait_recv()
        lat_row = jnp.broadcast_to(lat[0:1, :], (16, HALF))

        def smooth(diff):
            return diff * lax.rsqrt(diff * diff + SMOOTH * SMOOTH)

        def one(step, carry):
            at = pl.multiple_of(step * 16, 16)
            here = pl.ds(pl.multiple_of(own + at, 16), 16)
            values = [dec[q, here, :].astype(F32)]
            values += [recv[q, off, pl.ds(at, 16), :].astype(F32) for off in range(1, n)]
            sums = [None] * n
            for a in range(n):
                for b in range(a + 1, n):
                    pair = smooth(values[a] - values[b])
                    sums[a] = pair if sums[a] is None else sums[a] + pair
                    sums[b] = -pair if sums[b] is None else sums[b] - pair
            target = flat[here, :]
            for a in range(n):
                slope = smooth(values[a] - target) - sums[a] * (1.0 / (n - 1))
                result = (slope * lat_row).astype(BF16)
                if a == 0:
                    cot[q, here, :] = result
                else:
                    send[q, a, pl.ds(at, 16), :] = result
            return carry

        lax.fori_loop(0, share // 16, one, 0)
        for off in range(1, n):
            second(q, off).start()

    @pl.when(s == steps + 1)
    def _():
        for q in range(steps):
            for off in range(1, n):
                first(q, off).wait_send()
                second(q, off).wait()
        last = rim(cot.at[steps - 1, pl.ds(real - OP, OP)], rim_left, 2, after)
        opening = rim(cot.at[0, pl.ds(0, OP)], rim_right, 3, before)
        last.start()
        opening.start()
        for q in range(steps):
            out[q * n * share : (q + 1) * n * share, :] = cot[q]
        last.wait()
        opening.wait()
        rims[0] = rim_left[...]
        rims[1] = rim_right[...]


def forward(n, nl, feat, tail, head, weight, table, obs, lat, group, steps, share):
    chan = feat.shape[0]
    wide = group * BLK
    rows = n * share
    sem = pltpu.SemaphoreType.DMA((steps, n))
    return pl.pallas_call(
        functools.partial(forward_kernel, n, nl, group, steps, share),
        out_shape=(
            jax.ShapeDtypeStruct((steps * rows, HALF), BF16),
            jax.ShapeDtypeStruct((2, OP, HALF), BF16),
        ),
        grid=(steps + 2,),
        in_specs=[
            pl.BlockSpec((chan, wide), lambda s: (0, jnp.minimum(s, steps - 1))),
            whole(tail.shape),
            whole(head.shape),
            whole(weight.shape),
            whole(table.shape),
            pl.BlockSpec((O, wide), lambda s: (0, jnp.clip(s - 2, 0, steps - 1))),
            whole(lat.shape),
        ],
        out_specs=(whole((steps * rows, HALF)), whole((2, OP, HALF))),
        scratch_shapes=[
            pltpu.VMEM((K * OP, chan), BF16),
            pltpu.VMEM((K, 2 * BLK, BLK), BF16),
            pltpu.VMEM((K, steps * group + 1, OP, BLK), BF16),
            pltpu.VMEM((steps, rows, HALF), BF16),
            pltpu.VMEM((rows, HALF), F32),
            pltpu.VMEM((steps, n, share, HALF), BF16),
            pltpu.VMEM((steps, n, share, HALF), BF16),
            pltpu.VMEM((steps, rows, HALF), BF16),
            pltpu.VMEM((chan, HALF), BF16),
            pltpu.VMEM((chan, HALF), BF16),
            pltpu.VMEM((OP, HALF), BF16),
            pltpu.VMEM((OP, HALF), BF16),
            sem,
            sem,
            sem,
            sem,
            pltpu.SemaphoreType.DMA((4,)),
            pltpu.SemaphoreType.DMA((4,)),
        ],
        compiler_params=pltpu.CompilerParams(
            collective_id=0, has_side_effects=True, vmem_limit_bytes=VMEM_LIMIT
        ),
        name="forward_slopes",
    )(feat, tail, head, weight, table, obs, lat)


WG_ROWS = 2048
WG_PART = 656


def backward_kernel(
    group, steps, piece, share, cells, padded,
    cot, left, right, weight, table, feat, grad, wgrad,
    weight_t, band, ext, spread, acc,
):
    s = pl.program_id(0)
    blocks = steps * group

    @pl.when(s == 0)
    def _():
        ext[:, O:, :] = jnp.zeros((blocks + 1, OP - O, BLK), BF16)
        ext[0, :O, :HALF] = left[...].astype(F32)[OP - O :].astype(BF16)
        ext[blocks, :O, HALF:] = right[:O]

        weight_t[...] = padded_weight(weight).T.astype(BF16)
        build_band(table, band)

        def one(b, carry):
            start = lax.div(b, piece) * share + lax.rem(b, piece) * (2 * O)
            pair = cot[pl.ds(pl.multiple_of(start, 16), 2 * O), :].astype(F32)
            ext[b, :O, HALF:] = pair[:O].astype(BF16)
            ext[b + 1, :O, :HALF] = pair[O:].astype(BF16)
            return carry

        lax.fori_loop(0, blocks, one, 0)
        acc[...] = jnp.zeros_like(acc)

    g0 = s * group
    for k in range(K):
        got = jnp.zeros((group * OP, BLK), F32)
        for part in range(2):
            lhs = ext[pl.ds(g0 + part, group)].reshape(group * OP, BLK)
            got = got + jnp.dot(
                lhs, band[k, part * BLK : (part + 1) * BLK, :], preferred_element_type=F32
            )
        if padded:
            row = lax.broadcasted_iota(jnp.int32, got.shape, 0) // OP
            lane = lax.broadcasted_iota(jnp.int32, got.shape, 1)
            got = jnp.where((g0 + row) * BLK + lane < cells, got, 0.0)
        got = got.astype(BF16)
        for g in range(group):
            spread[k * OP : (k + 1) * OP, g * BLK : (g + 1) * BLK] = got[g * OP : (g + 1) * OP]

    acc[...] += lax.dot_general(
        spread[...], feat[...], (((1,), (1,)), ((), ())), preferred_element_type=F32
    )

    def one_grad(n, carry):
        lanes = pl.ds(pl.multiple_of(n * BLK, BLK), BLK)
        grad[:, lanes] = jnp.dot(
            weight_t[...], spread[:, lanes], preferred_element_type=F32
        ).astype(BF16)
        return carry

    lax.fori_loop(0, group, one_grad, 0)

    @pl.when(s == steps - 1)
    def _():
        parts = acc.shape[1] // HALF
        wgrad[parts * WG_PART - 16 :, :] = jnp.zeros((WG_ROWS - parts * WG_PART + 16, HALF), BF16)
        for t in range(parts):
            rows = [
                acc[k * OP : k * OP + O, t * HALF : (t + 1) * HALF] for k in range(K)
            ] + [jnp.zeros((8, HALF), F32)]
            wgrad[t * WG_PART : (t + 1) * WG_PART, :] = jnp.concatenate(rows, axis=0).astype(BF16)


def backward(cot, left, right, weight, table, feat, group, steps, piece, cells):
    chan = feat.shape[0]
    wide = group * BLK
    blocks = steps * group
    return pl.pallas_call(
        functools.partial(
            backward_kernel,
            group,
            steps,
            piece,
            cot.shape[0] * piece // blocks,
            cells,
            cells != blocks * BLK,
        ),
        out_shape=(
            jax.ShapeDtypeStruct(feat.shape, BF16),
            jax.ShapeDtypeStruct((WG_ROWS, HALF), BF16),
        ),
        grid=(steps,),
        in_specs=[
            whole(cot.shape),
            whole(left.shape),
            whole(right.shape),
            whole(weight.shape),
            whole(table.shape),
            pl.BlockSpec((chan, wide), lambda s: (0, s)),
        ],
        out_specs=(pl.BlockSpec((chan, wide), lambda s: (0, s)), whole((WG_ROWS, HALF))),
        scratch_shapes=[
            pltpu.VMEM((chan, K * OP), BF16),
            pltpu.VMEM((K, 2 * BLK, BLK), BF16),
            pltpu.VMEM((blocks + 1, OP, BLK), BF16),
            pltpu.VMEM((K * OP, wide), BF16),
            pltpu.VMEM((K * OP, chan), F32),
        ],
        compiler_params=pltpu.CompilerParams(vmem_limit_bytes=VMEM_LIMIT),
        name="backward_conv",
    )(cot, left, right, weight, table, feat)


def reduce_kernel(ne, nl, scale, part, out, recv1, mid, recv2, got, *sems):
    (ss1, rs1, ss2, rs2, ss3, rs3, ss4, rs4) = sems
    me = lax.axis_index("ens")
    at = lax.axis_index("lon")
    rows = WG_ROWS // ne
    small = rows // nl
    ens_peers = [{"ens": lax.rem(me + off, ne)} for off in range(1, ne)]
    lon_peers = [{"lon": lax.rem(at + off, nl)} for off in range(1, nl)]
    greet(ens_peers + lon_peers)

    def run(copies):
        for copy in copies:
            copy.start()
        for copy in copies:
            copy.wait()

    def send(src, dst, ssem, rsem, peer):
        return pltpu.make_async_remote_copy(
            src_ref=src, dst_ref=dst, send_sem=ssem, recv_sem=rsem, device_id=peer, device_id_type=MESH
        )

    own = pl.multiple_of(me * rows, 16)
    mine = pl.multiple_of(at * small, 8)
    run(
        [
            send(
                part.at[pl.ds(pl.multiple_of(lax.rem(me + off, ne) * rows, 16), rows)],
                recv1.at[off],
                ss1.at[off],
                rs1.at[off],
                {"ens": lax.rem(me + off, ne)},
            )
            for off in range(1, ne)
        ]
    )
    total = part[pl.ds(own, rows), :].astype(F32)
    for off in range(1, ne):
        total = total + recv1[off].astype(F32)
    mid[...] = total
    run(
        [
            send(
                mid.at[pl.ds(pl.multiple_of(lax.rem(at + off, nl) * small, 8), small)],
                recv2.at[off],
                ss2.at[off],
                rs2.at[off],
                {"lon": lax.rem(at + off, nl)},
            )
            for off in range(1, nl)
        ]
    )
    total = mid[pl.ds(mine, small), :]
    for off in range(1, nl):
        total = total + recv2[off]
    recv2[0] = total
    gat = got[1]
    gat[pl.ds(mine, small), :] = total
    run(
        [
            send(
                recv2.at[0],
                gat.at[pl.ds(mine, small)],
                ss3.at[off],
                rs3.at[off],
                {"lon": lax.rem(at + off, nl)},
            )
            for off in range(1, nl)
        ]
    )
    full = got[0]
    full[pl.ds(own, rows), :] = gat[...].astype(BF16)
    run(
        [
            send(
                full.at[pl.ds(own, rows)],
                full.at[pl.ds(own, rows)],
                ss4.at[off],
                rs4.at[off],
                {"ens": lax.rem(me + off, ne)},
            )
            for off in range(1, ne)
        ]
    )
    for t in range(out.shape[1] // HALF):
        piece = full[t * WG_PART : (t + 1) * WG_PART, :].astype(F32) * scale
        out[:, t * HALF : (t + 1) * HALF] = piece[: K * O]


def reduced(ne, nl, scale, part, chan):
    vmem = pl.BlockSpec(memory_space=pltpu.VMEM)
    rows = WG_ROWS // ne
    small = rows // nl

    def body(part, out, recv1, mid, recv2, full, gat, *sems):
        reduce_kernel(ne, nl, scale, part, out, recv1, mid, recv2, (full, gat), *sems)

    return pl.pallas_call(
        body,
        out_shape=jax.ShapeDtypeStruct((K * O, chan), F32),
        in_specs=[vmem],
        out_specs=vmem,
        scratch_shapes=[
            pltpu.VMEM((ne, rows, HALF), BF16),
            pltpu.VMEM((rows, HALF), F32),
            pltpu.VMEM((nl, small, HALF), F32),
            pltpu.VMEM((WG_ROWS, HALF), BF16),
            pltpu.VMEM((rows, HALF), F32),
        ]
        + [pltpu.SemaphoreType.DMA((n,)) for n in (ne, ne, nl, nl, nl, nl, ne, ne)],
        compiler_params=pltpu.CompilerParams(
            collective_id=1, has_side_effects=True, vmem_limit_bytes=VMEM_LIMIT
        ),
        name="weight_reduce",
    )(part)


def passed_along(value, axis, steps):
    count = lax.axis_size(axis)
    return lax.ppermute(value, axis, [(i, (i + steps) % count) for i in range(count)])


def split_shards(features, proj_weight, basis_vals, row_of, col_off, observed, lat_weight):
    ne = lax.axis_size("ens")
    nl = lax.axis_size("lon")
    assert features.shape[0] == 1
    feat = features[0]
    chan, cells = feat.shape
    aligned = cells % BLK == 0
    blocks = cells // BLK if aligned else pl.cdiv(cells + HALF, BLK)
    group_back = max(g for g in range(1, 10) if blocks % g == 0)
    steps_back = blocks // group_back
    group = max(g for g in range(1, 7) if blocks % g == 0)
    steps = blocks // group
    real = group * 2 * O
    share = pl.cdiv(pl.cdiv(real, ne), 16) * 16
    rows = ne * share
    extra = blocks * BLK - cells

    tail = feat[:, cells - HALF :]
    head = feat[:, :HALF]
    ahead, back = side_tables(kernel_rows(basis_vals, row_of, col_off))
    if not aligned:
        right = passed_along(head, "lon", -1)
        feat = jnp.pad(jnp.concatenate([feat, right], axis=1), ((0, 0), (0, extra - HALF)))
        observed = jnp.pad(observed, ((0, 0), (0, extra)))
    lat = jnp.broadcast_to(jnp.tile(lat_weight, HALF // LAT)[None, :], (8, HALF))
    cot, rims = forward(
        ne, nl, feat, tail, head, proj_weight, ahead, observed, lat, group, steps, share
    )

    if aligned:
        cot_left, cot_right = rims[0], rims[1]
    else:
        flat = cot.reshape(steps, rows, HALF)[:, :real].reshape(2 * blocks, O, HALF)
        flat = flat.transpose(1, 0, 2).reshape(O, blocks * BLK)[:, :cells]
        cot_left = passed_along(flat[:, cells - HALF :], "lon", 1)
        cot_right = passed_along(flat[:, :HALF], "lon", -1)
        flat = jnp.pad(
            jnp.concatenate([flat, cot_right], axis=1), ((0, 0), (0, extra - HALF))
        )
        flat = flat.reshape(O, 2 * blocks, HALF).transpose(1, 0, 2).reshape(steps, real, HALF)
        cot = jnp.pad(flat, ((0, 0), (0, rows - real), (0, 0))).reshape(steps * rows, HALF)
        cot_left = jnp.pad(cot_left, ((OP - O, 0), (0, 0)))
        cot_right = jnp.zeros((OP, HALF), BF16)
    grad, part = backward(
        cot, cot_left, cot_right, proj_weight, back, feat, group_back, steps_back, group, cells
    )
    scale = 1.0 / math.sqrt(ne * (cells // LAT) * nl * LAT)
    weight_grad = reduced(ne, nl, scale, part, chan)
    return (grad[:, :cells][None], weight_grad)


GROUP = 5
WIDE = GROUP * BLK
ROWS = GROUP * O
ROWS_P = ROWS + 8
MAIN = 64
LEFT = O - MAIN
SPLIT = GROUP * MAIN
TOPS = K * MAIN
USED = K * O + 8
LAG = 3
PART = 256
PARTS = 3


def ordered_weight(weight):
    rows = weight[...].astype(F32)
    parts = [rows[k * O : k * O + MAIN] for k in range(K)]
    parts += [rows[k * O + MAIN : (k + 1) * O] for k in range(K)]
    return jnp.concatenate(parts, axis=0)


def dot_lanes(left, right):
    return lax.dot_general(left, right, (((1,), (1,)), ((), ())), preferred_element_type=F32)


def table_columns(basis_vals, row_of, col_off):
    code = (col_off + R) * LAT + row_of
    ids = jnp.arange((2 * R + 1) * LAT, dtype=jnp.int32)
    hit = (code[:, :, None] == ids[None, None, :]).astype(F32)
    table = jnp.einsum("isk,isq->kiq", basis_vals, hit, precision=lax.Precision.HIGHEST)
    return table.astype(BF16)


def fused_kernel(
    n, nl, share, steps,
    feat, weight, table, obs, lat, grad, wout,
    wide, wrows, band, weight_t, lat_row, proj, sums, edge, first_edge, extra, edge_back,
    give, take, dec, recv, send, cot, seen, rim_left, rim_top, rim_low, spread, gout,
    wacc, wpart, wrecv, wmid, wfull,
    fsem, osem, hsend, hrecv, ssem1, rsem1, ssem2, rsem2, gsem,
    ws1, wr1, ws2, wr2, ws3, wr3,
):
    me = lax.axis_index("ens")
    at = lax.axis_index("lon")
    cells = steps * WIDE
    chan = feat.shape[0]
    own = pl.multiple_of(me * share, 16)
    after = {"lon": lax.rem(at + 1, nl)}
    before = {"lon": lax.rem(at + nl - 1, nl)}
    prow = PART // n

    def remote(src, dst, ssem, rsem, peer):
        return pltpu.make_async_remote_copy(
            src_ref=src, dst_ref=dst, send_sem=ssem, recv_sem=rsem, device_id=peer, device_id_type=MESH
        )

    def piece(c):
        if isinstance(c, int) and c == steps:
            return pltpu.make_async_copy(
                feat.at[:, pl.ds(0, HALF)], wide.at[:, pl.ds(HALF, HALF)], fsem.at[steps]
            )
        if isinstance(c, int) and c == steps - 1:
            lo, size = c * WIDE, WIDE - HALF
        else:
            lo, size = c * WIDE, WIDE
        return pltpu.make_async_copy(
            feat.at[:, pl.ds(pl.multiple_of(lo + HALF, HALF), size)],
            wide.at[:, pl.ds(pl.multiple_of(lo + 2 * HALF, HALF), size)],
            fsem.at[c],
        )

    def seen_copy(q, u):
        c = lax.rem(q + steps - 2, steps)
        t = jnp.minimum(me * (share // 8) + u, ROWS // 8 - 1)
        low = t // (SPLIT // 8)
        row = pl.multiple_of((1 - low) * (t % (MAIN // 8)) * 8 + low * MAIN, 8)
        block = (1 - low) * (t // (MAIN // 8)) + low * (ROWS // 8 - 1 - t)
        lane = pl.multiple_of(c * WIDE + block * BLK, BLK)
        return pltpu.make_async_copy(
            obs.at[pl.ds(row, 8), pl.ds(lane, BLK)], seen.at[q, pl.ds(u * 8, 8)], osem.at[q, u]
        )

    def first(q, off):
        peer = lax.rem(me + off, n)
        return remote(
            dec.at[q, pl.ds(pl.multiple_of(peer * share, 16), share)],
            recv.at[q, off], ssem1.at[q, off], rsem1.at[q, off], {"ens": peer},
        )

    def second(q, off):
        return remote(
            send.at[q, off], cot.at[q, pl.ds(own, share)],
            ssem2.at[q, off], rsem2.at[q, off], {"ens": lax.rem(me - off + n, n)},
        )

    def halo(slot):
        if slot == 0:
            src, dst, peer = give.at[0], take.at[0], after
        elif slot == 1:
            src, dst, peer = give.at[1], take.at[1], before
        elif slot == 2:
            src = cot.at[1, pl.ds(SPLIT - MAIN, MAIN + 16), pl.ds(HALF, HALF)]
            dst, peer = rim_left, after
        elif slot == 3:
            src, dst, peer = cot.at[2, pl.ds(0, MAIN), pl.ds(0, HALF)], rim_top, before
        else:
            src = cot.at[2, pl.ds(ROWS - LEFT, 16), pl.ds(0, HALF)]
            dst, peer = rim_low, before
        return remote(src, dst, hsend.at[slot], hrecv.at[slot], peer)

    def out_copy(t):
        return pltpu.make_async_copy(
            gout.at[lax.rem(t, 2)], grad.at[:, pl.ds(pl.multiple_of(t * WIDE, WIDE), WIDE)], gsem.at[t]
        )

    def scatter(j, off):
        peer = lax.rem(me + off, n)
        return remote(
            wpart.at[j, pl.ds(pl.multiple_of(peer * prow, 16), prow)], wrecv.at[j, off],
            ws1.at[j, off], wr1.at[j, off], {"ens": peer},
        )

    def across(j, off):
        return remote(
            wmid.at[j, at], wmid.at[j, at], ws2.at[j, off], wr2.at[j, off], {"lon": lax.rem(at + off, nl)}
        )

    def gather(j, off):
        mine = pl.ds(pl.multiple_of(me * prow, 16), prow)
        return remote(
            wfull.at[j, mine], wfull.at[j, mine], ws3.at[j, off], wr3.at[j, off],
            {"ens": lax.rem(me + off, n)},
        )

    def project_edges():
        start = (steps - 2) * WIDE
        lanes = jnp.concatenate(
            [wide[:, HALF:BLK], wide[:, cells : cells + HALF], wide[:, start : start + BLK]], axis=1
        )
        got = jnp.dot(wrows[...], lanes, preferred_element_type=F32)
        acc = jnp.zeros((3 * O, BLK), F32)
        out = jnp.zeros((O, BLK), F32)
        none = jnp.zeros((O, HALF), F32)
        for k in range(K):
            part = jnp.concatenate(
                [got[k * MAIN : (k + 1) * MAIN], got[TOPS + k * LEFT : TOPS + (k + 1) * LEFT]], axis=0
            )
            head = jnp.concatenate([none, part[:, :HALF]], axis=1)
            tail = jnp.concatenate([part[:, HALF:BLK], none], axis=1)
            lhs = jnp.concatenate([head, tail, part[:, BLK:]], axis=0).astype(BF16)
            acc = acc + jnp.dot(lhs, band[k, :BLK, :], preferred_element_type=F32)
            out = out + jnp.dot(head.astype(BF16), band[k, BLK:, :], preferred_element_type=F32)
        first_edge[...] = acc[:O]
        edge[...] = acc[2 * O :]
        give[0] = acc[O : 2 * O, :HALF]
        give[1] = out[:, HALF:]
        halo(0).start()
        halo(1).start()

    def forward_chunk(q):
        c = lax.rem(q + steps - 2, steps)
        got = jnp.dot(
            wrows[...],
            wide[:, pl.ds(pl.multiple_of(c * WIDE + BLK, BLK), WIDE)],
            preferred_element_type=F32,
        )
        gap = jnp.zeros((ROWS_P - ROWS, BLK), F32)
        tops = got[:TOPS].astype(BF16)
        for k in range(K):
            for g in range(GROUP):
                proj[k, g * MAIN : (g + 1) * MAIN, :] = tops[
                    k * MAIN : (k + 1) * MAIN, g * BLK : (g + 1) * BLK
                ]
            lows = [
                got[TOPS + k * LEFT : TOPS + (k + 1) * LEFT, g * BLK : (g + 1) * BLK]
                for g in reversed(range(GROUP))
            ]
            proj[k, SPLIT:, :] = jnp.concatenate(lows + [gap], axis=0).astype(BF16)
        def one_half(half, carry):
            acc = jnp.zeros((ROWS_P, BLK), F32)
            rows = pl.ds(pl.multiple_of(half * BLK, BLK), BLK)
            for k in range(K):
                acc = acc + jnp.dot(proj[k], band[k, rows, :], preferred_element_type=F32)
            sums[half] = acc
            return carry

        lax.fori_loop(0, 2, one_half, 0)

        @pl.when(q == 1)
        def _():
            halo(1).wait()
            extra[:, HALF:] = take[1]

        @pl.when(q == 2)
        def _():
            halo(0).wait()
            extra[...] = jnp.zeros_like(extra)
            edge[...] = first_edge[...]
            edge[:, :HALF] += take[0]

        last = SPLIT - MAIN
        dec[q, :last, :] = (
            jnp.concatenate([edge[:MAIN], sums[0, : last - MAIN]], axis=0) + sums[1, :last]
        ).astype(BF16)
        dec[q, last:SPLIT, :] = (
            sums[0, last - MAIN : last] + sums[1, last:SPLIT] + extra[:MAIN]
        ).astype(BF16)
        lows = jnp.concatenate([sums[0, SPLIT + LEFT : ROWS], edge[MAIN:]], axis=0) + sums[1, SPLIT:ROWS]
        lows = [lows[:LEFT] + extra[MAIN:], lows[LEFT:]]
        rest = jnp.zeros((n * share - ROWS, BLK), F32)
        dec[q, SPLIT:, :] = jnp.concatenate(lows + [rest], axis=0).astype(BF16)
        edge[...] = sums[0, last : SPLIT + LEFT]
        for off in range(1, n):
            first(q, off).start()

    def smooth(diff):
        return diff * lax.rsqrt(diff * diff + SMOOTH * SMOOTH)

    def slopes(q):
        for u in range(share // 8):
            seen_copy(q, u).wait()
        for off in range(1, n):
            first(q, off).wait_recv()

        def one(step, carry):
            row = pl.multiple_of(lax.div(step, 2) * 16, 16)
            lanes = pl.ds(pl.multiple_of(lax.rem(step, 2) * HALF, HALF), HALF)
            here = pl.ds(pl.multiple_of(own + row, 16), 16)
            values = [dec[q, here, lanes].astype(F32)]
            values += [recv[q, off, pl.ds(row, 16), lanes].astype(F32) for off in range(1, n)]
            sums = [None] * n
            for a in range(n):
                for b in range(a + 1, n):
                    pair = smooth(values[a] - values[b])
                    sums[a] = pair if sums[a] is None else sums[a] + pair
                    sums[b] = -pair if sums[b] is None else sums[b] - pair
            target = seen[q, pl.ds(row, 16), lanes]
            area = jnp.broadcast_to(lat_row[0:1, lanes], (16, HALF))
            for a in range(n):
                slope = smooth(values[a] - target) - sums[a] * (1.0 / (n - 1))
                result = (slope * area).astype(BF16)
                if a == 0:
                    cot[q, here, lanes] = result
                else:
                    send[q, a, pl.ds(row, 16), lanes] = result
            return carry

        lax.fori_loop(0, share // 16 * 2, one, 0)
        for off in range(1, n):
            second(q, off).start()

    def store_lows(lows, lanes):
        both = jnp.concatenate(lows + [jnp.zeros((USED - K * O, BLK), F32)], axis=0)
        spread[TOPS:USED, lanes] = both.astype(BF16)

    def backward_chunk(b):
        q = lax.rem(b + 2, steps)
        lhs = cot[q, pl.ds(0, ROWS_P), :]
        lows = [[] for _ in range(GROUP)]
        for k in range(K):
            ahead = dot_lanes(lhs, band[k, BLK:, :])
            here = dot_lanes(lhs, band[k, :BLK, :])
            for g in range(GROUP):
                low = SPLIT + (GROUP - 1 - g) * LEFT
                top = edge_back[k, :MAIN] if g == 0 else ahead[(g - 1) * MAIN : g * MAIN]
                end = edge_back[k, MAIN:] if g == 0 else ahead[low + LEFT : low + 2 * LEFT]
                lanes = pl.ds(pl.multiple_of(b * WIDE + g * BLK, BLK), BLK)
                spread[k * MAIN : (k + 1) * MAIN, lanes] = (
                    here[g * MAIN : (g + 1) * MAIN] + top
                ).astype(BF16)
                lows[g].append(here[low : low + LEFT] + end)
            edge_back[k] = ahead[SPLIT - MAIN : SPLIT + LEFT]
        for g in range(GROUP):
            store_lows(lows[g], pl.ds(pl.multiple_of(b * WIDE + g * BLK, BLK), BLK))

    def add_weight(lanes):
        wacc[:, : K * O] += lax.dot_general(
            wide[:, lanes], spread[: K * O, lanes], (((1,), (1,)), ((), ())), preferred_element_type=F32
        )

    def one_grad(t, carry):
        @pl.when(t >= 2)
        def _():
            out_copy(t - 2).wait()

        lanes = pl.ds(pl.multiple_of(t * WIDE + HALF, HALF), WIDE)
        gout[lax.rem(t, 2)] = jnp.dot(
            weight_t[:, :USED], spread[:, lanes], preferred_element_type=F32
        ).astype(BF16)
        out_copy(t).start()
        return carry

    def after_scatter(j):
        for off in range(1, n):
            scatter(j, off).wait_recv()
        total = wpart[j, pl.ds(pl.multiple_of(me * prow, 16), prow), :].astype(F32)
        for off in range(1, n):
            total = total + wrecv[j, off].astype(F32)
        wmid[j, at] = total.astype(BF16)
        for off in range(1, nl):
            across(j, off).start()

    def after_across(j):
        for off in range(1, nl):
            across(j, off).wait_recv()
        total = wmid[j, 0].astype(F32)
        for z in range(1, nl):
            total = total + wmid[j, z].astype(F32)
        wfull[j, pl.ds(pl.multiple_of(me * prow, 16), prow), :] = total.astype(BF16)
        for off in range(1, n):
            gather(j, off).start()

    for c in [steps - 1, steps, steps - 3, steps - 2]:
        piece(c).start()
    for c in range(steps - 3):
        piece(c).start()

    def look(q, carry):
        for u in range(share // 8):
            seen_copy(q, u).start()
        return carry

    lax.fori_loop(0, steps, look, 0)
    peers = [{"ens": lax.rem(me + off, n)} for off in range(1, n)]
    peers += [{"lon": lax.rem(at + off, nl)} for off in range(1, nl)]
    barrier = pltpu.get_barrier_semaphore()
    for peer in peers:
        pl.semaphore_signal(barrier, inc=1, device_id=peer, device_id_type=MESH)
    build_band_rows(table, band)
    lane = lax.broadcasted_iota(jnp.int32, (LAT, BLK), 1)
    ones = (lane % LAT == lax.broadcasted_iota(jnp.int32, (LAT, BLK), 0)).astype(F32)
    lat_row[...] = jnp.dot(
        jnp.broadcast_to(lat[...], (8, LAT)), ones, precision=lax.Precision.HIGHEST,
        preferred_element_type=F32,
    )
    wrows[...] = ordered_weight(weight).astype(BF16)
    wide[:, :HALF] = jnp.zeros((chan, HALF), BF16)
    wide[:, cells + HALF :] = jnp.zeros((chan, HALF), BF16)
    extra[...] = jnp.zeros_like(extra)
    for c in [steps - 1, steps, steps - 3, steps - 2]:
        piece(c).wait()
    pl.semaphore_wait(barrier, len(peers))
    project_edges()

    def step(s, carry):
        @pl.when(jnp.logical_and(s >= 2, s < steps - 1))
        def _():
            piece(s - 2).wait()

        @pl.when(s < steps)
        def _():
            forward_chunk(s)

        @pl.when(s >= LAG)
        def _():
            slopes(s - LAG)

        return carry

    lax.fori_loop(0, steps, step, 0)
    for q in (1, 2, 0):
        for off in range(1, n):
            second(q, off).wait_recv()
        if q == 1:
            halo(2).start()
        if q == 2:
            halo(3).start()
            halo(4).start()
    gap = jnp.zeros((PARTS * PART - K * O, chan), F32)
    rows = jnp.concatenate([ordered_weight(weight), gap], axis=0)
    weight_t[...] = rows.T.astype(BF16)
    wacc[...] = jnp.zeros_like(wacc)
    halo(2).wait()
    for k in range(K):
        got = dot_lanes(rim_left[...], band[k, BLK:, HALF:])
        edge_back[k] = got[:O]

    def step_back(b, carry):
        @pl.when(b < LAG)
        def _():
            slopes(steps - LAG + b)

        @pl.when(jnp.logical_and(b >= 1, b < steps - 2))
        def _():
            for off in range(1, n):
                second(b + 2, off).wait_recv()

        backward_chunk(b)

        @pl.when(b % 2 == 1)
        def _():
            add_weight(pl.ds(pl.multiple_of((b - 1) * WIDE, WIDE), 2 * WIDE))

        return carry

    lax.fori_loop(0, steps, step_back, 0)
    halo(3).wait()
    halo(4).wait()
    rim = jnp.concatenate([rim_top[...].astype(F32), rim_low[...].astype(F32)], axis=0).astype(BF16)
    lows = []
    for k in range(K):
        got = dot_lanes(rim, band[k, :BLK, :HALF])
        both = got[:O] + edge_back[k]
        spread[k * MAIN : (k + 1) * MAIN, cells : cells + BLK] = both[:MAIN].astype(BF16)
        lows.append(both[MAIN:])
    store_lows(lows, slice(cells, cells + BLK))
    rest = steps % 2 * WIDE
    add_weight(pl.ds(cells - rest, rest + BLK))

    def one_part(j, carry):
        wpart[j] = wacc[:, pl.ds(pl.multiple_of(j * PART, PART), PART)].T.astype(BF16)
        for off in range(1, n):
            scatter(j, off).start()
        return carry

    lax.fori_loop(0, PARTS, one_part, 0)

    def late(t, carry):
        one_grad(t, 0)

        @pl.when(jnp.logical_and(t >= 2, t < 2 + PARTS))
        def _():
            after_scatter(t - 2)

        @pl.when(jnp.logical_and(t >= 4, t < 4 + PARTS))
        def _():
            after_across(t - 4)

        return carry

    lax.fori_loop(0, steps, late, 0)
    for j in range(PARTS):
        for off in range(1, n):
            gather(j, off).wait_recv()

    def drain(q, carry):
        for off in range(1, n):
            first(q, off).wait_send()
            second(q, off).wait_send()
        return carry

    rows = [wfull[j].astype(F32) for j in range(PARTS)]
    rows = jnp.concatenate(rows, axis=0)
    parts = []
    for k in range(K):
        parts += [rows[k * MAIN : (k + 1) * MAIN], rows[TOPS + k * LEFT : TOPS + (k + 1) * LEFT]]
    wout[...] = jnp.concatenate(parts, axis=0).astype(BF16)
    lax.fori_loop(0, steps, drain, 0)
    for j in range(PARTS):
        for off in range(1, n):
            scatter(j, off).wait_send()
            gather(j, off).wait_send()
        for off in range(1, nl):
            across(j, off).wait_send()
    out_copy(steps - 2).wait()
    out_copy(steps - 1).wait()


def fused(n, nl, feat, weight, table, obs, lat, share):
    chan, cells = feat.shape
    steps = cells // WIDE
    vmem = pl.BlockSpec(memory_space=pltpu.VMEM)
    anywhere = pl.BlockSpec(memory_space=pl.ANY)
    dma = pltpu.SemaphoreType.DMA
    prow = PART // n
    return pl.pallas_call(
        functools.partial(fused_kernel, n, nl, share, steps),
        out_shape=(
            jax.ShapeDtypeStruct((chan, cells), BF16),
            jax.ShapeDtypeStruct((K * O, chan), BF16),
        ),
        in_specs=[anywhere, vmem, vmem, anywhere, vmem],
        out_specs=(anywhere, vmem),
        scratch_shapes=[
            pltpu.VMEM((chan, cells + BLK), BF16),
            pltpu.VMEM((K * O, chan), BF16),
            pltpu.VMEM((K, 2 * BLK, BLK), BF16),
            pltpu.VMEM((chan, PARTS * PART), BF16),
            pltpu.VMEM((8, BLK), F32),
            pltpu.VMEM((K, ROWS_P, BLK), BF16),
            pltpu.VMEM((2, ROWS_P, BLK), F32),
            pltpu.VMEM((O, BLK), F32),
            pltpu.VMEM((O, BLK), F32),
            pltpu.VMEM((O, BLK), F32),
            pltpu.VMEM((K, O, BLK), F32),
            pltpu.VMEM((2, O, HALF), F32),
            pltpu.VMEM((2, O, HALF), F32),
            pltpu.VMEM((steps, n * share, BLK), BF16),
            pltpu.VMEM((steps, n, share, BLK), BF16),
            pltpu.VMEM((steps, n, share, BLK), BF16),
            pltpu.VMEM((steps, n * share, BLK), BF16),
            pltpu.VMEM((steps, share, BLK), F32),
            pltpu.VMEM((MAIN + 16, HALF), BF16),
            pltpu.VMEM((MAIN, HALF), BF16),
            pltpu.VMEM((16, HALF), BF16),
            pltpu.VMEM((USED, cells + BLK), BF16),
            pltpu.VMEM((2, chan, WIDE), BF16),
            pltpu.VMEM((chan, PARTS * PART), F32),
            pltpu.VMEM((PARTS, PART, chan), BF16),
            pltpu.VMEM((PARTS, n, prow, chan), BF16),
            pltpu.VMEM((PARTS, nl, prow, chan), BF16),
            pltpu.VMEM((PARTS, PART, chan), BF16),
            dma((steps + 1,)),
            dma((steps, share // 8)),
            dma((5,)),
            dma((5,)),
            dma((steps, n)),
            dma((steps, n)),
            dma((steps, n)),
            dma((steps, n)),
            dma((steps,)),
            dma((PARTS, n)),
            dma((PARTS, n)),
            dma((PARTS, nl)),
            dma((PARTS, nl)),
            dma((PARTS, n)),
            dma((PARTS, n)),
        ],
        compiler_params=pltpu.CompilerParams(
            collective_id=2, has_side_effects=True, vmem_limit_bytes=VMEM_LIMIT
        ),
        name="fused_decoder",
    )(feat, weight, table, obs, lat)


def write_kernel(scale, grad, part, out, wout):
    out[...] = grad[...]

    @pl.when(pl.program_id(0) == 0)
    def _():
        wout[...] = part[...].astype(F32) * scale


def written(grad, part, scale, size):
    chan, cells = grad.shape
    block = pl.BlockSpec((size, cells), lambda s: (s, 0))
    return pl.pallas_call(
        functools.partial(write_kernel, scale),
        out_shape=(
            jax.ShapeDtypeStruct(grad.shape, BF16),
            jax.ShapeDtypeStruct(part.shape, F32),
        ),
        grid=(chan // size,),
        in_specs=[block, whole(part.shape)],
        out_specs=(block, whole(part.shape)),
        compiler_params=pltpu.CompilerParams(vmem_limit_bytes=VMEM_LIMIT),
        name="write_results",
    )(grad, part)


def fused_shards(features, proj_weight, basis_vals, row_of, col_off, observed, lat_weight):
    ne = lax.axis_size("ens")
    nl = lax.axis_size("lon")
    feat = features[0]
    chan, cells = feat.shape
    share = pl.cdiv(pl.cdiv(ROWS, ne), 16) * 16
    table = table_columns(basis_vals, row_of, col_off)
    grad, part = fused(
        ne, nl, feat, proj_weight, table, observed, lat_weight.reshape(1, LAT), share
    )
    scale = 1.0 / math.sqrt(ne * (cells // LAT) * nl * LAT)
    grad, weight_grad = written(grad, part, scale, 96)
    return (grad[None], weight_grad)


def shards(*args):
    cells = args[0].shape[2]
    sizes = (lax.axis_size("ens"), lax.axis_size("lon"))
    if cells % WIDE == 0 and cells // WIDE >= 8 and PART % (16 * sizes[0]) == 0 and sizes[1] > 1:
        return fused_shards(*args)
    return split_shards(*args)


def solution(mesh):
    in_specs = (P("ens", None, "lon"), P(), P(), P(), P(), P(None, "lon"), P())
    out_specs = (P("ens", None, "lon"), P())
    return jax.shard_map(shards, mesh=mesh, in_specs=in_specs, out_specs=out_specs, check_vma=False)
```
